256 devices in a mesh: su: 16 (over z, core), sv: 8 (over x, y_lo), nrm: 2 (over y_hi).
Axes of the slice: x: 4, y: 4 (y_hi: 2, y_lo: 2; y = y_hi * 2 + y_lo), z: 8, core: 2. Of those that a mesh axis runs over, the one named last changes fastest.
Arguments:
- primitive: float32 [5, 256, 320, 256], P(None, 'su', 'sv', 'nrm'), may hold values from -4 to 4, as said below
- adjoint_state: float32 [5, 256, 320, 256], P(None, 'su', 'sv', 'nrm'), may hold values from -0.6 to 0.6
- objective_grad: float32 [5, 256, 320, 256], P(None, 'su', 'sv', 'nrm'), may hold values from -6 to 6
- front_height: float32 [256, 320], P('su', 'sv'), may hold values from 0.8 to 1.25
- shock_state: float32 [5, 256, 320], P(None, 'su', 'sv'), may hold values from -4 to 4, as said below
- state_by_height: float32 [5, 256, 320], P(None, 'su', 'sv'), may hold values from -18 to 18
- state_by_slope: float32 [5, 256, 320], P(None, 'su', 'sv'), may hold values from -6 to 6
- fitted_flags: int32 [256, 320], P('su', 'sv'), may hold values 0 or 1
Outputs:
- adjoint_residual: float32 [5, 256, 320, 256], P(None, 'su', 'sv', 'nrm')
- slope_sensitivity: float32 [256, 320], P('su', 'sv')
The draws below stay inside these ranges and needn't reach their ends.
Inputs may be any that keep to these rules, and one draw needn't show every extreme that they name: `primitive`: variables 0 (density) and 4 (pressure) lie in 0.5 to 2; variables 1 to 3 are velocity components. `shock_state`: variables 0 (density) and 4 (pressure) lie in 0.5 to 2; variables 1 to 3 are velocity components.
All inputs are finite; a program needn't handle non-finite values. No bound on the sum of `fitted_flags` on one device may be relied on, other than what follows from the above.
Results may differ from the reference program's by a relative error of at most 0.0003.
Values sent between devices are 32-bit elements; how exact they have to be, the bound alone decides.
No kernel may reach another device: no remote copies, remote signals or barrier semaphores. Data moves between devices by JAX's collectives and lax.ppermute only.
A program may use at most 128 MiB of HBM per device.

```python
import jax
import jax.numpy as jnp
from jax import lax

CU = 16
NU = 256
NV = 320
NN = 256
N_SU = 16


def primitive_fields(key, shape):
    subkeys = jax.random.split(key, 3)
    density = jax.random.uniform(subkeys[0], shape, jnp.float32, 0.5, 2.0)
    pressure = jax.random.uniform(subkeys[2], shape, jnp.float32, 0.5, 2.0)
    velocity = jnp.clip(1.5 * jax.random.normal(subkeys[1], (3,) + shape, jnp.float32), -4.0, 4.0)
    return jnp.concatenate([density[None], velocity, pressure[None]], 0)


def draw_primitive(key, part):
    return primitive_fields(key, (NU, NV, NN))


def draw_shock_state(key, part):
    return primitive_fields(jax.random.fold_in(key, 7), (NU, NV))


def set_ends(entries, key, least, largest):
    longest = entries.shape.index(max(entries.shape))
    spots = []
    for shift in (0, 1):
        where = [jax.random.randint(jax.random.fold_in(key, axis), (), 0, length) for axis, length in enumerate(entries.shape)]
        where[longest] = (where[longest] + shift) % entries.shape[longest]
        spots.append(tuple(where))
    return entries.at[spots[0]].set(least).at[spots[1]].set(largest)


def level_of(rng, extent, cuts, low, high):
    gain, own = 1.0, jax.random.fold_in(rng, 6)
    for dim, parts in cuts:
        heights = jnp.exp(jax.random.uniform(jax.random.fold_in(own, dim), (parts,), jnp.float32, low / len(cuts), high / len(cuts)))
        gain = gain * jnp.repeat(heights, extent[dim] // parts).reshape([-1 if axis == dim else 1 for axis in range(len(extent))])
    return gain


def centred(key, shape, width, bound, cuts=(), kind=jnp.bfloat16):
    drawn = width * jax.random.normal(key, shape, jnp.float32)
    if cuts:
        drawn = drawn * level_of(key, shape, cuts, -0.22, 0.18)
    return jnp.clip(drawn, -bound, bound).astype(kind)


def setup_inputs(seed: int = 0) -> dict:
    keys = jax.random.split(jax.random.key(seed), 9)
    return {
        "primitive": draw_primitive(jax.random.fold_in(keys[8], 71), 0),
        "adjoint_state": centred(keys[1], (5, NU, NV, NN), 0.1, 0.6, ((1, 16), (2, 8), (3, 2)), jnp.float32),
        "objective_grad": centred(keys[2], (5, NU, NV, NN), 1.0, 6.0, ((1, 16), (2, 8), (3, 2)), jnp.float32),
        "front_height": jnp.clip(0.8 + 0.45 * jax.random.uniform(keys[3], (NU, NV), jnp.float32) ** level_of(keys[3], (NU, NV), ((0, 16), (1, 8)), -0.2, 0.2), 0.8, 1.25),
        "shock_state": draw_shock_state(jax.random.fold_in(keys[8], 71), 0),
        "state_by_height": centred(keys[5], (5, NU, NV), 3.0, 18.0, ((1, 16), (2, 8)), jnp.float32),
        "state_by_slope": centred(keys[6], (5, NU, NV), 1.0, 6.0, ((1, 16), (2, 8)), jnp.float32),
        "fitted_flags": set_ends((jax.random.randint(keys[7], (NU, NV), 0, 4) < 3).astype(jnp.int32), jax.random.fold_in(keys[7], 1), 0, 1),
    }


gamma_ratio = 1.4
damping_coef = 0.0625
stretch_rate = 2.2

def thermo(state):
    speed_square = state[1] * state[1] + state[2] * state[2] + state[3] * state[3]
    kinetic = 0.5 * (gamma_ratio - 1.0) * speed_square
    enthalpy = gamma_ratio * state[4] / ((gamma_ratio - 1.0) * state[0]) + 0.5 * speed_square
    return (kinetic, enthalpy)

def line_flux(state, enthalpy):
    mass_flow = state[0] * state[3]
    return jnp.stack([mass_flow, mass_flow * state[1], mass_flow * state[2], mass_flow * state[3] + state[4], mass_flow * enthalpy], 0)

def flux_transpose(state, kinetic, enthalpy, adjoint, direction):
    normal_speed = state[direction]
    projected = adjoint[direction]
    dotted = state[1] * adjoint[1] + state[2] * adjoint[2] + state[3] * adjoint[3]
    energy_term = adjoint[4]
    mass_row = kinetic * projected - normal_speed * dotted + normal_speed * (kinetic - enthalpy) * energy_term
    common = adjoint[0] + dotted + enthalpy * energy_term
    shared = projected + normal_speed * energy_term
    pieces = [mass_row]
    for component in (1, 2, 3):
        entry = normal_speed * adjoint[component] - (gamma_ratio - 1.0) * state[component] * shared
        if component == direction:
            entry = entry + common
        pieces.append(entry)
    pieces.append((gamma_ratio - 1.0) * projected + gamma_ratio * normal_speed * energy_term)
    return jnp.stack(pieces, 0)

def tangent_parts(padded_adjoint, padded_radius, along_axis, length):

    def window(source, offset):
        return lax.slice_in_dim(source, offset, offset + length, axis=along_axis)
    gradient = (8.0 * (window(padded_adjoint, 1) - window(padded_adjoint, 3)) - (window(padded_adjoint, 0) - window(padded_adjoint, 4))) / 12.0
    weighted = padded_radius[None] * padded_adjoint
    fourth = window(weighted, 0) - 4.0 * window(weighted, 1) + 6.0 * window(weighted, 2) - 4.0 * window(weighted, 3) + window(weighted, 4)
    return (gradient, fourth)

def reference(primitive, adjoint_state, objective_grad, front_height, shock_state, state_by_height, state_by_slope, fitted_flags):
    fraction = (jnp.arange(NN).astype(jnp.float32) + 0.5) / NN
    stretch = jnp.exp(stretch_rate * (fraction - 1.0))
    sound_speed = jnp.sqrt(gamma_ratio * primitive[4] / primitive[0])
    radius_first = jnp.abs(primitive[1]) + sound_speed
    padded_adjoint = jnp.pad(adjoint_state, ((0, 0), (2, 2), (0, 0), (0, 0)))
    padded_radius = jnp.pad(radius_first, ((2, 2), (0, 0), (0, 0)))
    shock_kinetic, shock_enthalpy = thermo(shock_state)
    shock_flux = line_flux(shock_state, shock_enthalpy)

    def block_terms(block_index):
        first_row = (block_index * CU).astype(jnp.int32)
        adjoint_rows = lax.dynamic_slice_in_dim(padded_adjoint, first_row, CU + 4, 1)
        radius_rows = lax.dynamic_slice_in_dim(padded_radius, first_row, CU + 4, 0)
        state = lax.dynamic_slice_in_dim(primitive, first_row, CU, 1)
        target = lax.dynamic_slice_in_dim(objective_grad, first_row, CU, 1)
        height = lax.dynamic_slice_in_dim(front_height, first_row, CU, 0)
        shock = lax.dynamic_slice_in_dim(shock_state, first_row, CU, 1)
        shock_kin = lax.dynamic_slice_in_dim(shock_kinetic, first_row, CU, 0)
        shock_enth = lax.dynamic_slice_in_dim(shock_enthalpy, first_row, CU, 0)
        flux_top = lax.dynamic_slice_in_dim(shock_flux, first_row, CU, 1)
        kinetic, enthalpy = thermo(state)
        center = adjoint_rows[:, 2:CU + 2]
        first_grad, first_fourth = tangent_parts(adjoint_rows, radius_rows, 1, CU)
        radius_second = jnp.abs(state[2]) + jnp.sqrt(gamma_ratio * state[4] / state[0])
        second_grad, second_fourth = tangent_parts(jnp.pad(center, ((0, 0), (0, 0), (2, 2), (0, 0))), jnp.pad(radius_second, ((0, 0), (2, 2), (0, 0))), 2, NV)
        scaled = center / (2.0 * height[None, :, :, None] * stretch[None, None, None, :])
        padded_scaled = jnp.pad(scaled, ((0, 0), (0, 0), (0, 0), (1, 1)))
        fluxes = line_flux(state, enthalpy)
        flux_above = jnp.concatenate([fluxes[..., 1:], flux_top[..., None]], -1)
        flux_below = jnp.concatenate([jnp.zeros_like(fluxes[..., :1]), fluxes[..., :-1]], -1)
        metric = -lax.optimization_barrier(jnp.sum(scaled * (flux_above - flux_below), axis=(0, 3))) / height
        shock_adjoint = flux_transpose(shock, shock_kin, shock_enth, scaled[..., -1], 3)
        residual = target + flux_transpose(state, kinetic, enthalpy, first_grad, 1) + flux_transpose(state, kinetic, enthalpy, second_grad, 2) + damping_coef * (first_fourth + second_fourth) + flux_transpose(state, kinetic, enthalpy, padded_scaled[..., :-2] - padded_scaled[..., 2:], 3)
        return (residual, metric, shock_adjoint)
    residual_blocks, metric_blocks, shock_blocks = lax.map(block_terms, jnp.arange(N_SU, dtype=jnp.int32))
    residual = jnp.moveaxis(residual_blocks, 0, 1).reshape(5, NU, NV, NN)
    metric = metric_blocks.reshape(NU, NV)
    shock_adjoint = jnp.moveaxis(shock_blocks, 0, 1).reshape(5, NU, NV)
    fitted = fitted_flags.astype(jnp.float32)
    height_term = metric + fitted * lax.optimization_barrier(jnp.sum(shock_adjoint * state_by_height, 0))
    slope_sensitivity = lax.cumsum(height_term, axis=0, reverse=True) / NU + fitted * lax.optimization_barrier(jnp.sum(shock_adjoint * state_by_slope, 0))
    enthalpy_all = thermo(primitive)[1]
    adjoint_residual = residual + fraction[None, None, None, :] * slope_sensitivity[None, :, :, None] * line_flux(primitive, enthalpy_all)
    return (adjoint_residual, slope_sensitivity)
```

```python
import functools

import jax
import jax.numpy as jnp
from jax import lax
from jax.experimental import pallas as pl
from jax.experimental.pallas import tpu as pltpu
from jax.sharding import PartitionSpec as P

gamma_ratio = 1.4
damping_coef = 0.0625
stretch_rate = 2.2
gm = gamma_ratio - 1.0
f32 = jnp.float32
VMEM = pltpu.VMEM


def lanes(shape=(8, 128)):
    return lax.broadcasted_iota(jnp.int32, shape, 1)


def spread_lane(tile, lane):
    return jnp.broadcast_to(tile[:, lane : lane + 1], tile.shape)


def edges_kernel(rows, tiles, prim, psi, ends, su_low, su_high, sv_low, sv_high):
    nrm = lax.axis_index("nrm")
    lane = lanes()
    extra = jnp.where(nrm == 0, 1, 0)
    for t in range(tiles):
        packed = jnp.zeros((8, 128), f32)
        for q in range(5):
            for i in range(rows):
                spot = rows * q + i
                moved = pltpu.roll(psi[q, i, 8 * t : 8 * t + 8, :], spot + extra, 1)
                packed = jnp.where(lane == spot, moved, packed)
        ends[8 * t : 8 * t + 8, :] = packed

    def radius(which, i, low, high):
        sound = jnp.sqrt(gamma_ratio * prim[4, i, low:high, :] / prim[0, i, low:high, :])
        return jnp.abs(prim[which, i, low:high, :]) + sound

    columns = 8 * tiles
    for r in range(2):
        for q in range(5):
            su_low[q, r] = psi[q, r]
            su_high[q, r] = psi[q, rows - 2 + r]
        su_low[5, r] = radius(1, r, 0, columns)
        su_high[5, r] = radius(1, rows - 2 + r, 0, columns)
    for i in range(rows):
        for q in range(5):
            sv_low[q, 2 * i : 2 * i + 2, :] = psi[q, i, 0:2, :]
            sv_high[q, 2 * i : 2 * i + 2, :] = psi[q, i, columns - 2 : columns, :]
        sv_low[5, 2 * i : 2 * i + 2, :] = radius(2, i, 0, 8)[0:2]
        sv_high[5, 2 * i : 2 * i + 2, :] = radius(2, i, columns - 8, columns)[6:8]


def flux_of(rho, u1, u2, u3, p, enthalpy):
    mass = rho * u3
    return (mass, mass * u1, mass * u2, mass * u3 + p, mass * enthalpy)


def thermo(rho, u1, u2, u3, p):
    half = 0.5 * (u1 * u1 + u2 * u2 + u3 * u3)
    return gm * half, (gamma_ratio / gm) * (p / rho) + half


def lines_kernel(
    rows, tiles, depth, total_depth, surface, fan,
    prim, psi, arrived, height, shock, by_height, by_slope, flags,
    chunk, normal,
    turn, facts,
):
    nrm = lax.axis_index("nrm")
    first = nrm == 0
    lane = lanes()
    lane_row = lanes((1, 128))
    depth_index = (lane_row + nrm * depth).astype(f32)
    inv_stretch = 1.0 / jnp.exp(stretch_rate * ((depth_index + 0.5) / total_depth - 1.0))
    partner = jnp.where(first, depth, depth - 1).astype(f32)
    partner_row = jnp.zeros((1, 128), f32) + partner
    partner_inv = 1.0 / jnp.exp(stretch_rate * ((partner_row + 0.5) / total_depth - 1.0))
    top_inv = 1.0 / jnp.exp(
        stretch_rate * ((jnp.zeros((1, 128), f32) + (total_depth - 0.5)) / total_depth - 1.0)
    )
    weight = 0.5 * inv_stretch
    lower = jnp.broadcast_to(jnp.where(lane_row == depth - 1, 0.0, weight), (8, 128))
    upper = jnp.broadcast_to(jnp.where(lane_row == 0, 0.0, weight), (8, 128))
    entry = jnp.where(first, depth - 1, 0)
    sign = jnp.where(first, -0.5, 0.5)
    edge = jnp.broadcast_to(jnp.where(lane_row == entry, sign * partner_inv, 0.0), (8, 128))

    turn[...] = jnp.zeros_like(turn)
    columns = 8 * tiles
    for place, array in enumerate(
        [height[...]]
        + [shock[q] for q in range(5)]
        + [flags[...].astype(f32)]
    ):
        turn[0, rows * place : rows * place + rows, 0:columns] = array
    for q in range(5):
        turn[1, rows * q : rows * q + rows, 0:columns] = by_height[q]
        turn[2, rows * q : rows * q + rows, 0:columns] = by_slope[q]
    for n in range(3):
        facts[n] = turn[n].T

    out = jnp.zeros((8, 128), f32)
    for t in range(tiles):
        span = slice(8 * t, 8 * t + 8)
        surf = facts[0, span, :]
        inv_height = jnp.where(lane < rows, 1.0 / jnp.where(lane < rows, surf, 1.0), 0.0)
        came = arrived[span, :]
        gathered = jnp.zeros((8, 128), f32)
        tops = jnp.zeros((8, 128), f32)
        for i in range(rows):
            rho, u1, u2, u3, p = (prim[q, i, span, :] for q in range(5))
            _, enthalpy = thermo(rho, u1, u2, u3, p)
            fluxes = flux_of(rho, u1, u2, u3, p, enthalpy)
            inv = spread_lane(inv_height, i)
            low, high, end = lower * inv, upper * inv, edge * inv
            work = None
            for q in range(5):
                value = psi[q, i, span, :]
                spot = rows * q + i
                step = (
                    pltpu.roll(value * low, 1, 1)
                    - pltpu.roll(value * high, 127, 1)
                    + end * spread_lane(came, spot)
                )
                normal[q, i, span, :] = step
                work = fluxes[q] * step if work is None else work + fluxes[q] * step
                tops = jnp.where(lane == spot, pltpu.roll(value, (spot + 1) % 128, 1), tops)
            summed = jnp.broadcast_to(jnp.sum(work, axis=1, keepdims=True), (8, 128))
            gathered = jnp.where(lane == i, summed, gathered)

        def part(array, q):
            return pltpu.roll(array, (128 - rows * q) % 128, 1) if q else array

        inside = lane < rows
        rho, u1, u2, u3, p = (
            jnp.where(inside, part(surf, q + 1), 1.0) for q in range(5)
        )
        fitted = jnp.where(inside, part(surf, 6), 0.0)
        top_scale = 0.5 * top_inv * inv_height
        s0, s1, s2, s3, s4 = (part(tops, q) * top_scale for q in range(5))
        kinetic, enthalpy = thermo(rho, u1, u2, u3, p)
        fluxes = flux_of(rho, u1, u2, u3, p, enthalpy)
        top_work = (
            fluxes[0] * s0 + fluxes[1] * s1 + fluxes[2] * s2 + fluxes[3] * s3 + fluxes[4] * s4
        )
        dotted = u1 * s1 + u2 * s2 + u3 * s3
        shared = gm * (s3 + u3 * s4)
        common = s0 + dotted + enthalpy * s4
        adjoint = (
            kinetic * s3 - u3 * dotted + u3 * (kinetic - enthalpy) * s4,
            u3 * s1 - u1 * shared,
            u3 * s2 - u2 * shared,
            u3 * s3 - u3 * shared + common,
            gm * s3 + gamma_ratio * u3 * s4,
        )
        heights = facts[1, span, :]
        slopes = facts[2, span, :]
        by_h = sum(adjoint[q] * part(heights, q) for q in range(5))
        by_s = sum(adjoint[q] * part(slopes, q) for q in range(5))
        front = jnp.where(first, 0.0, 1.0)
        metric = -inv_height * (gathered + front * top_work)
        term = jnp.where(inside, metric + front * fitted * by_h, 0.0)
        for d in (1, 2, 4, 8):
            if d < rows:
                term = term + pltpu.roll(term, 128 - d, 1)
        share = term * (1.0 / surface)
        mine = share + jnp.where(inside, front * fitted * by_s, 0.0)
        out = jnp.where(
            (lane >= rows * t) & (lane < rows * t + rows),
            pltpu.roll(mine, rows * t, 1) if t else mine,
            out,
        )
        out = jnp.where(lane == rows * tiles + t, spread_lane(share, 0), out)
    for n in range(fan):
        chunk[n] = out


def final_kernel(
    rows, tiles, depth, total_depth, su_count, sv_count, fan,
    prim, psi, target, normal, su_low, su_high, sv_low, sv_high, chunks,
    result, slope,
    wide, along, across, enth, turn,
):
    su, sv, nrm = lax.axis_index("su"), lax.axis_index("sv"), lax.axis_index("nrm")
    lane = lanes()
    columns = 8 * tiles
    lines = fan // su_count
    ahead = jnp.zeros((8, 128), f32)
    for n in range(fan):
        ahead = ahead + jnp.where(n // lines > su, chunks[n], 0.0)
    packed = chunks[lines * su]
    for n in range(1, lines):
        packed = packed + chunks[lines * su + n]
    upstream = jnp.zeros((8, 128), f32)
    for t in range(tiles):
        upstream = jnp.where(
            (lane >= rows * t) & (lane < rows * t + rows),
            spread_lane(ahead, rows * tiles + t),
            upstream,
        )
    packed = packed + upstream
    turn[...] = jnp.zeros_like(turn)
    for t in range(tiles):
        turn[8 * t : 8 * t + 8, :] = pltpu.roll(packed, 128 - rows * t, 1) if t else packed
    slope[...] = turn[...].T[0:rows, 0:columns]

    low_on, high_on = su > 0, su < su_count - 1
    for r in range(2):
        for ref, on, row in ((su_low, low_on, r), (su_high, high_on, rows + 2 + r)):
            radius = ref[5, r]
            for q in range(5):
                value = jnp.where(on, ref[q, r], 0.0)
                wide[q, row, 8 : 8 + columns, :] = value
                along[q, row] = value * radius
    left_on, right_on = sv > 0, sv < sv_count - 1
    for ref, on, col in ((sv_low, left_on, 6), (sv_high, right_on, 8 + columns)):
        for q in range(5):
            value = jnp.where(on, ref[q], 0.0)
            weighted = value * ref[5]
            for i in range(rows):
                wide[q, i + 2, col : col + 2, :] = value[2 * i : 2 * i + 2]
                across[q, i, col : col + 2, :] = weighted[2 * i : 2 * i + 2]

    @pl.loop(0, rows)
    def _(i):
        for t in range(tiles):
            span = slice(8 * t, 8 * t + 8)
            inner = slice(8 * t + 8, 8 * t + 16)
            rho, u1, u2, u3, p = (prim[q, i, span, :] for q in range(5))
            ratio = p / rho
            sound = jnp.sqrt(gamma_ratio * ratio)
            enth[i, span, :] = (gamma_ratio / gm) * ratio + 0.5 * (u1 * u1 + u2 * u2 + u3 * u3)
            radius_u = jnp.abs(u1) + sound
            radius_v = jnp.abs(u2) + sound
            for q in range(5):
                value = psi[q, i, span, :]
                wide[q, i + 2, inner, :] = value
                along[q, i + 2, span, :] = radius_u * value
                across[q, i, inner, :] = radius_v * value

    fraction = jnp.broadcast_to(
        ((lanes((1, 128)) + nrm * depth).astype(f32) + 0.5) / total_depth, (8, 128)
    )

    @pl.loop(0, rows)
    def _(i):
        turned = pltpu.roll(packed, 128 - i, 1)
        for t in range(tiles):
            span = slice(8 * t, 8 * t + 8)
            at = lambda k: slice(8 * t + 8 + k, 8 * t + 16 + k)
            first, second, damp = [], [], []
            for q in range(5):
                first.append(
                    (8.0 / 12.0) * (wide[q, i + 1, at(0), :] - wide[q, i + 3, at(0), :])
                    - (1.0 / 12.0) * (wide[q, i, at(0), :] - wide[q, i + 4, at(0), :])
                )
                second.append(
                    (8.0 / 12.0) * (wide[q, i + 2, at(-1), :] - wide[q, i + 2, at(1), :])
                    - (1.0 / 12.0) * (wide[q, i + 2, at(-2), :] - wide[q, i + 2, at(2), :])
                )
                far = (
                    along[q, i, span, :] + along[q, i + 4, span, :]
                    + across[q, i, at(-2), :] + across[q, i, at(2), :]
                )
                near = (
                    along[q, i + 1, span, :] + along[q, i + 3, span, :]
                    + across[q, i, at(-1), :] + across[q, i, at(1), :]
                )
                here = along[q, i + 2, span, :] + across[q, i, at(0), :]
                damp.append(
                    damping_coef * far - (4.0 * damping_coef) * near + (6.0 * damping_coef) * here
                )
            third = [normal[q, i, span, :] for q in range(5)]
            rho, u1, u2, u3, p = (prim[q, i, span, :] for q in range(5))
            enthalpy = enth[i, span, :]
            kinetic = (0.5 * gm) * (u1 * u1 + u2 * u2 + u3 * u3)
            fluxes = flux_of(rho, u1, u2, u3, p, enthalpy)
            projected = first[1] + second[2] + third[3]
            energy = u1 * first[4] + u2 * second[4] + u3 * third[4]
            dot = lambda g: u1 * g[1] + u2 * g[2] + u3 * g[3]
            dot1, dot2, dot3 = dot(first), dot(second), dot(third)
            mass_row = (
                kinetic * projected
                - (u1 * dot1 + u2 * dot2 + u3 * dot3)
                + (kinetic - enthalpy) * energy
            )
            shared = gm * (projected + energy)
            moved = lambda b: u1 * first[b] + u2 * second[b] + u3 * third[b]
            rows_out = (
                mass_row,
                moved(1) - u1 * shared + (first[0] + dot1 + enthalpy * first[4]),
                moved(2) - u2 * shared + (second[0] + dot2 + enthalpy * second[4]),
                moved(3) - u3 * shared + (third[0] + dot3 + enthalpy * third[4]),
                gm * projected + gamma_ratio * energy,
            )
            ramp = fraction * spread_lane(turned, rows * t)
            for q in range(5):
                result[q, i, span, :] = (
                    target[q, i, span, :] + rows_out[q] + damp[q] + ramp * fluxes[q]
                )


def call(kernel, outs, operands, scratch, flops, name):
    spec = pl.BlockSpec(memory_space=VMEM)
    many = isinstance(outs, (list, tuple))
    size = sum(4 * a.size for a in operands) + sum(
        4 * o.size for o in (outs if many else [outs])
    )
    return pl.pallas_call(
        kernel,
        out_shape=outs,
        in_specs=[spec] * len(operands),
        out_specs=[spec] * len(outs) if many else spec,
        scratch_shapes=scratch,
        cost_estimate=pl.CostEstimate(flops=flops, transcendentals=0, bytes_accessed=size),
        compiler_params=pltpu.CompilerParams(vmem_limit_bytes=16 << 20),
        name=name,
    )(*operands)


def local(
    primitive, adjoint_state, objective_grad, front_height,
    shock_state, state_by_height, state_by_slope, fitted_flags,
):
    _, rows, columns, depth = adjoint_state.shape
    tiles = columns // 8
    su_count, sv_count, lines = (lax.axis_size(a) for a in ("su", "sv", "nrm"))
    fan = su_count * lines
    shape = lambda *s: jax.ShapeDtypeStruct(s, f32)
    points = 5 * rows * columns * depth

    ends, su_low, su_high, sv_low, sv_high = call(
        functools.partial(edges_kernel, rows, tiles),
        [
            shape(columns, 128),
            shape(6, 2, columns, depth),
            shape(6, 2, columns, depth),
            shape(6, 2 * rows, depth),
            shape(6, 2 * rows, depth),
        ],
        (primitive, adjoint_state),
        [],
        4 * points,
        "edges",
    )

    def ring(count, by):
        return [(i, (i + by) % count) for i in range(count)]

    arrived = lax.ppermute(ends, "nrm", [(0, 1), (1, 0)])
    from_low = lax.ppermute(su_high, "su", ring(su_count, 1))
    from_high = lax.ppermute(su_low, "su", ring(su_count, -1))
    from_left = lax.ppermute(sv_high, "sv", ring(sv_count, 1))
    from_right = lax.ppermute(sv_low, "sv", ring(sv_count, -1))

    chunk, normal = call(
        functools.partial(
            lines_kernel, rows, tiles, depth, depth * lines, rows * su_count, fan
        ),
        [shape(fan, 8, 128), shape(5, rows, columns, depth)],
        (
            primitive, adjoint_state, arrived, front_height,
            shock_state, state_by_height, state_by_slope, fitted_flags,
        ),
        [VMEM((3, 128, 128), f32), VMEM((3, 128, 128), f32)],
        12 * points,
        "lines",
    )
    chunks = lax.all_to_all(chunk, ("su", "nrm"), 0, 0)
    result, slope = call(
        functools.partial(
            final_kernel, rows, tiles, depth, depth * lines, su_count, sv_count, fan
        ),
        [shape(5, rows, columns, depth), shape(rows, columns)],
        (
            primitive, adjoint_state, objective_grad, normal,
            from_low, from_high, from_left, from_right, chunks,
        ),
        [
            VMEM((5, rows + 4, columns + 16, depth), f32),
            VMEM((5, rows + 4, columns, depth), f32),
            VMEM((5, rows, columns + 16, depth), f32),
            VMEM((rows, columns, depth), f32),
            VMEM((128, 128), f32),
        ],
        40 * points,
        "final",
    )
    return result, slope


def solution(mesh):
    wide = P(None, "su", "sv", "nrm")
    flat = P("su", "sv")
    front = P(None, "su", "sv")
    return jax.shard_map(
        local,
        mesh=mesh,
        in_specs=(wide, wide, wide, flat, front, front, front, flat),
        out_specs=(wide, flat),
        check_vma=False,
    )
```

```python
import functools

import jax
import jax.numpy as jnp
from jax import lax
from jax.experimental import pallas as pl
from jax.experimental.pallas import tpu as pltpu
from jax.sharding import PartitionSpec as P

gamma_ratio = 1.4
damping_coef = 0.0625
stretch_rate = 2.2
gm = gamma_ratio - 1.0
f32 = jnp.float32
VMEM = pltpu.VMEM


def lanes(shape=(8, 128)):
    return lax.broadcasted_iota(jnp.int32, shape, 1)


def spread_lane(tile, lane):
    return jnp.broadcast_to(tile[:, lane : lane + 1], tile.shape)


def inv_stretch_at(index, total_depth):
    return 1.0 / jnp.exp(stretch_rate * ((index + 0.5) / total_depth - 1.0))


def even(axis):
    return lax.rem(lax.axis_index(axis), 2) == 0


def flux_of(rho, u1, u2, u3, p, enthalpy):
    mass = rho * u3
    return (mass, mass * u1, mass * u2, mass * u3 + p, mass * enthalpy)


def thermo(rho, u1, u2, u3, p):
    half = 0.5 * (u1 * u1 + u2 * u2 + u3 * u3)
    return gm * half, (gamma_ratio / gm) * (p / rho) + half


def part(array, q, rows):
    return pltpu.roll(array, 128 - rows * q, 1) if q else array


def prepare_kernel(
    rows, tiles, depth, total_depth,
    prim, psi, height, shock, by_height, by_slope, flags,
    packet, su_a, su_b, sv_a, sv_b, normal, flux, enth, tone, inverse,
    turn, facts, tops,
):
    nrm = lax.axis_index("nrm")
    first = nrm == 0
    lane = lanes()
    lane_row = lanes((1, 128))
    columns = 8 * tiles

    turn[...] = jnp.zeros_like(turn)
    tops[...] = jnp.zeros_like(tops)
    for place, array in enumerate(
        [height[...]]
        + [shock[q] for q in range(5)]
        + [flags[...].astype(f32)]
    ):
        turn[0, rows * place : rows * place + rows, 0:columns] = array
    for q in range(5):
        turn[1, rows * q : rows * q + rows, 0:columns] = by_height[q]
        turn[2, rows * q : rows * q + rows, 0:columns] = by_slope[q]
    for n in range(3):
        facts[n] = turn[n].T
    for t in range(tiles):
        span = slice(8 * t, 8 * t + 8)
        inverse[span, :] = jnp.where(
            lane < rows, 1.0 / jnp.where(lane < rows, facts[0, span, :], 1.0), 0.0
        )

    for t in range(tiles):
        span = slice(8 * t, 8 * t + 8)
        for i in range(rows):
            rho, u1, u2, u3, p = (prim[q, i, span, :] for q in range(5))
            ratio = p / rho
            enthalpy = (gamma_ratio / gm) * ratio + 0.5 * (u1 * u1 + u2 * u2 + u3 * u3)
            for q, value in enumerate(flux_of(rho, u1, u2, u3, p, enthalpy)):
                flux[q, i, span, :] = value
            enth[i, span, :] = enthalpy
            tone[i, span, :] = jnp.sqrt(gamma_ratio * ratio)

    extra = jnp.where(first, 1, 0)
    for t in range(tiles):
        span = slice(8 * t, 8 * t + 8)
        for half, ref in ((0, psi), (1, flux)):
            packed = jnp.zeros((8, 128), f32)
            for q in range(5):
                for i in range(rows):
                    spot = rows * q + i
                    moved = pltpu.roll(ref[q, i, span, :], spot + extra, 1)
                    packed = jnp.where(lane == spot, moved, packed)
            packet[span, 128 * half : 128 * half + 128] = packed

    @pl.when(jnp.logical_not(first))
    def _():
        for t in range(tiles):
            span = slice(8 * t, 8 * t + 8)
            packed = jnp.zeros((8, 128), f32)
            for q in range(5):
                for i in range(rows):
                    spot = rows * q + i
                    moved = pltpu.roll(psi[q, i, span, :], spot + 1, 1)
                    packed = jnp.where(lane == spot, moved, packed)
            tops[span, :] = packed

    depth_index = (lane_row + nrm * depth).astype(f32)
    weight = 0.5 * inv_stretch_at(depth_index, total_depth)
    lower = jnp.broadcast_to(jnp.where(lane_row == depth - 1, 0.0, weight), (8, 128))
    upper = jnp.broadcast_to(jnp.where(lane_row == 0, 0.0, weight), (8, 128))
    top_scale = 0.5 * inv_stretch_at(
        jnp.full((1, 128), total_depth - 1, f32), total_depth
    )
    front = jnp.where(first, 0.0, 1.0)
    for t in range(tiles):
        span = slice(8 * t, 8 * t + 8)
        inv_height = inverse[span, :]
        gathered = jnp.zeros((8, 128), f32)
        for i in range(rows):
            inv = spread_lane(inv_height, i)
            low, high = lower * inv, upper * inv
            work = None
            for q in range(5):
                value = psi[q, i, span, :]
                step = pltpu.roll(value * low, 1, 1) - pltpu.roll(value * high, 127, 1)
                normal[q, i, span, :] = step
                term = flux[q, i, span, :] * step
                work = term if work is None else work + term
            summed = jnp.broadcast_to(jnp.sum(work, axis=1, keepdims=True), (8, 128))
            gathered = jnp.where(lane == i, summed, gathered)

        inside = lane < rows
        surf = facts[0, span, :]
        rho, u1, u2, u3, p = (
            jnp.where(inside, part(surf, q + 1, rows), 1.0) for q in range(5)
        )
        fitted = jnp.where(inside, part(surf, 6, rows), 0.0)
        scale = top_scale * inv_height
        last = tops[span, :]
        s0, s1, s2, s3, s4 = (part(last, q, rows) * scale for q in range(5))
        kinetic, enthalpy = thermo(rho, u1, u2, u3, p)
        fluxes = flux_of(rho, u1, u2, u3, p, enthalpy)
        top_work = (
            fluxes[0] * s0 + fluxes[1] * s1 + fluxes[2] * s2 + fluxes[3] * s3 + fluxes[4] * s4
        )
        dotted = u1 * s1 + u2 * s2 + u3 * s3
        shared = gm * (s3 + u3 * s4)
        common = s0 + dotted + enthalpy * s4
        adjoint = (
            kinetic * s3 - u3 * dotted + u3 * (kinetic - enthalpy) * s4,
            u3 * s1 - u1 * shared,
            u3 * s2 - u2 * shared,
            u3 * s3 - u3 * shared + common,
            gm * s3 + gamma_ratio * u3 * s4,
        )
        heights = facts[1, span, :]
        slopes = facts[2, span, :]
        by_h = sum(adjoint[q] * part(heights, q, rows) for q in range(5))
        by_s = sum(adjoint[q] * part(slopes, q, rows) for q in range(5))
        metric = -inv_height * (gathered + front * top_work)
        term = jnp.where(inside, metric + front * fitted * by_h, 0.0)
        tilt = jnp.where(inside, front * fitted * by_s, 0.0)
        packet[span, 0:128] = (
            packet[span, 0:128] + pltpu.roll(term, 5 * rows, 1) + pltpu.roll(tilt, 6 * rows, 1)
        )

    su_even, sv_even = even("su"), even("sv")
    high_row = rows - 2
    row_a = jnp.where(su_even, high_row, 0)
    row_b = high_row - row_a
    for r in range(2):
        for ref, row in ((su_a, row_a + r), (su_b, row_b + r)):
            for q in range(5):
                ref[q, r] = psi[q, row]
            ref[5, r] = jnp.abs(prim[1, row]) + tone[row]
    for i in range(rows):
        pair = slice(2 * i, 2 * i + 2)
        for q in range(6):
            if q < 5:
                low, high = psi[q, i, 0:2, :], psi[q, i, columns - 2 : columns, :]
            else:
                low = jnp.abs(prim[2, i, 0:2, :]) + tone[i, 0:2, :]
                high = (
                    jnp.abs(prim[2, i, columns - 2 : columns, :])
                    + tone[i, columns - 2 : columns, :]
                )
            sv_a[q, pair, :] = jnp.where(sv_even, high, low)
            sv_b[q, pair, :] = jnp.where(sv_even, low, high)


def join_kernel(rows, tiles, depth, total_depth, surface, fan, *refs):
    own, arrived, inverse = refs[:3]
    chunk, mine = refs[-2:]
    first = lax.axis_index("nrm") == 0
    lane = lanes()
    one = jnp.zeros((1, 128), f32)
    before = 0.5 * inv_stretch_at(one + (depth - 1), total_depth)
    after = 0.5 * inv_stretch_at(one + depth, total_depth)
    own_scale = jnp.where(first, before, after)
    far_scale = jnp.where(first, after, before)
    sign = jnp.where(first, 1.0, -1.0)
    sums = jnp.zeros((8, 128), f32)
    kept = jnp.zeros((8, 128), f32)
    for t in range(tiles):
        span = slice(8 * t, 8 * t + 8)
        near, near_flux = own[span, 0:128], own[span, 128:256]
        far, far_flux = arrived[span, 0:128], arrived[span, 128:256]
        cross = near_flux * (far * far_scale) - far_flux * (near * own_scale)
        cross = jnp.where(lane < 5 * rows, cross, 0.0)
        for d in (1, 2, 4):
            cross = cross + pltpu.roll(cross, rows * d, 1)
        inv_height = inverse[span, :]
        total = near + far
        inside = lane < rows
        term = jnp.where(
            inside, part(total, 5, rows) + sign * inv_height * inv_height * cross, 0.0
        )
        for d in (1, 2, 4, 8):
            term = term + pltpu.roll(term, 128 - d, 1)
        share = term * (1.0 / surface)
        slope = jnp.where(inside, share + part(total, 6, rows), 0.0)
        kept = kept + (pltpu.roll(slope, rows * t, 1) if t else slope)
        sums = jnp.where(lane == t, pltpu.roll(share, t, 1) if t else share, sums)
    mine[...] = kept
    for n in range(fan):
        chunk[n] = sums


def final_kernel(
    rows, tiles, depth, total_depth, su_count, sv_count,
    prim, psi, target, normal, flux, enth, tone, inverse, arrived, mine,
    su_a, su_b, sv_a, sv_b, chunks,
    result, slope,
    wide, along, across, turn, done, sems,
):
    su, sv, nrm = lax.axis_index("su"), lax.axis_index("sv"), lax.axis_index("nrm")
    first = nrm == 0
    lane = lanes()
    columns = 8 * tiles
    ahead = jnp.zeros((8, 128), f32)
    for n in range(su_count):
        ahead = ahead + jnp.where(n > su, chunks[n], 0.0)
    upstream = jnp.zeros((8, 128), f32)
    for t in range(tiles):
        upstream = jnp.where(
            (lane >= rows * t) & (lane < rows * t + rows), spread_lane(ahead, t), upstream
        )
    packed = mine[...] + upstream
    turn[...] = jnp.zeros_like(turn)
    for t in range(tiles):
        turn[8 * t : 8 * t + 8, :] = pltpu.roll(packed, 128 - rows * t, 1) if t else packed
    slope[...] = turn[...].T[0:rows, 0:columns]

    su_even, sv_even = even("su"), even("sv")
    low_on, high_on = su > 0, su < su_count - 1
    for r in range(2):
        for swap, on, row in ((su_even, low_on, r), (~su_even, high_on, rows + 2 + r)):
            pick = lambda q: jnp.where(swap, su_b[q, r], su_a[q, r])
            radius = pick(5)
            for q in range(5):
                value = jnp.where(on, pick(q), 0.0)
                wide[q, row, 8 : 8 + columns, :] = value
                along[q, row] = value * radius
    left_on, right_on = sv > 0, sv < sv_count - 1
    for swap, on, col in ((sv_even, left_on, 6), (~sv_even, right_on, 8 + columns)):
        radius = jnp.where(swap, sv_b[5], sv_a[5])
        for q in range(5):
            value = jnp.where(on, jnp.where(swap, sv_b[q], sv_a[q]), 0.0)
            weighted = value * radius
            for i in range(rows):
                wide[q, i + 2, col : col + 2, :] = value[2 * i : 2 * i + 2]
                across[q, i, col : col + 2, :] = weighted[2 * i : 2 * i + 2]

    @pl.loop(0, rows)
    def _(i):
        for t in range(tiles):
            span = slice(8 * t, 8 * t + 8)
            inner = slice(8 * t + 8, 8 * t + 16)
            sound = tone[i, span, :]
            radius_u = jnp.abs(prim[1, i, span, :]) + sound
            radius_v = jnp.abs(prim[2, i, span, :]) + sound
            for q in range(5):
                value = psi[q, i, span, :]
                wide[q, i + 2, inner, :] = value
                along[q, i + 2, span, :] = radius_u * value
                across[q, i, inner, :] = radius_v * value

    fraction = jnp.broadcast_to(
        ((lanes((1, 128)) + nrm * depth).astype(f32) + 0.5) / total_depth, (8, 128)
    )
    one = jnp.zeros((1, 128), f32)
    edge_scale = jnp.where(
        first,
        -0.5 * inv_stretch_at(one + depth, total_depth),
        0.5 * inv_stretch_at(one + (depth - 1), total_depth),
    )
    entry = jnp.where(first, depth - 1, 0)
    at_entry = lane == entry
    for t in range(tiles):
        span = slice(8 * t, 8 * t + 8)
        repeated = inverse[span, :]
        for d in (1, 2, 4):
            repeated = repeated + pltpu.roll(repeated, rows * d, 1)
        turn[span, :] = arrived[span, 0:128] * edge_scale * repeated

    def out_copy(i):
        return pltpu.make_async_copy(done.at[:, i], result.at[:, i], sems.at[i])

    @pl.loop(0, rows)
    def _(i):
        turned = pltpu.roll(packed, 128 - i, 1)
        for t in range(tiles):
            span = slice(8 * t, 8 * t + 8)
            at = lambda k: slice(8 * t + 8 + k, 8 * t + 16 + k)
            ends = turn[span, :]
            first, second, third, damp = [], [], [], []
            for q in range(5):
                first.append(
                    (8.0 / 12.0) * (wide[q, i + 1, at(0), :] - wide[q, i + 3, at(0), :])
                    - (1.0 / 12.0) * (wide[q, i, at(0), :] - wide[q, i + 4, at(0), :])
                )
                second.append(
                    (8.0 / 12.0) * (wide[q, i + 2, at(-1), :] - wide[q, i + 2, at(1), :])
                    - (1.0 / 12.0) * (wide[q, i + 2, at(-2), :] - wide[q, i + 2, at(2), :])
                )
                far = (
                    along[q, i, span, :] + along[q, i + 4, span, :]
                    + across[q, i, at(-2), :] + across[q, i, at(2), :]
                )
                near = (
                    along[q, i + 1, span, :] + along[q, i + 3, span, :]
                    + across[q, i, at(-1), :] + across[q, i, at(1), :]
                )
                here = along[q, i + 2, span, :] + across[q, i, at(0), :]
                damp.append(
                    damping_coef * far - (4.0 * damping_coef) * near + (6.0 * damping_coef) * here
                )
                came = pltpu.roll(ends, entry + (128 - rows * q) - i, 1)
                third.append(normal[q, i, span, :] + jnp.where(at_entry, came, 0.0))
            u1, u2, u3 = (prim[q, i, span, :] for q in (1, 2, 3))
            enthalpy = enth[i, span, :]
            kinetic = (0.5 * gm) * (u1 * u1 + u2 * u2 + u3 * u3)
            projected = first[1] + second[2] + third[3]
            energy = u1 * first[4] + u2 * second[4] + u3 * third[4]
            dot = lambda g: u1 * g[1] + u2 * g[2] + u3 * g[3]
            dot1, dot2, dot3 = dot(first), dot(second), dot(third)
            mass_row = (
                kinetic * projected
                - (u1 * dot1 + u2 * dot2 + u3 * dot3)
                + (kinetic - enthalpy) * energy
            )
            shared = gm * (projected + energy)
            moved = lambda b: u1 * first[b] + u2 * second[b] + u3 * third[b]
            rows_out = (
                mass_row,
                moved(1) - u1 * shared + (first[0] + dot1 + enthalpy * first[4]),
                moved(2) - u2 * shared + (second[0] + dot2 + enthalpy * second[4]),
                moved(3) - u3 * shared + (third[0] + dot3 + enthalpy * third[4]),
                gm * projected + gamma_ratio * energy,
            )
            ramp = fraction * spread_lane(turned, rows * t)
            for q in range(5):
                done[q, i, span, :] = (
                    target[q, i, span, :] + rows_out[q] + damp[q] + ramp * flux[q, i, span, :]
                )
        out_copy(i).start()

    @pl.loop(0, rows)
    def _(i):
        out_copy(i).wait()


def call(kernel, outs, operands, scratch, flops, name, spaces=None):
    spec = pl.BlockSpec(memory_space=VMEM)
    size = sum(4 * a.size for a in operands) + sum(4 * o.size for o in outs)
    return pl.pallas_call(
        kernel,
        out_shape=outs,
        in_specs=[spec] * len(operands),
        out_specs=[pl.BlockSpec(memory_space=s) for s in (spaces or [VMEM] * len(outs))],
        scratch_shapes=scratch,
        cost_estimate=pl.CostEstimate(flops=flops, transcendentals=0, bytes_accessed=size),
        compiler_params=pltpu.CompilerParams(vmem_limit_bytes=16 << 20),
        name=name,
    )(*operands)


def local(
    primitive, adjoint_state, objective_grad, front_height,
    shock_state, state_by_height, state_by_slope, fitted_flags,
):
    _, rows, columns, depth = adjoint_state.shape
    tiles = columns // 8
    su_count, sv_count, lines = (lax.axis_size(a) for a in ("su", "sv", "nrm"))
    total_depth = depth * lines
    shape = lambda *s: jax.ShapeDtypeStruct(s, f32)
    field = shape(5, rows, columns, depth)
    plane = shape(rows, columns, depth)
    points = 5 * rows * columns * depth

    packet, su_a, su_b, sv_a, sv_b, normal, flux, enth, tone, inverse = call(
        functools.partial(prepare_kernel, rows, tiles, depth, total_depth),
        [
            shape(columns, 256),
            shape(6, 2, columns, depth),
            shape(6, 2, columns, depth),
            shape(6, 2 * rows, depth),
            shape(6, 2 * rows, depth),
            field, field, plane, plane,
            shape(columns, 128),
        ],
        (
            primitive, adjoint_state, front_height,
            shock_state, state_by_height, state_by_slope, fitted_flags,
        ),
        [VMEM((3, 128, 128), f32), VMEM((3, 128, 128), f32), VMEM((columns, 128), f32)],
        12 * points,
        "prepare",
    )

    def pairs(count, shift):
        out = []
        for i in range(0, count, 2):
            a, b = (i + shift) % count, (i + shift + 1) % count
            out += [(a, b), (b, a)]
        return out

    arrived = lax.ppermute(packet, "nrm", [(0, 1), (1, 0)])
    su_a = lax.ppermute(su_a, "su", pairs(su_count, 0))
    su_b = lax.ppermute(su_b, "su", pairs(su_count, 1))
    sv_a = lax.ppermute(sv_a, "sv", pairs(sv_count, 0))
    sv_b = lax.ppermute(sv_b, "sv", pairs(sv_count, 1))

    chunk, mine = call(
        functools.partial(
            join_kernel, rows, tiles, depth, total_depth, rows * su_count, su_count
        ),
        [shape(su_count, 8, 128), shape(8, 128)],
        (packet, arrived, inverse, su_a, su_b, sv_a, sv_b),
        [],
        points // 40,
        "join",
    )
    chunks = lax.all_to_all(chunk, "su", 0, 0)
    result, slope = call(
        functools.partial(
            final_kernel, rows, tiles, depth, total_depth, su_count, sv_count
        ),
        [field, shape(rows, columns)],
        (
            primitive, adjoint_state, objective_grad, normal, flux, enth, tone, inverse,
            arrived, mine, su_a, su_b, sv_a, sv_b, chunks,
        ),
        [
            VMEM((5, rows + 4, columns + 16, depth), f32),
            VMEM((5, rows + 4, columns, depth), f32),
            VMEM((5, rows, columns + 16, depth), f32),
            VMEM((128, 128), f32),
            VMEM((5, rows, columns, depth), f32),
            pltpu.SemaphoreType.DMA((rows,)),
        ],
        40 * points,
        "final",
        [pltpu.HBM, VMEM],
    )
    return result, slope


def solution(mesh):
    wide = P(None, "su", "sv", "nrm")
    flat = P("su", "sv")
    front = P(None, "su", "sv")
    return jax.shard_map(
        local,
        mesh=mesh,
        in_specs=(wide, wide, wide, flat, front, front, front, flat),
        out_specs=(wide, flat),
        check_vma=False,
    )
```

```python
import functools

import jax
import jax.numpy as jnp
from jax import lax
from jax.experimental import pallas as pl
from jax.experimental.pallas import tpu as pltpu
from jax.sharding import PartitionSpec as P

gamma_ratio = 1.4
damping_coef = 0.0625
stretch_rate = 2.2
gm = gamma_ratio - 1.0
f32 = jnp.float32
VMEM = pltpu.VMEM


def lanes(shape=(8, 128)):
    return lax.broadcasted_iota(jnp.int32, shape, 1)


def spread_lane(tile, lane):
    return jnp.broadcast_to(tile[:, lane : lane + 1], tile.shape)


def inv_stretch_at(index, total_depth):
    return 1.0 / jnp.exp(stretch_rate * ((index + 0.5) / total_depth - 1.0))


def even(axis):
    return lax.rem(lax.axis_index(axis), 2) == 0


def flux_of(rho, u1, u2, u3, p, enthalpy):
    mass = rho * u3
    return (mass, mass * u1, mass * u2, mass * u3 + p, mass * enthalpy)


def thermo(rho, u1, u2, u3, p):
    half = 0.5 * (u1 * u1 + u2 * u2 + u3 * u3)
    return gm * half, (gamma_ratio / gm) * (p / rho) + half


def part(array, q, rows):
    return pltpu.roll(array, 128 - rows * q, 1) if q else array


def prepare_kernel(
    rows, tiles, depth, total_depth, step_rows,
    prim_far, psi_far, height_far, shock_far, by_height_far, by_slope_far, flags_far,
    packet, su_a, su_b, sv_a, sv_b, normal, flux, enth, tone, inverse, prim, psi,
    turn, facts, tops, spread, work, height, shock, by_height, by_slope, flags, small, large,
):
    surfaces = [
        pltpu.make_async_copy(far, near, small.at[n])
        for n, (far, near) in enumerate(
            (
                (height_far, height),
                (shock_far, shock),
                (by_height_far, by_height),
                (by_slope_far, by_slope),
                (flags_far, flags),
            )
        )
    ]
    chunks = rows // step_rows
    loads = []
    for c in range(chunks):
        part_rows = pl.ds(c * step_rows, step_rows)
        loads.append(
            [
                pltpu.make_async_copy(far.at[:, part_rows], near.at[:, part_rows], large.at[n, c])
                for n, (far, near) in enumerate(((prim_far, prim), (psi_far, psi)))
            ]
        )
    for copy in surfaces:
        copy.start()
    for pair in loads:
        for copy in pair:
            copy.start()

    nrm = lax.axis_index("nrm")
    first = nrm == 0
    lane = lanes()
    lane_row = lanes((1, 128))
    columns = 8 * tiles
    spans = [slice(8 * t, 8 * t + 8) for t in range(tiles)]
    depth_index = (lane_row + nrm * depth).astype(f32)
    weight = 0.5 * inv_stretch_at(depth_index, total_depth)
    lower = jnp.broadcast_to(jnp.where(lane_row == depth - 1, 0.0, weight), (8, 128))
    upper = jnp.broadcast_to(jnp.where(lane_row == 0, 0.0, weight), (8, 128))
    top_scale = 0.5 * inv_stretch_at(
        jnp.full((1, 128), total_depth - 1, f32), total_depth
    )
    front = jnp.where(first, 0.0, 1.0)
    extra = jnp.where(first, 1, 0)

    turn[...] = jnp.zeros_like(turn)
    tops[...] = jnp.zeros_like(tops)
    packet[...] = jnp.zeros_like(packet)
    for copy in surfaces:
        copy.wait()
    for place, array in enumerate(
        [height[...]]
        + [shock[q] for q in range(5)]
        + [flags[...].astype(f32)]
    ):
        turn[0, rows * place : rows * place + rows, 0:columns] = array
    for q in range(5):
        turn[1, rows * q : rows * q + rows, 0:columns] = by_height[q]
        turn[2, rows * q : rows * q + rows, 0:columns] = by_slope[q]
    for n in range(3):
        facts[n] = turn[n].T
    for span in spans:
        inverse[span, :] = jnp.where(
            lane < rows, 1.0 / jnp.where(lane < rows, facts[0, span, :], 1.0), 0.0
        )
    for span in spans:
        inv_height = inverse[span, :]
        for i in range(rows):
            spread[i, span, :] = spread_lane(inv_height, i)

    for c in range(chunks):
        for copy in loads[c]:
            copy.wait()
        mine = range(c * step_rows, (c + 1) * step_rows)
        for i in mine:
            for span in spans:
                rho, u1, u2, u3, p = (prim[q, i, span, :] for q in range(5))
                ratio = p / rho
                enthalpy = (gamma_ratio / gm) * ratio + 0.5 * (u1 * u1 + u2 * u2 + u3 * u3)
                for q, value in enumerate(flux_of(rho, u1, u2, u3, p, enthalpy)):
                    flux[q, i, span, :] = value
                enth[i, span, :] = enthalpy
                tone[i, span, :] = jnp.sqrt(gamma_ratio * ratio)
        for i in mine:
            for span in spans:
                inv = spread[i, span, :]
                low, high = lower * inv, upper * inv
                total = None
                for q in range(5):
                    value = psi[q, i, span, :]
                    step = pltpu.roll(value * low, 1, 1) - pltpu.roll(value * high, 127, 1)
                    normal[q, i, span, :] = step
                    term = flux[q, i, span, :] * step
                    total = term if total is None else total + term
                work[i, span, :] = total
        for span in spans:
            for half, ref in ((0, psi), (1, flux)):
                packed = packet[span, 128 * half : 128 * half + 128]
                for q in range(5):
                    for i in mine:
                        spot = rows * q + i
                        moved = pltpu.roll(ref[q, i, span, :], spot + extra, 1)
                        packed = jnp.where(lane == spot, moved, packed)
                packet[span, 128 * half : 128 * half + 128] = packed

    @pl.when(jnp.logical_not(first))
    def _():
        for span in spans:
            packed = jnp.zeros((8, 128), f32)
            for q in range(5):
                for i in range(rows):
                    spot = rows * q + i
                    moved = pltpu.roll(psi[q, i, span, :], spot + 1, 1)
                    packed = jnp.where(lane == spot, moved, packed)
            tops[span, :] = packed

    for span in spans:
        gathered = jnp.zeros((8, 128), f32)
        for i in range(rows):
            total = jnp.sum(work[i, span, :], axis=1, keepdims=True)
            gathered = jnp.where(lane == i, jnp.broadcast_to(total, (8, 128)), gathered)
        turn[0, span, :] = gathered

    for span in spans:
        inv_height = inverse[span, :]
        gathered = turn[0, span, :]
        inside = lane < rows
        surf = facts[0, span, :]
        rho, u1, u2, u3, p = (
            jnp.where(inside, part(surf, q + 1, rows), 1.0) for q in range(5)
        )
        fitted = jnp.where(inside, part(surf, 6, rows), 0.0)
        scale = top_scale * inv_height
        last = tops[span, :]
        s0, s1, s2, s3, s4 = (part(last, q, rows) * scale for q in range(5))
        kinetic, enthalpy = thermo(rho, u1, u2, u3, p)
        fluxes = flux_of(rho, u1, u2, u3, p, enthalpy)
        top_work = (
            fluxes[0] * s0 + fluxes[1] * s1 + fluxes[2] * s2 + fluxes[3] * s3 + fluxes[4] * s4
        )
        dotted = u1 * s1 + u2 * s2 + u3 * s3
        shared = gm * (s3 + u3 * s4)
        common = s0 + dotted + enthalpy * s4
        adjoint = (
            kinetic * s3 - u3 * dotted + u3 * (kinetic - enthalpy) * s4,
            u3 * s1 - u1 * shared,
            u3 * s2 - u2 * shared,
            u3 * s3 - u3 * shared + common,
            gm * s3 + gamma_ratio * u3 * s4,
        )
        heights = facts[1, span, :]
        slopes = facts[2, span, :]
        by_h = sum(adjoint[q] * part(heights, q, rows) for q in range(5))
        by_s = sum(adjoint[q] * part(slopes, q, rows) for q in range(5))
        metric = -inv_height * (gathered + front * top_work)
        term = jnp.where(inside, metric + front * fitted * by_h, 0.0)
        tilt = jnp.where(inside, front * fitted * by_s, 0.0)
        packet[span, 0:128] = (
            packet[span, 0:128] + pltpu.roll(term, 5 * rows, 1) + pltpu.roll(tilt, 6 * rows, 1)
        )

    su_even, sv_even = even("su"), even("sv")
    high_row = rows - 2
    row_a = jnp.where(su_even, high_row, 0)
    row_b = high_row - row_a
    for r in range(2):
        for ref, row in ((su_a, row_a + r), (su_b, row_b + r)):
            for q in range(5):
                ref[q, r] = psi[q, row]
            ref[5, r] = jnp.abs(prim[1, row]) + tone[row]
    for i in range(rows):
        pair = slice(2 * i, 2 * i + 2)
        for q in range(6):
            if q < 5:
                low, high = psi[q, i, 0:2, :], psi[q, i, columns - 2 : columns, :]
            else:
                low = jnp.abs(prim[2, i, 0:2, :]) + tone[i, 0:2, :]
                high = (
                    jnp.abs(prim[2, i, columns - 2 : columns, :])
                    + tone[i, columns - 2 : columns, :]
                )
            sv_a[q, pair, :] = jnp.where(sv_even, high, low)
            sv_b[q, pair, :] = jnp.where(sv_even, low, high)


def join_kernel(rows, tiles, depth, total_depth, surface, fan, *refs):
    own, arrived, inverse = refs[:3]
    chunk, mine = refs[-2:]
    first = lax.axis_index("nrm") == 0
    lane = lanes()
    one = jnp.zeros((1, 128), f32)
    before = 0.5 * inv_stretch_at(one + (depth - 1), total_depth)
    after = 0.5 * inv_stretch_at(one + depth, total_depth)
    own_scale = jnp.where(first, before, after)
    far_scale = jnp.where(first, after, before)
    sign = jnp.where(first, 1.0, -1.0)
    sums = jnp.zeros((8, 128), f32)
    kept = jnp.zeros((8, 128), f32)
    for t in range(tiles):
        span = slice(8 * t, 8 * t + 8)
        near, near_flux = own[span, 0:128], own[span, 128:256]
        far, far_flux = arrived[span, 0:128], arrived[span, 128:256]
        cross = near_flux * (far * far_scale) - far_flux * (near * own_scale)
        cross = jnp.where(lane < 5 * rows, cross, 0.0)
        for d in (1, 2, 4):
            cross = cross + pltpu.roll(cross, rows * d, 1)
        inv_height = inverse[span, :]
        total = near + far
        inside = lane < rows
        term = jnp.where(
            inside, part(total, 5, rows) + sign * inv_height * inv_height * cross, 0.0
        )
        for d in (1, 2, 4, 8):
            term = term + pltpu.roll(term, 128 - d, 1)
        share = term * (1.0 / surface)
        slope = jnp.where(inside, share + part(total, 6, rows), 0.0)
        kept = kept + (pltpu.roll(slope, rows * t, 1) if t else slope)
        sums = jnp.where(lane == t, pltpu.roll(share, t, 1) if t else share, sums)
    mine[...] = kept
    for n in range(fan):
        chunk[n] = sums


def final_kernel(
    rows, tiles, depth, total_depth, su_count, sv_count,
    prim, psi, target_far, normal, flux, enth, tone, inverse, arrived, mine,
    su_a, su_b, sv_a, sv_b, chunks,
    result, slope,
    wide, along, across, turn, done, target, sems, large,
):
    step_rows = 4
    loads = [
        pltpu.make_async_copy(
            target_far.at[:, pl.ds(r, step_rows)], target.at[:, pl.ds(r, step_rows)],
            large.at[r // step_rows],
        )
        for r in range(0, rows, step_rows)
    ]
    for copy in loads:
        copy.start()
    su, sv, nrm = lax.axis_index("su"), lax.axis_index("sv"), lax.axis_index("nrm")
    first = nrm == 0
    lane = lanes()
    columns = 8 * tiles
    ahead = jnp.zeros((8, 128), f32)
    for n in range(su_count):
        ahead = ahead + jnp.where(n > su, chunks[n], 0.0)
    upstream = jnp.zeros((8, 128), f32)
    for t in range(tiles):
        upstream = jnp.where(
            (lane >= rows * t) & (lane < rows * t + rows), spread_lane(ahead, t), upstream
        )
    packed = mine[...] + upstream
    turn[...] = jnp.zeros_like(turn)
    for t in range(tiles):
        turn[8 * t : 8 * t + 8, :] = pltpu.roll(packed, 128 - rows * t, 1) if t else packed
    slope[...] = turn[...].T[0:rows, 0:columns]

    su_even, sv_even = even("su"), even("sv")
    low_on, high_on = su > 0, su < su_count - 1
    for r in range(2):
        for swap, on, row in ((su_even, low_on, r), (~su_even, high_on, rows + 2 + r)):
            pick = lambda q: jnp.where(swap, su_b[q, r], su_a[q, r])
            radius = pick(5)
            for q in range(5):
                value = jnp.where(on, pick(q), 0.0)
                wide[q, row, 8 : 8 + columns, :] = value
                along[q, row] = value * radius
    left_on, right_on = sv > 0, sv < sv_count - 1
    for swap, on, col in ((sv_even, left_on, 6), (~sv_even, right_on, 8 + columns)):
        radius = jnp.where(swap, sv_b[5], sv_a[5])
        for q in range(5):
            value = jnp.where(on, jnp.where(swap, sv_b[q], sv_a[q]), 0.0)
            weighted = value * radius
            for i in range(rows):
                wide[q, i + 2, col : col + 2, :] = value[2 * i : 2 * i + 2]
                across[q, i, col : col + 2, :] = weighted[2 * i : 2 * i + 2]

    @pl.loop(0, rows)
    def _(i):
        for t in range(tiles):
            span = slice(8 * t, 8 * t + 8)
            inner = slice(8 * t + 8, 8 * t + 16)
            sound = tone[i, span, :]
            radius_u = jnp.abs(prim[1, i, span, :]) + sound
            radius_v = jnp.abs(prim[2, i, span, :]) + sound
            for q in range(5):
                value = psi[q, i, span, :]
                wide[q, i + 2, inner, :] = value
                along[q, i + 2, span, :] = radius_u * value
                across[q, i, inner, :] = radius_v * value

    fraction = jnp.broadcast_to(
        ((lanes((1, 128)) + nrm * depth).astype(f32) + 0.5) / total_depth, (8, 128)
    )
    one = jnp.zeros((1, 128), f32)
    edge_scale = jnp.where(
        first,
        -0.5 * inv_stretch_at(one + depth, total_depth),
        0.5 * inv_stretch_at(one + (depth - 1), total_depth),
    )
    entry = jnp.where(first, depth - 1, 0)
    at_entry = lane == entry
    for t in range(tiles):
        span = slice(8 * t, 8 * t + 8)
        repeated = inverse[span, :]
        for d in (1, 2, 4):
            repeated = repeated + pltpu.roll(repeated, rows * d, 1)
        turn[span, :] = arrived[span, 0:128] * edge_scale * repeated

    def out_copy(i):
        return pltpu.make_async_copy(done.at[:, i], result.at[:, i], sems.at[i])

    def finish(i):
        turned = pltpu.roll(packed, 128 - i, 1)
        for t in range(tiles):
            span = slice(8 * t, 8 * t + 8)
            at = lambda k: slice(8 * t + 8 + k, 8 * t + 16 + k)
            ends = turn[span, :]
            first, second, third, damp = [], [], [], []
            for q in range(5):
                first.append(
                    (8.0 / 12.0) * (wide[q, i + 1, at(0), :] - wide[q, i + 3, at(0), :])
                    - (1.0 / 12.0) * (wide[q, i, at(0), :] - wide[q, i + 4, at(0), :])
                )
                second.append(
                    (8.0 / 12.0) * (wide[q, i + 2, at(-1), :] - wide[q, i + 2, at(1), :])
                    - (1.0 / 12.0) * (wide[q, i + 2, at(-2), :] - wide[q, i + 2, at(2), :])
                )
                far = (
                    along[q, i, span, :] + along[q, i + 4, span, :]
                    + across[q, i, at(-2), :] + across[q, i, at(2), :]
                )
                near = (
                    along[q, i + 1, span, :] + along[q, i + 3, span, :]
                    + across[q, i, at(-1), :] + across[q, i, at(1), :]
                )
                here = along[q, i + 2, span, :] + across[q, i, at(0), :]
                damp.append(
                    damping_coef * far - (4.0 * damping_coef) * near + (6.0 * damping_coef) * here
                )
                came = pltpu.roll(ends, entry + (128 - rows * q) - i, 1)
                third.append(normal[q, i, span, :] + jnp.where(at_entry, came, 0.0))
            u1, u2, u3 = (prim[q, i, span, :] for q in (1, 2, 3))
            enthalpy = enth[i, span, :]
            kinetic = (0.5 * gm) * (u1 * u1 + u2 * u2 + u3 * u3)
            projected = first[1] + second[2] + third[3]
            energy = u1 * first[4] + u2 * second[4] + u3 * third[4]
            dot = lambda g: u1 * g[1] + u2 * g[2] + u3 * g[3]
            dot1, dot2, dot3 = dot(first), dot(second), dot(third)
            mass_row = (
                kinetic * projected
                - (u1 * dot1 + u2 * dot2 + u3 * dot3)
                + (kinetic - enthalpy) * energy
            )
            shared = gm * (projected + energy)
            moved = lambda b: u1 * first[b] + u2 * second[b] + u3 * third[b]
            rows_out = (
                mass_row,
                moved(1) - u1 * shared + (first[0] + dot1 + enthalpy * first[4]),
                moved(2) - u2 * shared + (second[0] + dot2 + enthalpy * second[4]),
                moved(3) - u3 * shared + (third[0] + dot3 + enthalpy * third[4]),
                gm * projected + gamma_ratio * energy,
            )
            ramp = fraction * spread_lane(turned, rows * t)
            for q in range(5):
                done[q, i, span, :] = (
                    target[q, i, span, :] + rows_out[q] + damp[q] + ramp * flux[q, i, span, :]
                )
        out_copy(i).start()

    for c, copy in enumerate(loads):
        copy.wait()
        pl.loop(c * step_rows, (c + 1) * step_rows)(finish)

    @pl.loop(0, rows)
    def _(i):
        out_copy(i).wait()


def call(kernel, outs, operands, scratch, flops, name, spaces=None, far=()):
    spec = lambda n: pl.BlockSpec(memory_space=pltpu.HBM if n in far else VMEM)
    size = sum(4 * a.size for a in operands) + sum(4 * o.size for o in outs)
    operands = [
        pltpu.with_memory_space_constraint(a, pltpu.HBM) if n in far else a
        for n, a in enumerate(operands)
    ]
    return pl.pallas_call(
        kernel,
        out_shape=outs,
        in_specs=[spec(n) for n in range(len(operands))],
        out_specs=[pl.BlockSpec(memory_space=s) for s in (spaces or [VMEM] * len(outs))],
        scratch_shapes=scratch,
        cost_estimate=pl.CostEstimate(flops=flops, transcendentals=0, bytes_accessed=size),
        compiler_params=pltpu.CompilerParams(vmem_limit_bytes=16 << 20),
        name=name,
    )(*operands)


def local(
    primitive, adjoint_state, objective_grad, front_height,
    shock_state, state_by_height, state_by_slope, fitted_flags,
):
    _, rows, columns, depth = adjoint_state.shape
    tiles = columns // 8
    su_count, sv_count, lines = (lax.axis_size(a) for a in ("su", "sv", "nrm"))
    total_depth = depth * lines
    shape = lambda *s: jax.ShapeDtypeStruct(s, f32)
    field = shape(5, rows, columns, depth)
    plane = shape(rows, columns, depth)
    points = 5 * rows * columns * depth

    packet, su_a, su_b, sv_a, sv_b, normal, flux, enth, tone, inverse, prim, psi = call(
        functools.partial(prepare_kernel, rows, tiles, depth, total_depth, rows // 4),
        [
            shape(columns, 256),
            shape(6, 2, columns, depth),
            shape(6, 2, columns, depth),
            shape(6, 2 * rows, depth),
            shape(6, 2 * rows, depth),
            field, field, plane, plane,
            shape(columns, 128),
            field, field,
        ],
        (
            primitive, adjoint_state, front_height,
            shock_state, state_by_height, state_by_slope, fitted_flags,
        ),
        [
            VMEM((3, 128, 128), f32),
            VMEM((3, 128, 128), f32),
            VMEM((columns, 128), f32),
            VMEM((rows, columns, depth), f32),
            VMEM((rows, columns, depth), f32),
            VMEM((rows, columns), f32),
            VMEM((5, rows, columns), f32),
            VMEM((5, rows, columns), f32),
            VMEM((5, rows, columns), f32),
            VMEM((rows, columns), jnp.int32),
            pltpu.SemaphoreType.DMA((5,)),
            pltpu.SemaphoreType.DMA((2, 4)),
        ],
        12 * points,
        "prepare",
        far=range(7),
    )

    def pairs(count, shift):
        out = []
        for i in range(0, count, 2):
            a, b = (i + shift) % count, (i + shift + 1) % count
            out += [(a, b), (b, a)]
        return out

    arrived = lax.ppermute(packet, "nrm", [(0, 1), (1, 0)])
    su_a = lax.ppermute(su_a, "su", pairs(su_count, 0))
    su_b = lax.ppermute(su_b, "su", pairs(su_count, 1))
    sv_a = lax.ppermute(sv_a, "sv", pairs(sv_count, 0))
    sv_b = lax.ppermute(sv_b, "sv", pairs(sv_count, 1))

    chunk, mine = call(
        functools.partial(
            join_kernel, rows, tiles, depth, total_depth, rows * su_count, su_count
        ),
        [shape(su_count, 8, 128), shape(8, 128)],
        (packet, arrived, inverse, su_a, su_b, sv_a, sv_b),
        [],
        points // 40,
        "join",
    )
    chunks = lax.all_to_all(chunk, "su", 0, 0)
    result, slope = call(
        functools.partial(
            final_kernel, rows, tiles, depth, total_depth, su_count, sv_count
        ),
        [field, shape(rows, columns)],
        (
            prim, psi, objective_grad, normal, flux, enth, tone, inverse,
            arrived, mine, su_a, su_b, sv_a, sv_b, chunks,
        ),
        [
            VMEM((5, rows + 4, columns + 16, depth), f32),
            VMEM((5, rows + 4, columns, depth), f32),
            VMEM((5, rows, columns + 16, depth), f32),
            VMEM((128, 128), f32),
            VMEM((5, rows, columns, depth), f32),
            VMEM((5, rows, columns, depth), f32),
            pltpu.SemaphoreType.DMA((rows,)),
            pltpu.SemaphoreType.DMA((4,)),
        ],
        40 * points,
        "final",
        [pltpu.HBM, VMEM],
        far=(2,),
    )
    return result, slope


def solution(mesh):
    wide = P(None, "su", "sv", "nrm")
    flat = P("su", "sv")
    front = P(None, "su", "sv")
    return jax.shard_map(
        local,
        mesh=mesh,
        in_specs=(wide, wide, wide, flat, front, front, front, flat),
        out_specs=(wide, flat),
        check_vma=False,
    )
```

```python
import functools

import jax
import jax.numpy as jnp
from jax import lax
from jax.experimental import pallas as pl
from jax.experimental.pallas import tpu as pltpu
from jax.sharding import PartitionSpec as P

gamma_ratio = 1.4
damping_coef = 0.0625
stretch_rate = 2.2
gm = gamma_ratio - 1.0
f32 = jnp.float32
VMEM = pltpu.VMEM


def lanes(shape=(8, 128)):
    return lax.broadcasted_iota(jnp.int32, shape, 1)


def spread_lane(tile, lane):
    return jnp.broadcast_to(tile[:, lane : lane + 1], tile.shape)


def inv_stretch_at(index, total_depth):
    return 1.0 / jnp.exp(stretch_rate * ((index + 0.5) / total_depth - 1.0))


def even(axis):
    return lax.rem(lax.axis_index(axis), 2) == 0


def flux_of(rho, u1, u2, u3, p, enthalpy):
    mass = rho * u3
    return (mass, mass * u1, mass * u2, mass * u3 + p, mass * enthalpy)


def thermo(rho, u1, u2, u3, p):
    half = 0.5 * (u1 * u1 + u2 * u2 + u3 * u3)
    return gm * half, (gamma_ratio / gm) * (p / rho) + half


def part(array, q, rows):
    return pltpu.roll(array, 128 - rows * q, 1) if q else array


def prepare_kernel(
    rows, tiles, depth, total_depth, step_rows,
    prim_far, psi_far, height_far, shock_far, by_height_far, by_slope_far, flags_far,
    packet, su_a, su_b, sv_a, sv_b, normal, flux, enth, tone, inverse, prim, psi,
    turn, facts, tops, spread, work, height, shock, by_height, by_slope, flags, small, large,
):
    surfaces = [
        pltpu.make_async_copy(far, near, small.at[n])
        for n, (far, near) in enumerate(
            (
                (height_far, height),
                (shock_far, shock),
                (by_height_far, by_height),
                (by_slope_far, by_slope),
                (flags_far, flags),
            )
        )
    ]
    chunks = rows // step_rows
    loads = []
    for c in range(chunks):
        part_rows = pl.ds(c * step_rows, step_rows)
        loads.append(
            [
                pltpu.make_async_copy(far.at[:, part_rows], near.at[:, part_rows], large.at[n, c])
                for n, (far, near) in enumerate(((prim_far, prim), (psi_far, psi)))
            ]
        )
    for copy in surfaces:
        copy.start()
    for pair in loads:
        for copy in pair:
            copy.start()

    nrm = lax.axis_index("nrm")
    first = nrm == 0
    lane = lanes()
    lane_row = lanes((1, 128))
    columns = 8 * tiles
    spans = [slice(8 * t, 8 * t + 8) for t in range(tiles)]
    depth_index = (lane_row + nrm * depth).astype(f32)
    weight = 0.5 * inv_stretch_at(depth_index, total_depth)
    lower = jnp.broadcast_to(jnp.where(lane_row == depth - 1, 0.0, weight), (8, 128))
    upper = jnp.broadcast_to(jnp.where(lane_row == 0, 0.0, weight), (8, 128))
    top_scale = 0.5 * inv_stretch_at(
        jnp.full((1, 128), total_depth - 1, f32), total_depth
    )
    front = jnp.where(first, 0.0, 1.0)
    extra = jnp.where(first, 1, 0)

    turn[...] = jnp.zeros_like(turn)
    tops[...] = jnp.zeros_like(tops)
    packet[...] = jnp.zeros_like(packet)
    for copy in surfaces:
        copy.wait()
    for place, array in enumerate(
        [height[...]]
        + [shock[q] for q in range(5)]
        + [flags[...].astype(f32)]
    ):
        turn[0, rows * place : rows * place + rows, 0:columns] = array
    for q in range(5):
        turn[1, rows * q : rows * q + rows, 0:columns] = by_height[q]
        turn[2, rows * q : rows * q + rows, 0:columns] = by_slope[q]
    for n in range(3):
        facts[n] = turn[n].T
    for span in spans:
        inverse[span, :] = jnp.where(
            lane < rows, 1.0 / jnp.where(lane < rows, facts[0, span, :], 1.0), 0.0
        )
    for span in spans:
        inv_height = inverse[span, :]
        for i in range(rows):
            spread[i, span, :] = spread_lane(inv_height, i)

    for c in range(chunks):
        for copy in loads[c]:
            copy.wait()
        mine = range(c * step_rows, (c + 1) * step_rows)
        for i in mine:
            for span in spans:
                rho, u1, u2, u3, p = (prim[q, i, span, :] for q in range(5))
                ratio = p / rho
                enthalpy = (gamma_ratio / gm) * ratio + 0.5 * (u1 * u1 + u2 * u2 + u3 * u3)
                for q, value in enumerate(flux_of(rho, u1, u2, u3, p, enthalpy)):
                    flux[q, i, span, :] = value
                enth[i, span, :] = enthalpy
                tone[i, span, :] = jnp.sqrt(gamma_ratio * ratio)
        for i in mine:
            for span in spans:
                inv = spread[i, span, :]
                low, high = lower * inv, upper * inv
                total = None
                for q in range(5):
                    value = psi[q, i, span, :]
                    step = pltpu.roll(value * low, 1, 1) - pltpu.roll(value * high, 127, 1)
                    normal[q, i, span, :] = step
                    term = flux[q, i, span, :] * step
                    total = term if total is None else total + term
                work[i, span, :] = total
        for span in spans:
            for half, ref in ((0, psi), (1, flux)):
                packed = packet[span, 128 * half : 128 * half + 128]
                for q in range(5):
                    for i in mine:
                        spot = rows * q + i
                        moved = pltpu.roll(ref[q, i, span, :], spot + extra, 1)
                        packed = jnp.where(lane == spot, moved, packed)
                packet[span, 128 * half : 128 * half + 128] = packed

    @pl.when(jnp.logical_not(first))
    def _():
        for span in spans:
            packed = jnp.zeros((8, 128), f32)
            for q in range(5):
                for i in range(rows):
                    spot = rows * q + i
                    moved = pltpu.roll(psi[q, i, span, :], spot + 1, 1)
                    packed = jnp.where(lane == spot, moved, packed)
            tops[span, :] = packed

    for span in spans:
        gathered = jnp.zeros((8, 128), f32)
        for i in range(rows):
            total = jnp.sum(work[i, span, :], axis=1, keepdims=True)
            gathered = jnp.where(lane == i, jnp.broadcast_to(total, (8, 128)), gathered)
        turn[0, span, :] = gathered

    for span in spans:
        inv_height = inverse[span, :]
        gathered = turn[0, span, :]
        inside = lane < rows
        surf = facts[0, span, :]
        rho, u1, u2, u3, p = (
            jnp.where(inside, part(surf, q + 1, rows), 1.0) for q in range(5)
        )
        fitted = jnp.where(inside, part(surf, 6, rows), 0.0)
        scale = top_scale * inv_height
        last = tops[span, :]
        s0, s1, s2, s3, s4 = (part(last, q, rows) * scale for q in range(5))
        kinetic, enthalpy = thermo(rho, u1, u2, u3, p)
        fluxes = flux_of(rho, u1, u2, u3, p, enthalpy)
        top_work = (
            fluxes[0] * s0 + fluxes[1] * s1 + fluxes[2] * s2 + fluxes[3] * s3 + fluxes[4] * s4
        )
        dotted = u1 * s1 + u2 * s2 + u3 * s3
        shared = gm * (s3 + u3 * s4)
        common = s0 + dotted + enthalpy * s4
        adjoint = (
            kinetic * s3 - u3 * dotted + u3 * (kinetic - enthalpy) * s4,
            u3 * s1 - u1 * shared,
            u3 * s2 - u2 * shared,
            u3 * s3 - u3 * shared + common,
            gm * s3 + gamma_ratio * u3 * s4,
        )
        heights = facts[1, span, :]
        slopes = facts[2, span, :]
        by_h = sum(adjoint[q] * part(heights, q, rows) for q in range(5))
        by_s = sum(adjoint[q] * part(slopes, q, rows) for q in range(5))
        metric = -inv_height * (gathered + front * top_work)
        term = jnp.where(inside, metric + front * fitted * by_h, 0.0)
        tilt = jnp.where(inside, front * fitted * by_s, 0.0)
        packet[span, 0:128] = (
            packet[span, 0:128] + pltpu.roll(term, 5 * rows, 1) + pltpu.roll(tilt, 6 * rows, 1)
        )

    su_even, sv_even = even("su"), even("sv")
    high_row = rows - 2
    row_a = jnp.where(su_even, high_row, 0)
    row_b = high_row - row_a
    for r in range(2):
        for ref, row in ((su_a, row_a + r), (su_b, row_b + r)):
            for q in range(5):
                ref[q, r] = psi[q, row]
            ref[5, r] = jnp.abs(prim[1, row]) + tone[row]
    for i in range(rows):
        pair = slice(2 * i, 2 * i + 2)
        for q in range(6):
            if q < 5:
                low, high = psi[q, i, 0:2, :], psi[q, i, columns - 2 : columns, :]
            else:
                low = jnp.abs(prim[2, i, 0:2, :]) + tone[i, 0:2, :]
                high = (
                    jnp.abs(prim[2, i, columns - 2 : columns, :])
                    + tone[i, columns - 2 : columns, :]
                )
            sv_a[q, pair, :] = jnp.where(sv_even, high, low)
            sv_b[q, pair, :] = jnp.where(sv_even, low, high)


def join_kernel(
    rows, tiles, depth, total_depth, surface, fan, own, arrived, inverse, chunk, mine
):
    first = lax.axis_index("nrm") == 0
    lane = lanes()
    one = jnp.zeros((1, 128), f32)
    before = 0.5 * inv_stretch_at(one + (depth - 1), total_depth)
    after = 0.5 * inv_stretch_at(one + depth, total_depth)
    own_scale = jnp.where(first, before, after)
    far_scale = jnp.where(first, after, before)
    sign = jnp.where(first, 1.0, -1.0)
    sums = jnp.zeros((8, 128), f32)
    kept = jnp.zeros((8, 128), f32)
    for t in range(tiles):
        span = slice(8 * t, 8 * t + 8)
        near, near_flux = own[span, 0:128], own[span, 128:256]
        far, far_flux = arrived[span, 0:128], arrived[span, 128:256]
        cross = near_flux * (far * far_scale) - far_flux * (near * own_scale)
        cross = jnp.where(lane < 5 * rows, cross, 0.0)
        for d in (1, 2, 4):
            cross = cross + pltpu.roll(cross, rows * d, 1)
        inv_height = inverse[span, :]
        total = near + far
        inside = lane < rows
        term = jnp.where(
            inside, part(total, 5, rows) + sign * inv_height * inv_height * cross, 0.0
        )
        for d in (1, 2, 4, 8):
            term = term + pltpu.roll(term, 128 - d, 1)
        share = term * (1.0 / surface)
        slope = jnp.where(inside, share + part(total, 6, rows), 0.0)
        kept = kept + (pltpu.roll(slope, rows * t, 1) if t else slope)
        sums = jnp.where(lane == t, pltpu.roll(share, t, 1) if t else share, sums)
    mine[...] = kept
    for n in range(fan):
        chunk[n] = sums


def final_kernel(
    rows, tiles, depth, total_depth, su_count, sv_count,
    prim, psi, target_far, normal, flux, enth, tone, inverse, arrived, mine,
    su_a, su_b, sv_a, sv_b, chunks,
    result, slope,
    wide, along, across, turn, done, target, sems, large,
):
    step_rows = 4
    loads = [
        pltpu.make_async_copy(
            target_far.at[:, pl.ds(r, step_rows)], target.at[:, pl.ds(r, step_rows)],
            large.at[r // step_rows],
        )
        for r in range(0, rows, step_rows)
    ]
    for copy in loads:
        copy.start()
    su, sv, nrm = lax.axis_index("su"), lax.axis_index("sv"), lax.axis_index("nrm")
    first = nrm == 0
    lane = lanes()
    columns = 8 * tiles
    ahead = jnp.zeros((8, 128), f32)
    for n in range(su_count):
        ahead = ahead + jnp.where(n > su, chunks[n], 0.0)
    upstream = jnp.zeros((8, 128), f32)
    for t in range(tiles):
        upstream = jnp.where(
            (lane >= rows * t) & (lane < rows * t + rows), spread_lane(ahead, t), upstream
        )
    packed = mine[...] + upstream
    turn[...] = jnp.zeros_like(turn)
    for t in range(tiles):
        turn[8 * t : 8 * t + 8, :] = pltpu.roll(packed, 128 - rows * t, 1) if t else packed
    slope[...] = turn[...].T[0:rows, 0:columns]

    su_even, sv_even = even("su"), even("sv")
    low_on, high_on = su > 0, su < su_count - 1
    for r in range(2):
        for swap, on, row in ((su_even, low_on, r), (~su_even, high_on, rows + 2 + r)):
            pick = lambda q: jnp.where(swap, su_b[q, r], su_a[q, r])
            radius = pick(5)
            for q in range(5):
                value = jnp.where(on, pick(q), 0.0)
                wide[q, row, 8 : 8 + columns, :] = value
                along[q, row] = value * radius
    left_on, right_on = sv > 0, sv < sv_count - 1
    for swap, on, col in ((sv_even, left_on, 6), (~sv_even, right_on, 8 + columns)):
        radius = jnp.where(swap, sv_b[5], sv_a[5])
        for q in range(5):
            value = jnp.where(on, jnp.where(swap, sv_b[q], sv_a[q]), 0.0)
            weighted = value * radius
            for i in range(rows):
                wide[q, i + 2, col : col + 2, :] = value[2 * i : 2 * i + 2]
                across[q, i, col : col + 2, :] = weighted[2 * i : 2 * i + 2]

    @pl.loop(0, rows, unroll=4)
    def _(i):
        for t in range(tiles):
            span = slice(8 * t, 8 * t + 8)
            inner = slice(8 * t + 8, 8 * t + 16)
            sound = tone[i, span, :]
            radius_u = jnp.abs(prim[1, i, span, :]) + sound
            radius_v = jnp.abs(prim[2, i, span, :]) + sound
            for q in range(5):
                value = psi[q, i, span, :]
                wide[q, i + 2, inner, :] = value
                along[q, i + 2, span, :] = radius_u * value
                across[q, i, inner, :] = radius_v * value

    fraction = jnp.broadcast_to(
        ((lanes((1, 128)) + nrm * depth).astype(f32) + 0.5) / total_depth, (8, 128)
    )
    one = jnp.zeros((1, 128), f32)
    edge_scale = jnp.where(
        first,
        -0.5 * inv_stretch_at(one + depth, total_depth),
        0.5 * inv_stretch_at(one + (depth - 1), total_depth),
    )
    entry = jnp.where(first, depth - 1, 0)
    at_entry = lane == entry
    for t in range(tiles):
        span = slice(8 * t, 8 * t + 8)
        repeated = inverse[span, :]
        for d in (1, 2, 4):
            repeated = repeated + pltpu.roll(repeated, rows * d, 1)
        turn[span, :] = arrived[span, 0:128] * edge_scale * repeated

    def out_copy(i):
        return pltpu.make_async_copy(done.at[:, i], result.at[:, i], sems.at[i])

    def finish(i):
        turned = pltpu.roll(packed, 128 - i, 1)
        for t in range(tiles):
            span = slice(8 * t, 8 * t + 8)
            at = lambda k: slice(8 * t + 8 + k, 8 * t + 16 + k)
            ends = turn[span, :]
            first, second, third, damp = [], [], [], []
            for q in range(5):
                first.append(
                    (8.0 / 12.0) * (wide[q, i + 1, at(0), :] - wide[q, i + 3, at(0), :])
                    - (1.0 / 12.0) * (wide[q, i, at(0), :] - wide[q, i + 4, at(0), :])
                )
                second.append(
                    (8.0 / 12.0) * (wide[q, i + 2, at(-1), :] - wide[q, i + 2, at(1), :])
                    - (1.0 / 12.0) * (wide[q, i + 2, at(-2), :] - wide[q, i + 2, at(2), :])
                )
                far = (
                    along[q, i, span, :] + along[q, i + 4, span, :]
                    + across[q, i, at(-2), :] + across[q, i, at(2), :]
                )
                near = (
                    along[q, i + 1, span, :] + along[q, i + 3, span, :]
                    + across[q, i, at(-1), :] + across[q, i, at(1), :]
                )
                here = along[q, i + 2, span, :] + across[q, i, at(0), :]
                damp.append(
                    damping_coef * far - (4.0 * damping_coef) * near + (6.0 * damping_coef) * here
                )
                came = pltpu.roll(ends, entry + (128 - rows * q) - i, 1)
                third.append(normal[q, i, span, :] + jnp.where(at_entry, came, 0.0))
            u1, u2, u3 = (prim[q, i, span, :] for q in (1, 2, 3))
            enthalpy = enth[i, span, :]
            kinetic = (0.5 * gm) * (u1 * u1 + u2 * u2 + u3 * u3)
            projected = first[1] + second[2] + third[3]
            energy = u1 * first[4] + u2 * second[4] + u3 * third[4]
            dot = lambda g: u1 * g[1] + u2 * g[2] + u3 * g[3]
            dot1, dot2, dot3 = dot(first), dot(second), dot(third)
            mass_row = (
                kinetic * projected
                - (u1 * dot1 + u2 * dot2 + u3 * dot3)
                + (kinetic - enthalpy) * energy
            )
            shared = gm * (projected + energy)
            moved = lambda b: u1 * first[b] + u2 * second[b] + u3 * third[b]
            rows_out = (
                mass_row,
                moved(1) - u1 * shared + (first[0] + dot1 + enthalpy * first[4]),
                moved(2) - u2 * shared + (second[0] + dot2 + enthalpy * second[4]),
                moved(3) - u3 * shared + (third[0] + dot3 + enthalpy * third[4]),
                gm * projected + gamma_ratio * energy,
            )
            ramp = fraction * spread_lane(turned, rows * t)
            for q in range(5):
                done[q, i, span, :] = (
                    target[q, i, span, :] + rows_out[q] + damp[q] + ramp * flux[q, i, span, :]
                )
        out_copy(i).start()

    for c, copy in enumerate(loads):
        copy.wait()
        pl.loop(c * step_rows, (c + 1) * step_rows, unroll=step_rows)(finish)

    @pl.loop(0, rows)
    def _(i):
        out_copy(i).wait()


def call(kernel, outs, operands, scratch, flops, name, spaces=None, far=()):
    spec = lambda n: pl.BlockSpec(memory_space=pltpu.HBM if n in far else VMEM)
    size = sum(4 * a.size for a in operands) + sum(4 * o.size for o in outs)
    operands = [
        pltpu.with_memory_space_constraint(a, pltpu.HBM) if n in far else a
        for n, a in enumerate(operands)
    ]
    return pl.pallas_call(
        kernel,
        out_shape=outs,
        in_specs=[spec(n) for n in range(len(operands))],
        out_specs=[pl.BlockSpec(memory_space=s) for s in (spaces or [VMEM] * len(outs))],
        scratch_shapes=scratch,
        cost_estimate=pl.CostEstimate(flops=flops, transcendentals=0, bytes_accessed=size),
        compiler_params=pltpu.CompilerParams(vmem_limit_bytes=16 << 20),
        name=name,
    )(*operands)


def local(
    primitive, adjoint_state, objective_grad, front_height,
    shock_state, state_by_height, state_by_slope, fitted_flags,
):
    _, rows, columns, depth = adjoint_state.shape
    tiles = columns // 8
    su_count, sv_count, lines = (lax.axis_size(a) for a in ("su", "sv", "nrm"))
    total_depth = depth * lines
    shape = lambda *s: jax.ShapeDtypeStruct(s, f32)
    field = shape(5, rows, columns, depth)
    plane = shape(rows, columns, depth)
    points = 5 * rows * columns * depth

    packet, su_a, su_b, sv_a, sv_b, normal, flux, enth, tone, inverse, prim, psi = call(
        functools.partial(prepare_kernel, rows, tiles, depth, total_depth, rows // 4),
        [
            shape(columns, 256),
            shape(6, 2, columns, depth),
            shape(6, 2, columns, depth),
            shape(6, 2 * rows, depth),
            shape(6, 2 * rows, depth),
            field, field, plane, plane,
            shape(columns, 128),
            field, field,
        ],
        (
            primitive, adjoint_state, front_height,
            shock_state, state_by_height, state_by_slope, fitted_flags,
        ),
        [
            VMEM((3, 128, 128), f32),
            VMEM((3, 128, 128), f32),
            VMEM((columns, 128), f32),
            VMEM((rows, columns, depth), f32),
            VMEM((rows, columns, depth), f32),
            VMEM((rows, columns), f32),
            VMEM((5, rows, columns), f32),
            VMEM((5, rows, columns), f32),
            VMEM((5, rows, columns), f32),
            VMEM((rows, columns), jnp.int32),
            pltpu.SemaphoreType.DMA((5,)),
            pltpu.SemaphoreType.DMA((2, 4)),
        ],
        12 * points,
        "prepare",
        far=range(7),
    )

    def pairs(count, shift):
        out = []
        for i in range(0, count, 2):
            a, b = (i + shift) % count, (i + shift + 1) % count
            out += [(a, b), (b, a)]
        return out

    arrived = lax.ppermute(packet, "nrm", [(0, 1), (1, 0)])
    su_a = lax.ppermute(su_a, "su", pairs(su_count, 0))
    su_b = lax.ppermute(su_b, "su", pairs(su_count, 1))
    sv_a = lax.ppermute(sv_a, "sv", pairs(sv_count, 0))
    sv_b = lax.ppermute(sv_b, "sv", pairs(sv_count, 1))

    chunk, mine = call(
        functools.partial(
            join_kernel, rows, tiles, depth, total_depth, rows * su_count, su_count
        ),
        [shape(su_count, 8, 128), shape(8, 128)],
        (packet, arrived, inverse),
        [],
        100_000 * points,
        "join",
    )
    chunk, su_a, su_b, sv_a, sv_b = lax.optimization_barrier((chunk, su_a, su_b, sv_a, sv_b))
    chunks = lax.all_to_all(chunk, "su", 0, 0)
    result, slope = call(
        functools.partial(
            final_kernel, rows, tiles, depth, total_depth, su_count, sv_count
        ),
        [field, shape(rows, columns)],
        (
            prim, psi, objective_grad, normal, flux, enth, tone, inverse,
            arrived, mine, su_a, su_b, sv_a, sv_b, chunks,
        ),
        [
            VMEM((5, rows + 4, columns + 16, depth), f32),
            VMEM((5, rows + 4, columns, depth), f32),
            VMEM((5, rows, columns + 16, depth), f32),
            VMEM((128, 128), f32),
            VMEM((5, rows, columns, depth), f32),
            VMEM((5, rows, columns, depth), f32),
            pltpu.SemaphoreType.DMA((rows,)),
            pltpu.SemaphoreType.DMA((4,)),
        ],
        40 * points,
        "final",
        [pltpu.HBM, VMEM],
        far=(2,),
    )
    return result, slope


def solution(mesh):
    wide = P(None, "su", "sv", "nrm")
    flat = P("su", "sv")
    front = P(None, "su", "sv")
    return jax.shard_map(
        local,
        mesh=mesh,
        in_specs=(wide, wide, wide, flat, front, front, front, flat),
        out_specs=(wide, flat),
        check_vma=False,
    )
```

```python
import functools

import jax
import jax.numpy as jnp
from jax import lax
from jax.experimental import pallas as pl
from jax.experimental.pallas import tpu as pltpu
from jax.sharding import PartitionSpec as P

gamma_ratio = 1.4
damping_coef = 0.0625
stretch_rate = 2.2
gm = gamma_ratio - 1.0
f32 = jnp.float32
VMEM = pltpu.VMEM
JOIN_COST = 5_000
INTERIOR_COST = 5_000


def lanes(shape=(8, 128)):
    return lax.broadcasted_iota(jnp.int32, shape, 1)


def spread_lane(tile, lane):
    return jnp.broadcast_to(tile[:, lane : lane + 1], tile.shape)


def inv_stretch_at(index, total_depth):
    return 1.0 / jnp.exp(stretch_rate * ((index + 0.5) / total_depth - 1.0))


def even(axis):
    return lax.rem(lax.axis_index(axis), 2) == 0


def flux_of(rho, u1, u2, u3, p, enthalpy):
    mass = rho * u3
    return (mass, mass * u1, mass * u2, mass * u3 + p, mass * enthalpy)


def thermo(rho, u1, u2, u3, p):
    half = 0.5 * (u1 * u1 + u2 * u2 + u3 * u3)
    return gm * half, (gamma_ratio / gm) * (p / rho) + half


def part(array, q, rows):
    return pltpu.roll(array, 128 - rows * q, 1) if q else array


def prepare_kernel(
    rows, tiles, depth, total_depth, step_rows,
    prim_far, psi_far, height_far, shock_far, by_height_far, by_slope_far, flags_far,
    packet, su_a, su_b, sv_a, sv_b, normal, flux, enth, tone, inverse, prim, psi,
    turn, facts, tops, spread, work, height, shock, by_height, by_slope, flags, small, large,
):
    surfaces = [
        pltpu.make_async_copy(far, near, small.at[n])
        for n, (far, near) in enumerate(
            (
                (height_far, height),
                (shock_far, shock),
                (by_height_far, by_height),
                (by_slope_far, by_slope),
                (flags_far, flags),
            )
        )
    ]
    chunks = rows // step_rows
    loads = []
    for c in range(chunks):
        part_rows = pl.ds(c * step_rows, step_rows)
        loads.append(
            [
                pltpu.make_async_copy(far.at[:, part_rows], near.at[:, part_rows], large.at[n, c])
                for n, (far, near) in enumerate(((prim_far, prim), (psi_far, psi)))
            ]
        )
    for copy in surfaces:
        copy.start()
    for pair in loads:
        for copy in pair:
            copy.start()

    nrm = lax.axis_index("nrm")
    first = nrm == 0
    lane = lanes()
    lane_row = lanes((1, 128))
    columns = 8 * tiles
    spans = [slice(8 * t, 8 * t + 8) for t in range(tiles)]
    depth_index = (lane_row + nrm * depth).astype(f32)
    weight = 0.5 * inv_stretch_at(depth_index, total_depth)
    lower = jnp.broadcast_to(jnp.where(lane_row == depth - 1, 0.0, weight), (8, 128))
    upper = jnp.broadcast_to(jnp.where(lane_row == 0, 0.0, weight), (8, 128))
    top_scale = 0.5 * inv_stretch_at(
        jnp.full((1, 128), total_depth - 1, f32), total_depth
    )
    front = jnp.where(first, 0.0, 1.0)
    extra = jnp.where(first, 1, 0)

    turn[...] = jnp.zeros_like(turn)
    tops[...] = jnp.zeros_like(tops)
    packet[...] = jnp.zeros_like(packet)
    for copy in surfaces:
        copy.wait()
    for place, array in enumerate(
        [height[...]]
        + [shock[q] for q in range(5)]
        + [flags[...].astype(f32)]
    ):
        turn[0, rows * place : rows * place + rows, 0:columns] = array
    for q in range(5):
        turn[1, rows * q : rows * q + rows, 0:columns] = by_height[q]
        turn[2, rows * q : rows * q + rows, 0:columns] = by_slope[q]
    for n in range(3):
        facts[n] = turn[n].T
    for span in spans:
        inverse[span, :] = jnp.where(
            lane < rows, 1.0 / jnp.where(lane < rows, facts[0, span, :], 1.0), 0.0
        )
    for span in spans:
        inv_height = inverse[span, :]
        for i in range(rows):
            spread[i, span, :] = spread_lane(inv_height, i)

    for c in range(chunks):
        for copy in loads[c]:
            copy.wait()
        mine = range(c * step_rows, (c + 1) * step_rows)
        for i in mine:
            for span in spans:
                rho, u1, u2, u3, p = (prim[q, i, span, :] for q in range(5))
                ratio = p / rho
                enthalpy = (gamma_ratio / gm) * ratio + 0.5 * (u1 * u1 + u2 * u2 + u3 * u3)
                for q, value in enumerate(flux_of(rho, u1, u2, u3, p, enthalpy)):
                    flux[q, i, span, :] = value
                enth[i, span, :] = enthalpy
                tone[i, span, :] = jnp.sqrt(gamma_ratio * ratio)
        for i in mine:
            for span in spans:
                inv = spread[i, span, :]
                low, high = lower * inv, upper * inv
                total = None
                for q in range(5):
                    value = psi[q, i, span, :]
                    step = pltpu.roll(value * low, 1, 1) - pltpu.roll(value * high, 127, 1)
                    normal[q, i, span, :] = step
                    term = flux[q, i, span, :] * step
                    total = term if total is None else total + term
                work[i, span, :] = total
        for span in spans:
            for half, ref in ((0, psi), (1, flux)):
                packed = packet[span, 128 * half : 128 * half + 128]
                for q in range(5):
                    for i in mine:
                        spot = rows * q + i
                        moved = pltpu.roll(ref[q, i, span, :], spot + extra, 1)
                        packed = jnp.where(lane == spot, moved, packed)
                packet[span, 128 * half : 128 * half + 128] = packed

    @pl.when(jnp.logical_not(first))
    def _():
        for span in spans:
            packed = jnp.zeros((8, 128), f32)
            for q in range(5):
                for i in range(rows):
                    spot = rows * q + i
                    moved = pltpu.roll(psi[q, i, span, :], spot + 1, 1)
                    packed = jnp.where(lane == spot, moved, packed)
            tops[span, :] = packed

    for span in spans:
        gathered = jnp.zeros((8, 128), f32)
        for i in range(rows):
            total = jnp.sum(work[i, span, :], axis=1, keepdims=True)
            gathered = jnp.where(lane == i, jnp.broadcast_to(total, (8, 128)), gathered)
        turn[0, span, :] = gathered

    for span in spans:
        inv_height = inverse[span, :]
        gathered = turn[0, span, :]
        inside = lane < rows
        surf = facts[0, span, :]
        rho, u1, u2, u3, p = (
            jnp.where(inside, part(surf, q + 1, rows), 1.0) for q in range(5)
        )
        fitted = jnp.where(inside, part(surf, 6, rows), 0.0)
        scale = top_scale * inv_height
        last = tops[span, :]
        s0, s1, s2, s3, s4 = (part(last, q, rows) * scale for q in range(5))
        kinetic, enthalpy = thermo(rho, u1, u2, u3, p)
        fluxes = flux_of(rho, u1, u2, u3, p, enthalpy)
        top_work = (
            fluxes[0] * s0 + fluxes[1] * s1 + fluxes[2] * s2 + fluxes[3] * s3 + fluxes[4] * s4
        )
        dotted = u1 * s1 + u2 * s2 + u3 * s3
        shared = gm * (s3 + u3 * s4)
        common = s0 + dotted + enthalpy * s4
        adjoint = (
            kinetic * s3 - u3 * dotted + u3 * (kinetic - enthalpy) * s4,
            u3 * s1 - u1 * shared,
            u3 * s2 - u2 * shared,
            u3 * s3 - u3 * shared + common,
            gm * s3 + gamma_ratio * u3 * s4,
        )
        heights = facts[1, span, :]
        slopes = facts[2, span, :]
        by_h = sum(adjoint[q] * part(heights, q, rows) for q in range(5))
        by_s = sum(adjoint[q] * part(slopes, q, rows) for q in range(5))
        metric = -inv_height * (gathered + front * top_work)
        term = jnp.where(inside, metric + front * fitted * by_h, 0.0)
        tilt = jnp.where(inside, front * fitted * by_s, 0.0)
        packet[span, 0:128] = (
            packet[span, 0:128] + pltpu.roll(term, 5 * rows, 1) + pltpu.roll(tilt, 6 * rows, 1)
        )

    su_even, sv_even = even("su"), even("sv")
    high_row = rows - 2
    row_a = jnp.where(su_even, high_row, 0)
    row_b = high_row - row_a
    for r in range(2):
        for ref, row in ((su_a, row_a + r), (su_b, row_b + r)):
            for q in range(5):
                ref[q, r] = psi[q, row]
            ref[5, r] = jnp.abs(prim[1, row]) + tone[row]
    for i in range(rows):
        pair = slice(2 * i, 2 * i + 2)
        for q in range(6):
            if q < 5:
                low, high = psi[q, i, 0:2, :], psi[q, i, columns - 2 : columns, :]
            else:
                low = jnp.abs(prim[2, i, 0:2, :]) + tone[i, 0:2, :]
                high = (
                    jnp.abs(prim[2, i, columns - 2 : columns, :])
                    + tone[i, columns - 2 : columns, :]
                )
            sv_a[q, pair, :] = jnp.where(sv_even, high, low)
            sv_b[q, pair, :] = jnp.where(sv_even, low, high)


def join_kernel(
    rows, tiles, depth, total_depth, surface, fan, own, arrived, inverse, chunk, mine
):
    first = lax.axis_index("nrm") == 0
    lane = lanes()
    one = jnp.zeros((1, 128), f32)
    before = 0.5 * inv_stretch_at(one + (depth - 1), total_depth)
    after = 0.5 * inv_stretch_at(one + depth, total_depth)
    own_scale = jnp.where(first, before, after)
    far_scale = jnp.where(first, after, before)
    sign = jnp.where(first, 1.0, -1.0)
    sums = jnp.zeros((8, 128), f32)
    kept = jnp.zeros((8, 128), f32)
    for t in range(tiles):
        span = slice(8 * t, 8 * t + 8)
        near, near_flux = own[span, 0:128], own[span, 128:256]
        far, far_flux = arrived[span, 0:128], arrived[span, 128:256]
        cross = near_flux * (far * far_scale) - far_flux * (near * own_scale)
        cross = jnp.where(lane < 5 * rows, cross, 0.0)
        for d in (1, 2, 4):
            cross = cross + pltpu.roll(cross, rows * d, 1)
        inv_height = inverse[span, :]
        total = near + far
        inside = lane < rows
        term = jnp.where(
            inside, part(total, 5, rows) + sign * inv_height * inv_height * cross, 0.0
        )
        for d in (1, 2, 4, 8):
            term = term + pltpu.roll(term, 128 - d, 1)
        share = term * (1.0 / surface)
        slope = jnp.where(inside, share + part(total, 6, rows), 0.0)
        kept = kept + (pltpu.roll(slope, rows * t, 1) if t else slope)
        sums = jnp.where(lane == t, pltpu.roll(share, t, 1) if t else share, sums)
    mine[...] = kept
    for n in range(fan):
        chunk[n] = sums


def transposed(speeds, kinetic, enthalpy, first, second, third):
    given = [(d, g) for d, g in ((0, first), (1, second), (2, third)) if g is not None]
    add = lambda parts: functools.reduce(lambda x, y: x + y, parts)
    projected = add([g[d + 1] for d, g in given])
    energy = add([speeds[d] * g[4] for d, g in given])
    dots = {
        d: speeds[0] * g[1] + speeds[1] * g[2] + speeds[2] * g[3] for d, g in given
    }
    shared = gm * (projected + energy)
    out = [
        kinetic * projected
        - add([speeds[d] * dots[d] for d, _ in given])
        + (kinetic - enthalpy) * energy
    ]
    for c in range(3):
        value = add([speeds[d] * g[c + 1] for d, g in given]) - speeds[c] * shared
        for d, g in given:
            if d == c:
                value = value + (g[0] + dots[d] + enthalpy * g[4])
        out.append(value)
    out.append(gm * projected + gamma_ratio * energy)
    return out


near_weight, far_weight = 8.0 / 12.0, 1.0 / 12.0


def interior_kernel(
    rows, tiles, prim, psi, target_far, normal, enth, tone,
    base,
    wide, along, across, target, large,
):
    step_rows = 4
    columns = 8 * tiles
    loads = [
        pltpu.make_async_copy(
            target_far.at[:, pl.ds(r, step_rows)], target.at[:, pl.ds(r, step_rows)],
            large.at[r // step_rows],
        )
        for r in range(0, rows, step_rows)
    ]
    for copy in loads:
        copy.start()
    for q in range(5):
        for row in (0, 1, rows + 2, rows + 3):
            wide[q, row] = jnp.zeros_like(wide[q, row])
            along[q, row] = jnp.zeros_like(along[q, row])
        for i in range(rows):
            for low in (0, 8 + columns):
                wide[q, i + 2, low : low + 8, :] = jnp.zeros((8, 128), f32)
                across[q, i, low : low + 8, :] = jnp.zeros((8, 128), f32)

    @pl.loop(0, rows, unroll=4)
    def _(i):
        for t in range(tiles):
            span = slice(8 * t, 8 * t + 8)
            inner = slice(8 * t + 8, 8 * t + 16)
            sound = tone[i, span, :]
            radius_u = jnp.abs(prim[1, i, span, :]) + sound
            radius_v = jnp.abs(prim[2, i, span, :]) + sound
            for q in range(5):
                value = psi[q, i, span, :]
                wide[q, i + 2, inner, :] = value
                along[q, i + 2, span, :] = radius_u * value
                across[q, i, inner, :] = radius_v * value

    def fill(i):
        for t in range(tiles):
            span = slice(8 * t, 8 * t + 8)
            at = lambda k: slice(8 * t + 8 + k, 8 * t + 16 + k)
            first, second, third, damp = [], [], [], []
            for q in range(5):
                first.append(
                    near_weight * (wide[q, i + 1, at(0), :] - wide[q, i + 3, at(0), :])
                    - far_weight * (wide[q, i, at(0), :] - wide[q, i + 4, at(0), :])
                )
                second.append(
                    near_weight * (wide[q, i + 2, at(-1), :] - wide[q, i + 2, at(1), :])
                    - far_weight * (wide[q, i + 2, at(-2), :] - wide[q, i + 2, at(2), :])
                )
                far = (
                    along[q, i, span, :] + along[q, i + 4, span, :]
                    + across[q, i, at(-2), :] + across[q, i, at(2), :]
                )
                near = (
                    along[q, i + 1, span, :] + along[q, i + 3, span, :]
                    + across[q, i, at(-1), :] + across[q, i, at(1), :]
                )
                here = along[q, i + 2, span, :] + across[q, i, at(0), :]
                damp.append(
                    damping_coef * far - (4.0 * damping_coef) * near + (6.0 * damping_coef) * here
                )
                third.append(normal[q, i, span, :])
            speeds = tuple(prim[q, i, span, :] for q in (1, 2, 3))
            u1, u2, u3 = speeds
            kinetic = (0.5 * gm) * (u1 * u1 + u2 * u2 + u3 * u3)
            terms = transposed(speeds, kinetic, enth[i, span, :], first, second, third)
            for q in range(5):
                base[q, i, span, :] = target[q, i, span, :] + terms[q] + damp[q]

    for c, copy in enumerate(loads):
        copy.wait()
        pl.loop(c * step_rows, (c + 1) * step_rows, unroll=step_rows)(fill)


def final_kernel(
    rows, tiles, depth, total_depth, su_count, sv_count,
    prim, base, flux, enth, inverse, arrived, mine,
    su_a, su_b, sv_a, sv_b, chunks,
    result, slope,
    left, right, turn, done, sems,
):
    su, sv, nrm = lax.axis_index("su"), lax.axis_index("sv"), lax.axis_index("nrm")
    before = nrm == 0
    lane = lanes()
    line = lax.broadcasted_iota(jnp.int32, (8, 128), 0)
    columns = 8 * tiles
    ahead = jnp.zeros((8, 128), f32)
    for n in range(su_count):
        ahead = ahead + jnp.where(n > su, chunks[n], 0.0)
    upstream = jnp.zeros((8, 128), f32)
    for t in range(tiles):
        upstream = jnp.where(
            (lane >= rows * t) & (lane < rows * t + rows), spread_lane(ahead, t), upstream
        )
    packed = mine[...] + upstream
    turn[...] = jnp.zeros_like(turn)
    for t in range(tiles):
        turn[8 * t : 8 * t + 8, :] = pltpu.roll(packed, 128 - rows * t, 1) if t else packed
    slope[...] = turn[...].T[0:rows, 0:columns]

    one = jnp.zeros((1, 128), f32)
    edge_scale = jnp.where(
        before,
        -0.5 * inv_stretch_at(one + depth, total_depth),
        0.5 * inv_stretch_at(one + (depth - 1), total_depth),
    )
    entry = jnp.where(before, depth - 1, 0)
    at_entry = lane == entry
    for t in range(tiles):
        span = slice(8 * t, 8 * t + 8)
        repeated = inverse[span, :]
        for d in (1, 2, 4):
            repeated = repeated + pltpu.roll(repeated, rows * d, 1)
        turn[span, :] = arrived[span, 0:128] * edge_scale * repeated

    su_even, sv_even = even("su"), even("sv")
    for piece in range(2 * rows // 8):
        at = slice(8 * piece, 8 * piece + 8)
        outer = lax.rem(line, 2) == 0
        for swap, on, ref, offset, sign in (
            (sv_even, sv > 0, left, 0, 1.0),
            (~sv_even, sv < sv_count - 1, right, 8, -1.0),
        ):
            into = slice(8 * piece + offset, 8 * piece + offset + 8)
            pick = lambda q: jnp.where(swap, sv_b[q, at, :], sv_a[q, at, :])
            radius = pick(5)
            for q in range(5):
                value = jnp.where(on, pick(q), 0.0)
                weighted = value * radius
                grads, damps = [], []
                for array, close, away, kept in (
                    (value, sign * near_weight, -sign * far_weight, grads),
                    (weighted, -4.0 * damping_coef, damping_coef, damps),
                ):
                    if offset == 0:
                        even_part = close * pltpu.roll(array, 7, 0) + away * array
                        odd_part = away * array
                    else:
                        even_part = away * array
                        odd_part = close * pltpu.roll(array, 1, 0) + away * array
                    kept.append(jnp.where(outer, even_part, odd_part))
                ref[q, into, :] = grads[0]
                ref[5 + q, into, :] = damps[0]

    def out_copy(i):
        return pltpu.make_async_copy(done.at[:, i], result.at[:, i], sems.at[i])

    fraction = jnp.broadcast_to(
        ((lanes((1, 128)) + nrm * depth).astype(f32) + 0.5) / total_depth, (8, 128)
    )

    def finish(i, beside):
        turned = pltpu.roll(packed, 128 - i, 1)
        for t in range(tiles):
            span = slice(8 * t, 8 * t + 8)
            ends = turn[span, :]
            third = [
                jnp.where(at_entry, pltpu.roll(ends, entry + (128 - rows * q) - i, 1), 0.0)
                for q in range(5)
            ]
            first = second = None
            damp = [None] * 5
            if beside is not None:
                first, damp = beside(span)
            if t in (0, tiles - 1):
                ref, start = (left, 2 * i) if t == 0 else (right, 2 * i + 2)
                here = line < 2 if t == 0 else line >= 6
                load = lambda q: jnp.where(here, ref[q, pl.ds(start, 8), :], 0.0)
                second = [load(q) for q in range(5)]
                damp = [
                    load(5 + q) if damp[q] is None else damp[q] + load(5 + q) for q in range(5)
                ]
            speeds = tuple(prim[q, i, span, :] for q in (1, 2, 3))
            u1, u2, u3 = speeds
            kinetic = (0.5 * gm) * (u1 * u1 + u2 * u2 + u3 * u3)
            terms = transposed(speeds, kinetic, enth[i, span, :], first, second, third)
            ramp = fraction * spread_lane(turned, rows * t)
            for q in range(5):
                value = base[q, i, span, :] + terms[q] + ramp * flux[q, i, span, :]
                done[q, i, span, :] = value if damp[q] is None else value + damp[q]
        out_copy(i).start()

    def edge_row(low, inner):
        swap, on, sign = (
            (su_even, su > 0, 1.0) if low else (~su_even, su < su_count - 1, -1.0)
        )

        def beside(span):
            pick = lambda q, r: jnp.where(swap, su_b[q, r, span, :], su_a[q, r, span, :])
            close, away = (1, 0) if low else (0, 1)
            grads, damps = [], []
            for q in range(5):
                value = jnp.where(on, pick(q, close), 0.0)
                weighted = value * pick(5, close)
                if inner:
                    grads.append((-sign * far_weight) * value)
                    damps.append(damping_coef * weighted)
                else:
                    other = jnp.where(on, pick(q, away), 0.0)
                    grads.append((sign * near_weight) * value - (sign * far_weight) * other)
                    damps.append(
                        damping_coef * (other * pick(5, away)) - (4.0 * damping_coef) * weighted
                    )
            return grads, damps

        return beside

    finish(0, edge_row(True, False))
    finish(1, edge_row(True, True))
    pl.loop(2, rows - 2, unroll=4)(lambda i: finish(i, None))
    finish(rows - 2, edge_row(False, True))
    finish(rows - 1, edge_row(False, False))

    @pl.loop(0, rows)
    def _(i):
        out_copy(i).wait()


def call(kernel, outs, operands, scratch, flops, name, spaces=None, far=()):
    spec = lambda n: pl.BlockSpec(memory_space=pltpu.HBM if n in far else VMEM)
    size = sum(4 * a.size for a in operands) + sum(4 * o.size for o in outs)
    operands = [
        pltpu.with_memory_space_constraint(a, pltpu.HBM) if n in far else a
        for n, a in enumerate(operands)
    ]
    return pl.pallas_call(
        kernel,
        out_shape=outs,
        in_specs=[spec(n) for n in range(len(operands))],
        out_specs=[pl.BlockSpec(memory_space=s) for s in (spaces or [VMEM] * len(outs))],
        scratch_shapes=scratch,
        cost_estimate=pl.CostEstimate(flops=flops, transcendentals=0, bytes_accessed=size),
        compiler_params=pltpu.CompilerParams(vmem_limit_bytes=16 << 20),
        name=name,
    )(*operands)


def local(
    primitive, adjoint_state, objective_grad, front_height,
    shock_state, state_by_height, state_by_slope, fitted_flags,
):
    _, rows, columns, depth = adjoint_state.shape
    tiles = columns // 8
    su_count, sv_count, lines = (lax.axis_size(a) for a in ("su", "sv", "nrm"))
    total_depth = depth * lines
    shape = lambda *s: jax.ShapeDtypeStruct(s, f32)
    field = shape(5, rows, columns, depth)
    plane = shape(rows, columns, depth)
    points = 5 * rows * columns * depth

    packet, su_a, su_b, sv_a, sv_b, normal, flux, enth, tone, inverse, prim, psi = call(
        functools.partial(prepare_kernel, rows, tiles, depth, total_depth, rows // 4),
        [
            shape(columns, 256),
            shape(6, 2, columns, depth),
            shape(6, 2, columns, depth),
            shape(6, 2 * rows, depth),
            shape(6, 2 * rows, depth),
            field, field, plane, plane,
            shape(columns, 128),
            field, field,
        ],
        (
            primitive, adjoint_state, front_height,
            shock_state, state_by_height, state_by_slope, fitted_flags,
        ),
        [
            VMEM((3, 128, 128), f32),
            VMEM((3, 128, 128), f32),
            VMEM((columns, 128), f32),
            VMEM((rows, columns, depth), f32),
            VMEM((rows, columns, depth), f32),
            VMEM((rows, columns), f32),
            VMEM((5, rows, columns), f32),
            VMEM((5, rows, columns), f32),
            VMEM((5, rows, columns), f32),
            VMEM((rows, columns), jnp.int32),
            pltpu.SemaphoreType.DMA((5,)),
            pltpu.SemaphoreType.DMA((2, 4)),
        ],
        12 * points,
        "prepare",
        far=range(7),
    )

    def pairs(count, shift):
        out = []
        for i in range(0, count, 2):
            a, b = (i + shift) % count, (i + shift + 1) % count
            out += [(a, b), (b, a)]
        return out

    arrived = lax.ppermute(packet, "nrm", [(0, 1), (1, 0)])
    su_a = lax.ppermute(su_a, "su", pairs(su_count, 0))
    su_b = lax.ppermute(su_b, "su", pairs(su_count, 1))
    sv_a = lax.ppermute(sv_a, "sv", pairs(sv_count, 0))
    sv_b = lax.ppermute(sv_b, "sv", pairs(sv_count, 1))

    chunk, mine = call(
        functools.partial(
            join_kernel, rows, tiles, depth, total_depth, rows * su_count, su_count
        ),
        [shape(su_count, 8, 128), shape(8, 128)],
        (packet, arrived, inverse),
        [],
        JOIN_COST * points,
        "join",
    )
    (base,) = call(
        functools.partial(interior_kernel, rows, tiles),
        [field],
        (prim, psi, objective_grad, normal, enth, tone),
        [
            VMEM((5, rows + 4, columns + 16, depth), f32),
            VMEM((5, rows + 4, columns, depth), f32),
            VMEM((5, rows, columns + 16, depth), f32),
            VMEM((5, rows, columns, depth), f32),
            pltpu.SemaphoreType.DMA((4,)),
        ],
        INTERIOR_COST * points,
        "interior",
        far=(2,),
    )
    chunk, su_a, su_b, sv_a, sv_b, base = lax.optimization_barrier(
        (chunk, su_a, su_b, sv_a, sv_b, base)
    )
    chunks = lax.all_to_all(chunk, "su", 0, 0)
    result, slope = call(
        functools.partial(
            final_kernel, rows, tiles, depth, total_depth, su_count, sv_count
        ),
        [field, shape(rows, columns)],
        (
            prim, base, flux, enth, inverse,
            arrived, mine, su_a, su_b, sv_a, sv_b, chunks,
        ),
        [
            VMEM((10, 2 * rows + 8, depth), f32),
            VMEM((10, 2 * rows + 16, depth), f32),
            VMEM((128, 128), f32),
            VMEM((5, rows, columns, depth), f32),
            pltpu.SemaphoreType.DMA((rows,)),
        ],
        20 * points,
        "final",
        [pltpu.HBM, VMEM],
    )
    return result, slope


def solution(mesh):
    wide = P(None, "su", "sv", "nrm")
    flat = P("su", "sv")
    front = P(None, "su", "sv")
    return jax.shard_map(
        local,
        mesh=mesh,
        in_specs=(wide, wide, wide, flat, front, front, front, flat),
        out_specs=(wide, flat),
        check_vma=False,
    )
```

```python
import functools

import jax
import jax.numpy as jnp
from jax import lax
from jax.experimental import pallas as pl
from jax.experimental.pallas import tpu as pltpu
from jax.sharding import PartitionSpec as P

gamma_ratio = 1.4
damping_coef = 0.0625
stretch_rate = 2.2
gm = gamma_ratio - 1.0
f32 = jnp.float32
VMEM = pltpu.VMEM
JOIN_COST = 5_000
INTERIOR_COST = 5_000


def lanes(shape=(8, 128)):
    return lax.broadcasted_iota(jnp.int32, shape, 1)


def spread_lane(tile, lane):
    return jnp.broadcast_to(tile[:, lane : lane + 1], tile.shape)


def inv_stretch_at(index, total_depth):
    return 1.0 / jnp.exp(stretch_rate * ((index + 0.5) / total_depth - 1.0))


def even(axis):
    return lax.rem(lax.axis_index(axis), 2) == 0


def flux_of(rho, u1, u2, u3, p, enthalpy):
    mass = rho * u3
    return (mass, mass * u1, mass * u2, mass * u3 + p, mass * enthalpy)


def thermo(rho, u1, u2, u3, p):
    half = 0.5 * (u1 * u1 + u2 * u2 + u3 * u3)
    return gm * half, (gamma_ratio / gm) * (p / rho) + half


def part(array, q, rows):
    return pltpu.roll(array, 128 - rows * q, 1) if q else array


def prepare_kernel(
    rows, tiles, depth, total_depth, step_rows,
    prim_far, psi_far, height_far, shock_far, by_height_far, by_slope_far, flags_far,
    packet, su_a, su_b, sv_a, sv_b, normal, flux, enth, tone, inverse, prim, psi,
    turn, facts, tops, feet, spread, work, height, shock, by_height, by_slope, flags, small, large,
):
    surfaces = [
        pltpu.make_async_copy(far, near, small.at[n])
        for n, (far, near) in enumerate(
            (
                (height_far, height),
                (shock_far, shock),
                (by_height_far, by_height),
                (by_slope_far, by_slope),
                (flags_far, flags),
            )
        )
    ]
    chunks = rows // step_rows
    loads = []
    for c in range(chunks):
        part_rows = pl.ds(c * step_rows, step_rows)
        loads.append(
            [
                pltpu.make_async_copy(far.at[:, part_rows], near.at[:, part_rows], large.at[n, c])
                for n, (far, near) in enumerate(((prim_far, prim), (psi_far, psi)))
            ]
        )
    for copy in surfaces:
        copy.start()
    for pair in loads:
        for copy in pair:
            copy.start()

    nrm = lax.axis_index("nrm")
    first = nrm == 0
    lane = lanes()
    lane_row = lanes((1, 128))
    columns = 8 * tiles
    spans = [slice(8 * t, 8 * t + 8) for t in range(tiles)]
    depth_index = (lane_row + nrm * depth).astype(f32)
    weight = 0.5 * inv_stretch_at(depth_index, total_depth)
    lower = jnp.broadcast_to(jnp.where(lane_row == depth - 1, 0.0, weight), (8, 128))
    upper = jnp.broadcast_to(jnp.where(lane_row == 0, 0.0, weight), (8, 128))
    top_scale = 0.5 * inv_stretch_at(
        jnp.full((1, 128), total_depth - 1, f32), total_depth
    )
    front = jnp.where(first, 0.0, 1.0)
    extra = jnp.where(first, 1, 0)

    turn[...] = jnp.zeros_like(turn)
    tops[...] = jnp.zeros_like(tops)
    feet[...] = jnp.zeros_like(feet)
    packet[...] = jnp.zeros_like(packet)
    for c in range(chunks):
        for copy in loads[c]:
            copy.wait()
        mine = range(c * step_rows, (c + 1) * step_rows)
        for i in mine:
            for span in spans:
                rho, u1, u2, u3, p = (prim[q, i, span, :] for q in range(5))
                ratio = p / rho
                enthalpy = (gamma_ratio / gm) * ratio + 0.5 * (u1 * u1 + u2 * u2 + u3 * u3)
                for q, value in enumerate(flux_of(rho, u1, u2, u3, p, enthalpy)):
                    flux[q, i, span, :] = value
                enth[i, span, :] = enthalpy
                tone[i, span, :] = jnp.sqrt(gamma_ratio * ratio)
        if c == 0:
            for copy in surfaces:
                copy.wait()
            for place, array in enumerate(
                [height[...]]
                + [shock[q] for q in range(5)]
                + [flags[...].astype(f32)]
            ):
                turn[0, rows * place : rows * place + rows, 0:columns] = array
            for q in range(5):
                turn[1, rows * q : rows * q + rows, 0:columns] = by_height[q]
                turn[2, rows * q : rows * q + rows, 0:columns] = by_slope[q]
            for n in range(3):
                facts[n] = turn[n].T
            for span in spans:
                inverse[span, :] = jnp.where(
                    lane < rows, 1.0 / jnp.where(lane < rows, facts[0, span, :], 1.0), 0.0
                )
            for span in spans:
                inv_height = inverse[span, :]
                for i in range(rows):
                    spread[i, span, :] = spread_lane(inv_height, i)
        for i in mine:
            for span in spans:
                inv = spread[i, span, :]
                low, high = lower * inv, upper * inv
                total = None
                for q in range(5):
                    value = psi[q, i, span, :]
                    step = pltpu.roll(value * low, 1, 1) - pltpu.roll(value * high, 127, 1)
                    normal[q, i, span, :] = step
                    term = flux[q, i, span, :] * step
                    total = term if total is None else total + term
                work[i, span, :] = total
        for span in spans:
            high, low = tops[span, :], feet[span, :]
            packed = packet[span, 128:256]
            for q in range(5):
                for i in mine:
                    spot = rows * q + i
                    moved = pltpu.roll(psi[q, i, span, :], spot + 1, 1)
                    high = jnp.where(lane == spot, moved, high)
                    low = jnp.where(lane == spot + 1, moved, low)
                    moved = pltpu.roll(flux[q, i, span, :], spot + extra, 1)
                    packed = jnp.where(lane == spot, moved, packed)
            tops[span, :] = high
            feet[span, :] = low
            packet[span, 128:256] = packed

    for span in spans:
        packet[span, 0:128] = jnp.where(
            first, tops[span, :], pltpu.roll(feet[span, :], 127, 1)
        )

    for span in spans:
        gathered = jnp.zeros((8, 128), f32)
        for i in range(rows):
            total = jnp.sum(work[i, span, :], axis=1, keepdims=True)
            gathered = jnp.where(lane == i, jnp.broadcast_to(total, (8, 128)), gathered)
        turn[0, span, :] = gathered

    for span in spans:
        inv_height = inverse[span, :]
        gathered = turn[0, span, :]
        inside = lane < rows
        surf = facts[0, span, :]
        rho, u1, u2, u3, p = (
            jnp.where(inside, part(surf, q + 1, rows), 1.0) for q in range(5)
        )
        fitted = jnp.where(inside, part(surf, 6, rows), 0.0)
        scale = top_scale * inv_height
        last = tops[span, :]
        s0, s1, s2, s3, s4 = (part(last, q, rows) * scale for q in range(5))
        kinetic, enthalpy = thermo(rho, u1, u2, u3, p)
        fluxes = flux_of(rho, u1, u2, u3, p, enthalpy)
        top_work = (
            fluxes[0] * s0 + fluxes[1] * s1 + fluxes[2] * s2 + fluxes[3] * s3 + fluxes[4] * s4
        )
        dotted = u1 * s1 + u2 * s2 + u3 * s3
        shared = gm * (s3 + u3 * s4)
        common = s0 + dotted + enthalpy * s4
        adjoint = (
            kinetic * s3 - u3 * dotted + u3 * (kinetic - enthalpy) * s4,
            u3 * s1 - u1 * shared,
            u3 * s2 - u2 * shared,
            u3 * s3 - u3 * shared + common,
            gm * s3 + gamma_ratio * u3 * s4,
        )
        heights = facts[1, span, :]
        slopes = facts[2, span, :]
        by_h = sum(adjoint[q] * part(heights, q, rows) for q in range(5))
        by_s = sum(adjoint[q] * part(slopes, q, rows) for q in range(5))
        metric = -inv_height * (gathered + front * top_work)
        term = jnp.where(inside, metric + front * fitted * by_h, 0.0)
        tilt = jnp.where(inside, front * fitted * by_s, 0.0)
        packet[span, 0:128] = (
            packet[span, 0:128] + pltpu.roll(term, 5 * rows, 1) + pltpu.roll(tilt, 6 * rows, 1)
        )

    su_even, sv_even = even("su"), even("sv")
    high_row = rows - 2
    row_a = jnp.where(su_even, high_row, 0)
    row_b = high_row - row_a
    for r in range(2):
        for ref, row in ((su_a, row_a + r), (su_b, row_b + r)):
            for q in range(5):
                ref[q, r] = psi[q, row]
            ref[5, r] = jnp.abs(prim[1, row]) + tone[row]
    for i in range(rows):
        pair = slice(2 * i, 2 * i + 2)
        for q in range(6):
            if q < 5:
                low, high = psi[q, i, 0:2, :], psi[q, i, columns - 2 : columns, :]
            else:
                low = jnp.abs(prim[2, i, 0:2, :]) + tone[i, 0:2, :]
                high = (
                    jnp.abs(prim[2, i, columns - 2 : columns, :])
                    + tone[i, columns - 2 : columns, :]
                )
            sv_a[q, pair, :] = jnp.where(sv_even, high, low)
            sv_b[q, pair, :] = jnp.where(sv_even, low, high)


def join_kernel(
    rows, tiles, depth, total_depth, surface, fan, own, arrived, inverse, chunk, mine
):
    first = lax.axis_index("nrm") == 0
    lane = lanes()
    one = jnp.zeros((1, 128), f32)
    before = 0.5 * inv_stretch_at(one + (depth - 1), total_depth)
    after = 0.5 * inv_stretch_at(one + depth, total_depth)
    own_scale = jnp.where(first, before, after)
    far_scale = jnp.where(first, after, before)
    sign = jnp.where(first, 1.0, -1.0)
    sums = jnp.zeros((8, 128), f32)
    kept = jnp.zeros((8, 128), f32)
    for t in range(tiles):
        span = slice(8 * t, 8 * t + 8)
        near, near_flux = own[span, 0:128], own[span, 128:256]
        far, far_flux = arrived[span, 0:128], arrived[span, 128:256]
        cross = near_flux * (far * far_scale) - far_flux * (near * own_scale)
        cross = jnp.where(lane < 5 * rows, cross, 0.0)
        for d in (1, 2, 4):
            cross = cross + pltpu.roll(cross, rows * d, 1)
        inv_height = inverse[span, :]
        total = near + far
        inside = lane < rows
        term = jnp.where(
            inside, part(total, 5, rows) + sign * inv_height * inv_height * cross, 0.0
        )
        for d in (1, 2, 4, 8):
            term = term + pltpu.roll(term, 128 - d, 1)
        share = term * (1.0 / surface)
        slope = jnp.where(inside, share + part(total, 6, rows), 0.0)
        kept = kept + (pltpu.roll(slope, rows * t, 1) if t else slope)
        sums = jnp.where(lane == t, pltpu.roll(share, t, 1) if t else share, sums)
    mine[...] = kept
    for n in range(fan):
        chunk[n] = sums


def transposed(speeds, kinetic, enthalpy, first, second, third):
    given = [(d, g) for d, g in ((0, first), (1, second), (2, third)) if g is not None]
    add = lambda parts: functools.reduce(lambda x, y: x + y, parts)
    projected = add([g[d + 1] for d, g in given])
    energy = add([speeds[d] * g[4] for d, g in given])
    dots = {
        d: speeds[0] * g[1] + speeds[1] * g[2] + speeds[2] * g[3] for d, g in given
    }
    shared = gm * (projected + energy)
    out = [
        kinetic * projected
        - add([speeds[d] * dots[d] for d, _ in given])
        + (kinetic - enthalpy) * energy
    ]
    for c in range(3):
        value = add([speeds[d] * g[c + 1] for d, g in given]) - speeds[c] * shared
        for d, g in given:
            if d == c:
                value = value + (g[0] + dots[d] + enthalpy * g[4])
        out.append(value)
    out.append(gm * projected + gamma_ratio * energy)
    return out


near_weight, far_weight = 8.0 / 12.0, 1.0 / 12.0


def interior_kernel(
    rows, tiles, prim, psi, target_far, normal, enth, tone,
    base,
    wide, along, across, target, large,
):
    step_rows = 4
    columns = 8 * tiles
    loads = [
        pltpu.make_async_copy(
            target_far.at[:, pl.ds(r, step_rows)], target.at[:, pl.ds(r, step_rows)],
            large.at[r // step_rows],
        )
        for r in range(0, rows, step_rows)
    ]
    for copy in loads:
        copy.start()
    for q in range(5):
        for row in (0, 1, rows + 2, rows + 3):
            wide[q, row] = jnp.zeros_like(wide[q, row])
            along[q, row] = jnp.zeros_like(along[q, row])
        for i in range(rows):
            for low in (0, 8 + columns):
                wide[q, i + 2, low : low + 8, :] = jnp.zeros((8, 128), f32)
                across[q, i, low : low + 8, :] = jnp.zeros((8, 128), f32)

    @pl.loop(0, rows, unroll=4)
    def _(i):
        for t in range(tiles):
            span = slice(8 * t, 8 * t + 8)
            inner = slice(8 * t + 8, 8 * t + 16)
            sound = tone[i, span, :]
            radius_u = jnp.abs(prim[1, i, span, :]) + sound
            radius_v = jnp.abs(prim[2, i, span, :]) + sound
            for q in range(5):
                value = psi[q, i, span, :]
                wide[q, i + 2, inner, :] = value
                along[q, i + 2, span, :] = radius_u * value
                across[q, i, inner, :] = radius_v * value

    def fill(i):
        for t in range(tiles):
            span = slice(8 * t, 8 * t + 8)
            at = lambda k: slice(8 * t + 8 + k, 8 * t + 16 + k)
            first, second, third, damp = [], [], [], []
            for q in range(5):
                first.append(
                    near_weight * (wide[q, i + 1, at(0), :] - wide[q, i + 3, at(0), :])
                    - far_weight * (wide[q, i, at(0), :] - wide[q, i + 4, at(0), :])
                )
                second.append(
                    near_weight * (wide[q, i + 2, at(-1), :] - wide[q, i + 2, at(1), :])
                    - far_weight * (wide[q, i + 2, at(-2), :] - wide[q, i + 2, at(2), :])
                )
                far = (
                    along[q, i, span, :] + along[q, i + 4, span, :]
                    + across[q, i, at(-2), :] + across[q, i, at(2), :]
                )
                near = (
                    along[q, i + 1, span, :] + along[q, i + 3, span, :]
                    + across[q, i, at(-1), :] + across[q, i, at(1), :]
                )
                here = along[q, i + 2, span, :] + across[q, i, at(0), :]
                damp.append(
                    damping_coef * far - (4.0 * damping_coef) * near + (6.0 * damping_coef) * here
                )
                third.append(normal[q, i, span, :])
            speeds = tuple(prim[q, i, span, :] for q in (1, 2, 3))
            u1, u2, u3 = speeds
            kinetic = (0.5 * gm) * (u1 * u1 + u2 * u2 + u3 * u3)
            terms = transposed(speeds, kinetic, enth[i, span, :], first, second, third)
            for q in range(5):
                base[q, i, span, :] = target[q, i, span, :] + terms[q] + damp[q]

    for c, copy in enumerate(loads):
        copy.wait()
        pl.loop(c * step_rows, (c + 1) * step_rows, unroll=step_rows)(fill)


def final_kernel(
    rows, tiles, depth, total_depth, su_count, sv_count,
    prim, base, flux, enth, inverse, arrived, mine,
    su_a, su_b, sv_a, sv_b, chunks,
    result, slope,
    left, right, turn, done, sems,
):
    su, sv, nrm = lax.axis_index("su"), lax.axis_index("sv"), lax.axis_index("nrm")
    before = nrm == 0
    lane = lanes()
    line = lax.broadcasted_iota(jnp.int32, (8, 128), 0)
    columns = 8 * tiles
    ahead = jnp.zeros((8, 128), f32)
    for n in range(su_count):
        ahead = ahead + jnp.where(n > su, chunks[n], 0.0)
    upstream = jnp.zeros((8, 128), f32)
    for t in range(tiles):
        upstream = jnp.where(
            (lane >= rows * t) & (lane < rows * t + rows), spread_lane(ahead, t), upstream
        )
    packed = mine[...] + upstream
    turn[...] = jnp.zeros_like(turn)
    for t in range(tiles):
        turn[8 * t : 8 * t + 8, :] = pltpu.roll(packed, 128 - rows * t, 1) if t else packed
    slope[...] = turn[...].T[0:rows, 0:columns]

    one = jnp.zeros((1, 128), f32)
    edge_scale = jnp.where(
        before,
        -0.5 * inv_stretch_at(one + depth, total_depth),
        0.5 * inv_stretch_at(one + (depth - 1), total_depth),
    )
    entry = jnp.where(before, depth - 1, 0)
    at_entry = lane == entry
    for t in range(tiles):
        span = slice(8 * t, 8 * t + 8)
        repeated = inverse[span, :]
        for d in (1, 2, 4):
            repeated = repeated + pltpu.roll(repeated, rows * d, 1)
        turn[span, :] = arrived[span, 0:128] * edge_scale * repeated

    su_even, sv_even = even("su"), even("sv")
    for piece in range(2 * rows // 8):
        at = slice(8 * piece, 8 * piece + 8)
        outer = lax.rem(line, 2) == 0
        for swap, on, ref, offset, sign in (
            (sv_even, sv > 0, left, 0, 1.0),
            (~sv_even, sv < sv_count - 1, right, 8, -1.0),
        ):
            into = slice(8 * piece + offset, 8 * piece + offset + 8)
            pick = lambda q: jnp.where(swap, sv_b[q, at, :], sv_a[q, at, :])
            radius = pick(5)
            for q in range(5):
                value = jnp.where(on, pick(q), 0.0)
                weighted = value * radius
                grads, damps = [], []
                for array, close, away, kept in (
                    (value, sign * near_weight, -sign * far_weight, grads),
                    (weighted, -4.0 * damping_coef, damping_coef, damps),
                ):
                    if offset == 0:
                        even_part = close * pltpu.roll(array, 7, 0) + away * array
                        odd_part = away * array
                    else:
                        even_part = away * array
                        odd_part = close * pltpu.roll(array, 1, 0) + away * array
                    kept.append(jnp.where(outer, even_part, odd_part))
                ref[q, into, :] = grads[0]
                ref[5 + q, into, :] = damps[0]

    def out_copy(i):
        return pltpu.make_async_copy(done.at[:, i], result.at[:, i], sems.at[i])

    fraction = jnp.broadcast_to(
        ((lanes((1, 128)) + nrm * depth).astype(f32) + 0.5) / total_depth, (8, 128)
    )

    def finish(i, beside):
        turned = pltpu.roll(packed, 128 - i, 1)
        for t in range(tiles):
            span = slice(8 * t, 8 * t + 8)
            ends = turn[span, :]
            third = [
                jnp.where(at_entry, pltpu.roll(ends, entry + (128 - rows * q) - i, 1), 0.0)
                for q in range(5)
            ]
            first = second = None
            damp = [None] * 5
            if beside is not None:
                first, damp = beside(span)
            if t in (0, tiles - 1):
                ref, start = (left, 2 * i) if t == 0 else (right, 2 * i + 2)
                here = line < 2 if t == 0 else line >= 6
                load = lambda q: jnp.where(here, ref[q, pl.ds(start, 8), :], 0.0)
                second = [load(q) for q in range(5)]
                damp = [
                    load(5 + q) if damp[q] is None else damp[q] + load(5 + q) for q in range(5)
                ]
            speeds = tuple(prim[q, i, span, :] for q in (1, 2, 3))
            u1, u2, u3 = speeds
            kinetic = (0.5 * gm) * (u1 * u1 + u2 * u2 + u3 * u3)
            terms = transposed(speeds, kinetic, enth[i, span, :], first, second, third)
            ramp = fraction * spread_lane(turned, rows * t)
            for q in range(5):
                value = base[q, i, span, :] + terms[q] + ramp * flux[q, i, span, :]
                done[q, i, span, :] = value if damp[q] is None else value + damp[q]
        out_copy(i).start()

    def edge_row(low, inner):
        swap, on, sign = (
            (su_even, su > 0, 1.0) if low else (~su_even, su < su_count - 1, -1.0)
        )

        def beside(span):
            pick = lambda q, r: jnp.where(swap, su_b[q, r, span, :], su_a[q, r, span, :])
            close, away = (1, 0) if low else (0, 1)
            grads, damps = [], []
            for q in range(5):
                value = jnp.where(on, pick(q, close), 0.0)
                weighted = value * pick(5, close)
                if inner:
                    grads.append((-sign * far_weight) * value)
                    damps.append(damping_coef * weighted)
                else:
                    other = jnp.where(on, pick(q, away), 0.0)
                    grads.append((sign * near_weight) * value - (sign * far_weight) * other)
                    damps.append(
                        damping_coef * (other * pick(5, away)) - (4.0 * damping_coef) * weighted
                    )
            return grads, damps

        return beside

    finish(0, edge_row(True, False))
    finish(1, edge_row(True, True))
    pl.loop(2, rows - 2, unroll=4)(lambda i: finish(i, None))
    finish(rows - 2, edge_row(False, True))
    finish(rows - 1, edge_row(False, False))

    @pl.loop(0, rows)
    def _(i):
        out_copy(i).wait()


def call(kernel, outs, operands, scratch, flops, name, spaces=None, far=()):
    spec = lambda n: pl.BlockSpec(memory_space=pltpu.HBM if n in far else VMEM)
    size = sum(4 * a.size for a in operands) + sum(4 * o.size for o in outs)
    operands = [
        pltpu.with_memory_space_constraint(a, pltpu.HBM) if n in far else a
        for n, a in enumerate(operands)
    ]
    return pl.pallas_call(
        kernel,
        out_shape=outs,
        in_specs=[spec(n) for n in range(len(operands))],
        out_specs=[pl.BlockSpec(memory_space=s) for s in (spaces or [VMEM] * len(outs))],
        scratch_shapes=scratch,
        cost_estimate=pl.CostEstimate(flops=flops, transcendentals=0, bytes_accessed=size),
        compiler_params=pltpu.CompilerParams(vmem_limit_bytes=16 << 20),
        name=name,
    )(*operands)


def local(
    primitive, adjoint_state, objective_grad, front_height,
    shock_state, state_by_height, state_by_slope, fitted_flags,
):
    _, rows, columns, depth = adjoint_state.shape
    tiles = columns // 8
    su_count, sv_count, lines = (lax.axis_size(a) for a in ("su", "sv", "nrm"))
    total_depth = depth * lines
    shape = lambda *s: jax.ShapeDtypeStruct(s, f32)
    field = shape(5, rows, columns, depth)
    plane = shape(rows, columns, depth)
    points = 5 * rows * columns * depth

    packet, su_a, su_b, sv_a, sv_b, normal, flux, enth, tone, inverse, prim, psi = call(
        functools.partial(prepare_kernel, rows, tiles, depth, total_depth, rows // 4),
        [
            shape(columns, 256),
            shape(6, 2, columns, depth),
            shape(6, 2, columns, depth),
            shape(6, 2 * rows, depth),
            shape(6, 2 * rows, depth),
            field, field, plane, plane,
            shape(columns, 128),
            field, field,
        ],
        (
            primitive, adjoint_state, front_height,
            shock_state, state_by_height, state_by_slope, fitted_flags,
        ),
        [
            VMEM((3, 128, 128), f32),
            VMEM((3, 128, 128), f32),
            VMEM((columns, 128), f32),
            VMEM((columns, 128), f32),
            VMEM((rows, columns, depth), f32),
            VMEM((rows, columns, depth), f32),
            VMEM((rows, columns), f32),
            VMEM((5, rows, columns), f32),
            VMEM((5, rows, columns), f32),
            VMEM((5, rows, columns), f32),
            VMEM((rows, columns), jnp.int32),
            pltpu.SemaphoreType.DMA((5,)),
            pltpu.SemaphoreType.DMA((2, 4)),
        ],
        12 * points,
        "prepare",
        far=range(7),
    )

    def pairs(count, shift):
        out = []
        for i in range(0, count, 2):
            a, b = (i + shift) % count, (i + shift + 1) % count
            out += [(a, b), (b, a)]
        return out

    arrived = lax.ppermute(packet, "nrm", [(0, 1), (1, 0)])
    su_a = lax.ppermute(su_a, "su", pairs(su_count, 0))
    su_b = lax.ppermute(su_b, "su", pairs(su_count, 1))
    sv_a = lax.ppermute(sv_a, "sv", pairs(sv_count, 0))
    sv_b = lax.ppermute(sv_b, "sv", pairs(sv_count, 1))

    chunk, mine = call(
        functools.partial(
            join_kernel, rows, tiles, depth, total_depth, rows * su_count, su_count
        ),
        [shape(su_count, 8, 128), shape(8, 128)],
        (packet, arrived, inverse),
        [],
        JOIN_COST * points,
        "join",
    )
    (base,) = call(
        functools.partial(interior_kernel, rows, tiles),
        [field],
        (prim, psi, objective_grad, normal, enth, tone),
        [
            VMEM((5, rows + 4, columns + 16, depth), f32),
            VMEM((5, rows + 4, columns, depth), f32),
            VMEM((5, rows, columns + 16, depth), f32),
            VMEM((5, rows, columns, depth), f32),
            pltpu.SemaphoreType.DMA((4,)),
        ],
        INTERIOR_COST * points,
        "interior",
        far=(2,),
    )
    chunk, su_a, su_b, sv_a, sv_b, base = lax.optimization_barrier(
        (chunk, su_a, su_b, sv_a, sv_b, base)
    )
    chunks = lax.all_to_all(chunk, "su", 0, 0)
    result, slope = call(
        functools.partial(
            final_kernel, rows, tiles, depth, total_depth, su_count, sv_count
        ),
        [field, shape(rows, columns)],
        (
            prim, base, flux, enth, inverse,
            arrived, mine, su_a, su_b, sv_a, sv_b, chunks,
        ),
        [
            VMEM((10, 2 * rows + 8, depth), f32),
            VMEM((10, 2 * rows + 16, depth), f32),
            VMEM((128, 128), f32),
            VMEM((5, rows, columns, depth), f32),
            pltpu.SemaphoreType.DMA((rows,)),
        ],
        20 * points,
        "final",
        [pltpu.HBM, VMEM],
    )
    return result, slope


def solution(mesh):
    wide = P(None, "su", "sv", "nrm")
    flat = P("su", "sv")
    front = P(None, "su", "sv")
    return jax.shard_map(
        local,
        mesh=mesh,
        in_specs=(wide, wide, wide, flat, front, front, front, flat),
        out_specs=(wide, flat),
        check_vma=False,
    )
```

```python
import functools

import jax
import jax.numpy as jnp
from jax import lax
from jax.experimental import pallas as pl
from jax.experimental.pallas import tpu as pltpu
from jax.sharding import PartitionSpec as P

gamma_ratio = 1.4
damping_coef = 0.0625
stretch_rate = 2.2
gm = gamma_ratio - 1.0
f32 = jnp.float32
VMEM = pltpu.VMEM
JOIN_COST = 100
INTERIOR_COST = 5_000


def lanes(shape=(8, 128)):
    return lax.broadcasted_iota(jnp.int32, shape, 1)


def spread_lane(tile, lane):
    return jnp.broadcast_to(tile[:, lane : lane + 1], tile.shape)


def inv_stretch_at(index, total_depth):
    return 1.0 / jnp.exp(stretch_rate * ((index + 0.5) / total_depth - 1.0))


def even(axis):
    return lax.rem(lax.axis_index(axis), 2) == 0


def flux_of(rho, u1, u2, u3, p, enthalpy):
    mass = rho * u3
    return (mass, mass * u1, mass * u2, mass * u3 + p, mass * enthalpy)


def thermo(rho, u1, u2, u3, p):
    half = 0.5 * (u1 * u1 + u2 * u2 + u3 * u3)
    return gm * half, (gamma_ratio / gm) * (p / rho) + half


def part(array, q, rows):
    return pltpu.roll(array, 128 - rows * q, 1) if q else array


def prepare_kernel(
    rows, tiles, depth, total_depth, step_rows,
    prim_far, psi_far, height_far, shock_far, by_height_far, by_slope_far, flags_far,
    packet, su_a, su_b, sv_a, sv_b, normal, flux, enth, tone, inverse, prim, psi,
    turn, facts, tops, feet, spread, work, height, shock, by_height, by_slope, flags, small, large,
):
    surfaces = [
        pltpu.make_async_copy(far, near, small.at[n])
        for n, (far, near) in enumerate(
            (
                (height_far, height),
                (shock_far, shock),
                (by_height_far, by_height),
                (by_slope_far, by_slope),
                (flags_far, flags),
            )
        )
    ]
    chunks = rows // step_rows
    loads = []
    for c in range(chunks):
        part_rows = pl.ds(c * step_rows, step_rows)
        loads.append(
            [
                pltpu.make_async_copy(far.at[:, part_rows], near.at[:, part_rows], large.at[n, c])
                for n, (far, near) in enumerate(((prim_far, prim), (psi_far, psi)))
            ]
        )
    for copy in surfaces:
        copy.start()
    for pair in loads:
        for copy in pair:
            copy.start()

    nrm = lax.axis_index("nrm")
    first = nrm == 0
    lane = lanes()
    lane_row = lanes((1, 128))
    columns = 8 * tiles
    spans = [slice(8 * t, 8 * t + 8) for t in range(tiles)]
    depth_index = (lane_row + nrm * depth).astype(f32)
    weight = 0.5 * inv_stretch_at(depth_index, total_depth)
    lower = jnp.broadcast_to(jnp.where(lane_row == depth - 1, 0.0, weight), (8, 128))
    upper = jnp.broadcast_to(jnp.where(lane_row == 0, 0.0, weight), (8, 128))
    top_scale = 0.5 * inv_stretch_at(
        jnp.full((1, 128), total_depth - 1, f32), total_depth
    )
    front = jnp.where(first, 0.0, 1.0)
    extra = jnp.where(first, 1, 0)

    turn[...] = jnp.zeros_like(turn)
    tops[...] = jnp.zeros_like(tops)
    feet[...] = jnp.zeros_like(feet)
    packet[...] = jnp.zeros_like(packet)
    for c in range(chunks):
        for copy in loads[c]:
            copy.wait()
        mine = range(c * step_rows, (c + 1) * step_rows)
        for i in mine:
            for span in spans:
                rho, u1, u2, u3, p = (prim[q, i, span, :] for q in range(5))
                ratio = p / rho
                enthalpy = (gamma_ratio / gm) * ratio + 0.5 * (u1 * u1 + u2 * u2 + u3 * u3)
                for q, value in enumerate(flux_of(rho, u1, u2, u3, p, enthalpy)):
                    flux[q, i, span, :] = value
                enth[i, span, :] = enthalpy
                tone[i, span, :] = jnp.sqrt(gamma_ratio * ratio)
        if c == 0:
            for copy in surfaces:
                copy.wait()
            for place, array in enumerate(
                [height[...]]
                + [shock[q] for q in range(5)]
                + [flags[...].astype(f32)]
            ):
                turn[0, rows * place : rows * place + rows, 0:columns] = array
            for q in range(5):
                turn[1, rows * q : rows * q + rows, 0:columns] = by_height[q]
                turn[2, rows * q : rows * q + rows, 0:columns] = by_slope[q]
            for n in range(3):
                facts[n] = turn[n].T
            for span in spans:
                inverse[span, :] = jnp.where(
                    lane < rows, 1.0 / jnp.where(lane < rows, facts[0, span, :], 1.0), 0.0
                )
            for span in spans:
                inv_height = inverse[span, :]
                for i in range(rows):
                    spread[i, span, :] = spread_lane(inv_height, i)
        for i in mine:
            for span in spans:
                inv = spread[i, span, :]
                low, high = lower * inv, upper * inv
                total = None
                for q in range(5):
                    value = psi[q, i, span, :]
                    step = pltpu.roll(value * low, 1, 1) - pltpu.roll(value * high, 127, 1)
                    normal[q, i, span, :] = step
                    term = flux[q, i, span, :] * step
                    total = term if total is None else total + term
                work[i, span, :] = total
        for span in spans:
            high, low = tops[span, :], feet[span, :]
            packed = packet[span, 128:256]
            for q in range(5):
                for i in mine:
                    spot = rows * q + i
                    moved = pltpu.roll(psi[q, i, span, :], spot + 1, 1)
                    high = jnp.where(lane == spot, moved, high)
                    low = jnp.where(lane == spot + 1, moved, low)
                    moved = pltpu.roll(flux[q, i, span, :], spot + extra, 1)
                    packed = jnp.where(lane == spot, moved, packed)
            tops[span, :] = high
            feet[span, :] = low
            packet[span, 128:256] = packed

    for span in spans:
        packet[span, 0:128] = jnp.where(
            first, tops[span, :], pltpu.roll(feet[span, :], 127, 1)
        )

    for span in spans:
        gathered = jnp.zeros((8, 128), f32)
        for i in range(rows):
            total = jnp.sum(work[i, span, :], axis=1, keepdims=True)
            gathered = jnp.where(lane == i, jnp.broadcast_to(total, (8, 128)), gathered)
        turn[0, span, :] = gathered

    for span in spans:
        inv_height = inverse[span, :]
        gathered = turn[0, span, :]
        inside = lane < rows
        surf = facts[0, span, :]
        rho, u1, u2, u3, p = (
            jnp.where(inside, part(surf, q + 1, rows), 1.0) for q in range(5)
        )
        fitted = jnp.where(inside, part(surf, 6, rows), 0.0)
        scale = top_scale * inv_height
        last = tops[span, :]
        s0, s1, s2, s3, s4 = (part(last, q, rows) * scale for q in range(5))
        kinetic, enthalpy = thermo(rho, u1, u2, u3, p)
        fluxes = flux_of(rho, u1, u2, u3, p, enthalpy)
        top_work = (
            fluxes[0] * s0 + fluxes[1] * s1 + fluxes[2] * s2 + fluxes[3] * s3 + fluxes[4] * s4
        )
        dotted = u1 * s1 + u2 * s2 + u3 * s3
        shared = gm * (s3 + u3 * s4)
        common = s0 + dotted + enthalpy * s4
        adjoint = (
            kinetic * s3 - u3 * dotted + u3 * (kinetic - enthalpy) * s4,
            u3 * s1 - u1 * shared,
            u3 * s2 - u2 * shared,
            u3 * s3 - u3 * shared + common,
            gm * s3 + gamma_ratio * u3 * s4,
        )
        heights = facts[1, span, :]
        slopes = facts[2, span, :]
        by_h = sum(adjoint[q] * part(heights, q, rows) for q in range(5))
        by_s = sum(adjoint[q] * part(slopes, q, rows) for q in range(5))
        metric = -inv_height * (gathered + front * top_work)
        term = jnp.where(inside, metric + front * fitted * by_h, 0.0)
        tilt = jnp.where(inside, front * fitted * by_s, 0.0)
        packet[span, 0:128] = (
            packet[span, 0:128] + pltpu.roll(term, 5 * rows, 1) + pltpu.roll(tilt, 6 * rows, 1)
        )

    su_even, sv_even = even("su"), even("sv")
    high_row = rows - 2
    row_a = jnp.where(su_even, high_row, 0)
    row_b = high_row - row_a
    for r in range(2):
        for ref, row in ((su_a, row_a + r), (su_b, row_b + r)):
            for q in range(5):
                ref[q, r] = psi[q, row]
            ref[5, r] = jnp.abs(prim[1, row]) + tone[row]
    for i in range(rows):
        pair = slice(2 * i, 2 * i + 2)
        for q in range(6):
            if q < 5:
                low, high = psi[q, i, 0:2, :], psi[q, i, columns - 2 : columns, :]
            else:
                low = jnp.abs(prim[2, i, 0:2, :]) + tone[i, 0:2, :]
                high = (
                    jnp.abs(prim[2, i, columns - 2 : columns, :])
                    + tone[i, columns - 2 : columns, :]
                )
            sv_a[q, pair, :] = jnp.where(sv_even, high, low)
            sv_b[q, pair, :] = jnp.where(sv_even, low, high)


def join_kernel(
    rows, tiles, depth, total_depth, surface, fan, own, arrived, inverse, chunk, mine
):
    first = lax.axis_index("nrm") == 0
    lane = lanes()
    one = jnp.zeros((1, 128), f32)
    before = 0.5 * inv_stretch_at(one + (depth - 1), total_depth)
    after = 0.5 * inv_stretch_at(one + depth, total_depth)
    own_scale = jnp.where(first, before, after)
    far_scale = jnp.where(first, after, before)
    sign = jnp.where(first, 1.0, -1.0)
    sums = jnp.zeros((8, 128), f32)
    kept = jnp.zeros((8, 128), f32)
    for t in range(tiles):
        span = slice(8 * t, 8 * t + 8)
        near, near_flux = own[span, 0:128], own[span, 128:256]
        far, far_flux = arrived[span, 0:128], arrived[span, 128:256]
        cross = near_flux * (far * far_scale) - far_flux * (near * own_scale)
        cross = jnp.where(lane < 5 * rows, cross, 0.0)
        for d in (1, 2, 4):
            cross = cross + pltpu.roll(cross, rows * d, 1)
        inv_height = inverse[span, :]
        total = near + far
        inside = lane < rows
        term = jnp.where(
            inside, part(total, 5, rows) + sign * inv_height * inv_height * cross, 0.0
        )
        for d in (1, 2, 4, 8):
            term = term + pltpu.roll(term, 128 - d, 1)
        share = term * (1.0 / surface)
        slope = jnp.where(inside, share + part(total, 6, rows), 0.0)
        kept = kept + (pltpu.roll(slope, rows * t, 1) if t else slope)
        sums = jnp.where(lane == t, pltpu.roll(share, t, 1) if t else share, sums)
    mine[...] = kept
    for n in range(fan):
        chunk[n] = sums


def transposed(speeds, kinetic, enthalpy, first, second, third):
    given = [(d, g) for d, g in ((0, first), (1, second), (2, third)) if g is not None]
    add = lambda parts: functools.reduce(lambda x, y: x + y, parts)
    projected = add([g[d + 1] for d, g in given])
    energy = add([speeds[d] * g[4] for d, g in given])
    dots = {
        d: speeds[0] * g[1] + speeds[1] * g[2] + speeds[2] * g[3] for d, g in given
    }
    shared = gm * (projected + energy)
    out = [
        kinetic * projected
        - add([speeds[d] * dots[d] for d, _ in given])
        + (kinetic - enthalpy) * energy
    ]
    for c in range(3):
        value = add([speeds[d] * g[c + 1] for d, g in given]) - speeds[c] * shared
        for d, g in given:
            if d == c:
                value = value + (g[0] + dots[d] + enthalpy * g[4])
        out.append(value)
    out.append(gm * projected + gamma_ratio * energy)
    return out


near_weight, far_weight = 8.0 / 12.0, 1.0 / 12.0


def interior_kernel(
    rows, tiles, prim, psi, target_far, normal, enth, tone,
    base,
    wide, along, across, target, large,
):
    step_rows = 4
    columns = 8 * tiles
    loads = [
        pltpu.make_async_copy(
            target_far.at[:, pl.ds(r, step_rows)], target.at[:, pl.ds(r, step_rows)],
            large.at[r // step_rows],
        )
        for r in range(0, rows, step_rows)
    ]
    for copy in loads:
        copy.start()
    for q in range(5):
        for i in range(rows):
            for low in (0, 8 + columns):
                wide[q, i + 2, low : low + 8, :] = jnp.zeros((8, 128), f32)
                across[q, i, low : low + 8, :] = jnp.zeros((8, 128), f32)

    @pl.loop(0, rows, unroll=4)
    def _(i):
        for t in range(tiles):
            span = slice(8 * t, 8 * t + 8)
            inner = slice(8 * t + 8, 8 * t + 16)
            sound = tone[i, span, :]
            radius_u = jnp.abs(prim[1, i, span, :]) + sound
            radius_v = jnp.abs(prim[2, i, span, :]) + sound
            for q in range(5):
                value = psi[q, i, span, :]
                wide[q, i + 2, inner, :] = value
                along[q, i, span, :] = radius_u * value
                across[q, i, inner, :] = radius_v * value

    def pair(i, tap, k, sign):
        if i < k:
            return sign * tap(k)
        if i + k >= rows:
            return tap(-k)
        return tap(-k) + tap(k) if sign > 0 else tap(-k) - tap(k)

    def fill(i):
        for t in range(tiles):
            span = slice(8 * t, 8 * t + 8)
            at = lambda k: slice(8 * t + 8 + k, 8 * t + 16 + k)
            first, second, third, damp = [], [], [], []
            for q in range(5):
                tap = lambda k: wide[q, i + 2 + k, at(0), :]
                first.append(
                    near_weight * pair(i, tap, 1, -1.0) - far_weight * pair(i, tap, 2, -1.0)
                )
                second.append(
                    near_weight * (wide[q, i + 2, at(-1), :] - wide[q, i + 2, at(1), :])
                    - far_weight * (wide[q, i + 2, at(-2), :] - wide[q, i + 2, at(2), :])
                )
                tap = lambda k: along[q, i + k, span, :]
                far = pair(i, tap, 2, 1.0) + (across[q, i, at(-2), :] + across[q, i, at(2), :])
                near = pair(i, tap, 1, 1.0) + (across[q, i, at(-1), :] + across[q, i, at(1), :])
                here = along[q, i, span, :] + across[q, i, at(0), :]
                damp.append(
                    damping_coef * far - (4.0 * damping_coef) * near + (6.0 * damping_coef) * here
                )
                third.append(normal[q, i, span, :])
            speeds = tuple(prim[q, i, span, :] for q in (1, 2, 3))
            u1, u2, u3 = speeds
            kinetic = (0.5 * gm) * (u1 * u1 + u2 * u2 + u3 * u3)
            terms = transposed(speeds, kinetic, enth[i, span, :], first, second, third)
            for q in range(5):
                base[q, i, span, :] = target[q, i, span, :] + terms[q] + damp[q]

    for c, copy in enumerate(loads):
        copy.wait()
        for i in range(c * step_rows, (c + 1) * step_rows):
            fill(i)


def final_kernel(
    rows, tiles, depth, total_depth, su_count, sv_count,
    prim, base, flux, enth, inverse, arrived, mine,
    su_a, su_b, sv_a, sv_b, chunks,
    result, slope,
    left, right, turn, done, sems,
):
    su, sv, nrm = lax.axis_index("su"), lax.axis_index("sv"), lax.axis_index("nrm")
    before = nrm == 0
    lane = lanes()
    line = lax.broadcasted_iota(jnp.int32, (8, 128), 0)
    columns = 8 * tiles
    ahead = jnp.zeros((8, 128), f32)
    for n in range(su_count):
        ahead = ahead + jnp.where(n > su, chunks[n], 0.0)
    upstream = jnp.zeros((8, 128), f32)
    for t in range(tiles):
        upstream = jnp.where(
            (lane >= rows * t) & (lane < rows * t + rows), spread_lane(ahead, t), upstream
        )
    packed = mine[...] + upstream
    turn[...] = jnp.zeros_like(turn)
    for t in range(tiles):
        turn[8 * t : 8 * t + 8, :] = pltpu.roll(packed, 128 - rows * t, 1) if t else packed
    slope[...] = turn[...].T[0:rows, 0:columns]

    one = jnp.zeros((1, 128), f32)
    edge_scale = jnp.where(
        before,
        -0.5 * inv_stretch_at(one + depth, total_depth),
        0.5 * inv_stretch_at(one + (depth - 1), total_depth),
    )
    entry = jnp.where(before, depth - 1, 0)
    at_entry = lane == entry
    for t in range(tiles):
        span = slice(8 * t, 8 * t + 8)
        repeated = inverse[span, :]
        for d in (1, 2, 4):
            repeated = repeated + pltpu.roll(repeated, rows * d, 1)
        turn[span, :] = arrived[span, 0:128] * edge_scale * repeated

    su_even, sv_even = even("su"), even("sv")
    for piece in range(2 * rows // 8):
        at = slice(8 * piece, 8 * piece + 8)
        outer = lax.rem(line, 2) == 0
        for swap, on, ref, offset, sign in (
            (sv_even, sv > 0, left, 0, 1.0),
            (~sv_even, sv < sv_count - 1, right, 8, -1.0),
        ):
            into = slice(8 * piece + offset, 8 * piece + offset + 8)
            pick = lambda q: jnp.where(swap, sv_b[q, at, :], sv_a[q, at, :])
            radius = pick(5)
            for q in range(5):
                value = jnp.where(on, pick(q), 0.0)
                weighted = value * radius
                grads, damps = [], []
                for array, close, away, kept in (
                    (value, sign * near_weight, -sign * far_weight, grads),
                    (weighted, -4.0 * damping_coef, damping_coef, damps),
                ):
                    if offset == 0:
                        even_part = close * pltpu.roll(array, 7, 0) + away * array
                        odd_part = away * array
                    else:
                        even_part = away * array
                        odd_part = close * pltpu.roll(array, 1, 0) + away * array
                    kept.append(jnp.where(outer, even_part, odd_part))
                ref[q, into, :] = grads[0]
                ref[5 + q, into, :] = damps[0]

    def out_copy(i):
        return pltpu.make_async_copy(done.at[:, i], result.at[:, i], sems.at[i])

    fraction = jnp.broadcast_to(
        ((lanes((1, 128)) + nrm * depth).astype(f32) + 0.5) / total_depth, (8, 128)
    )

    def finish(i, beside):
        turned = pltpu.roll(packed, 128 - i, 1)
        for t in range(tiles):
            span = slice(8 * t, 8 * t + 8)
            ends = turn[span, :]
            third = [
                jnp.where(at_entry, pltpu.roll(ends, entry + (128 - rows * q) - i, 1), 0.0)
                for q in range(5)
            ]
            first = second = None
            damp = [None] * 5
            if beside is not None:
                first, damp = beside(span)
            if t in (0, tiles - 1):
                ref, start = (left, 2 * i) if t == 0 else (right, 2 * i + 2)
                here = line < 2 if t == 0 else line >= 6
                load = lambda q: jnp.where(here, ref[q, pl.ds(start, 8), :], 0.0)
                second = [load(q) for q in range(5)]
                damp = [
                    load(5 + q) if damp[q] is None else damp[q] + load(5 + q) for q in range(5)
                ]
            speeds = tuple(prim[q, i, span, :] for q in (1, 2, 3))
            u1, u2, u3 = speeds
            kinetic = (0.5 * gm) * (u1 * u1 + u2 * u2 + u3 * u3)
            terms = transposed(speeds, kinetic, enth[i, span, :], first, second, third)
            ramp = fraction * spread_lane(turned, rows * t)
            for q in range(5):
                value = base[q, i, span, :] + terms[q] + ramp * flux[q, i, span, :]
                done[q, i, span, :] = value if damp[q] is None else value + damp[q]
        out_copy(i).start()

    def edge_row(low, inner):
        swap, on, sign = (
            (su_even, su > 0, 1.0) if low else (~su_even, su < su_count - 1, -1.0)
        )

        def beside(span):
            pick = lambda q, r: jnp.where(swap, su_b[q, r, span, :], su_a[q, r, span, :])
            close, away = (1, 0) if low else (0, 1)
            grads, damps = [], []
            for q in range(5):
                value = jnp.where(on, pick(q, close), 0.0)
                weighted = value * pick(5, close)
                if inner:
                    grads.append((-sign * far_weight) * value)
                    damps.append(damping_coef * weighted)
                else:
                    other = jnp.where(on, pick(q, away), 0.0)
                    grads.append((sign * near_weight) * value - (sign * far_weight) * other)
                    damps.append(
                        damping_coef * (other * pick(5, away)) - (4.0 * damping_coef) * weighted
                    )
            return grads, damps

        return beside

    finish(0, edge_row(True, False))
    finish(1, edge_row(True, True))
    pl.loop(2, rows - 2, unroll=4)(lambda i: finish(i, None))
    finish(rows - 2, edge_row(False, True))
    finish(rows - 1, edge_row(False, False))

    @pl.loop(0, rows)
    def _(i):
        out_copy(i).wait()


def call(kernel, outs, operands, scratch, flops, name, spaces=None, far=()):
    spec = lambda n: pl.BlockSpec(memory_space=pltpu.HBM if n in far else VMEM)
    size = sum(4 * a.size for a in operands) + sum(4 * o.size for o in outs)
    operands = [
        pltpu.with_memory_space_constraint(a, pltpu.HBM) if n in far else a
        for n, a in enumerate(operands)
    ]
    return pl.pallas_call(
        kernel,
        out_shape=outs,
        in_specs=[spec(n) for n in range(len(operands))],
        out_specs=[pl.BlockSpec(memory_space=s) for s in (spaces or [VMEM] * len(outs))],
        scratch_shapes=scratch,
        cost_estimate=pl.CostEstimate(flops=flops, transcendentals=0, bytes_accessed=size),
        compiler_params=pltpu.CompilerParams(vmem_limit_bytes=16 << 20),
        name=name,
    )(*operands)


def local(
    primitive, adjoint_state, objective_grad, front_height,
    shock_state, state_by_height, state_by_slope, fitted_flags,
):
    _, rows, columns, depth = adjoint_state.shape
    tiles = columns // 8
    su_count, sv_count, lines = (lax.axis_size(a) for a in ("su", "sv", "nrm"))
    total_depth = depth * lines
    shape = lambda *s: jax.ShapeDtypeStruct(s, f32)
    field = shape(5, rows, columns, depth)
    plane = shape(rows, columns, depth)
    points = 5 * rows * columns * depth

    packet, su_a, su_b, sv_a, sv_b, normal, flux, enth, tone, inverse, prim, psi = call(
        functools.partial(prepare_kernel, rows, tiles, depth, total_depth, rows // 4),
        [
            shape(columns, 256),
            shape(6, 2, columns, depth),
            shape(6, 2, columns, depth),
            shape(6, 2 * rows, depth),
            shape(6, 2 * rows, depth),
            field, field, plane, plane,
            shape(columns, 128),
            field, field,
        ],
        (
            primitive, adjoint_state, front_height,
            shock_state, state_by_height, state_by_slope, fitted_flags,
        ),
        [
            VMEM((3, 128, 128), f32),
            VMEM((3, 128, 128), f32),
            VMEM((columns, 128), f32),
            VMEM((columns, 128), f32),
            VMEM((rows, columns, depth), f32),
            VMEM((rows, columns, depth), f32),
            VMEM((rows, columns), f32),
            VMEM((5, rows, columns), f32),
            VMEM((5, rows, columns), f32),
            VMEM((5, rows, columns), f32),
            VMEM((rows, columns), jnp.int32),
            pltpu.SemaphoreType.DMA((5,)),
            pltpu.SemaphoreType.DMA((2, 4)),
        ],
        12 * points,
        "prepare",
        far=range(7),
    )

    def pairs(count, shift):
        out = []
        for i in range(0, count, 2):
            a, b = (i + shift) % count, (i + shift + 1) % count
            out += [(a, b), (b, a)]
        return out

    arrived = lax.ppermute(packet, "nrm", [(0, 1), (1, 0)])
    su_a = lax.ppermute(su_a, "su", pairs(su_count, 0))
    su_b = lax.ppermute(su_b, "su", pairs(su_count, 1))
    sv_a = lax.ppermute(sv_a, "sv", pairs(sv_count, 0))
    sv_b = lax.ppermute(sv_b, "sv", pairs(sv_count, 1))

    chunk, mine = call(
        functools.partial(
            join_kernel, rows, tiles, depth, total_depth, rows * su_count, su_count
        ),
        [shape(su_count, 8, 128), shape(8, 128)],
        (packet, arrived, inverse),
        [],
        JOIN_COST * points,
        "join",
    )
    (base,) = call(
        functools.partial(interior_kernel, rows, tiles),
        [field],
        (prim, psi, objective_grad, normal, enth, tone),
        [
            VMEM((5, rows + 4, columns + 16, depth), f32),
            VMEM((5, rows, columns, depth), f32),
            VMEM((5, rows, columns + 16, depth), f32),
            VMEM((5, rows, columns, depth), f32),
            pltpu.SemaphoreType.DMA((4,)),
        ],
        INTERIOR_COST * points,
        "interior",
        far=(2,),
    )
    chunk, su_a, su_b, sv_a, sv_b, base = lax.optimization_barrier(
        (chunk, su_a, su_b, sv_a, sv_b, base)
    )
    chunks = lax.all_to_all(chunk, "su", 0, 0)
    result, slope = call(
        functools.partial(
            final_kernel, rows, tiles, depth, total_depth, su_count, sv_count
        ),
        [field, shape(rows, columns)],
        (
            prim, base, flux, enth, inverse,
            arrived, mine, su_a, su_b, sv_a, sv_b, chunks,
        ),
        [
            VMEM((10, 2 * rows + 8, depth), f32),
            VMEM((10, 2 * rows + 16, depth), f32),
            VMEM((128, 128), f32),
            VMEM((5, rows, columns, depth), f32),
            pltpu.SemaphoreType.DMA((rows,)),
        ],
        20 * points,
        "final",
        [pltpu.HBM, VMEM],
    )
    return result, slope


def solution(mesh):
    wide = P(None, "su", "sv", "nrm")
    flat = P("su", "sv")
    front = P(None, "su", "sv")
    return jax.shard_map(
        local,
        mesh=mesh,
        in_specs=(wide, wide, wide, flat, front, front, front, flat),
        out_specs=(wide, flat),
        check_vma=False,
    )
```

```python
import functools

import jax
import jax.numpy as jnp
from jax import lax
from jax.experimental import pallas as pl
from jax.experimental.pallas import tpu as pltpu
from jax.sharding import PartitionSpec as P

gamma_ratio = 1.4
damping_coef = 0.0625
stretch_rate = 2.2
gm = gamma_ratio - 1.0
f32 = jnp.float32
VMEM = pltpu.VMEM
JOIN_COST = 100
INTERIOR_COST = 5_000


def lanes(shape=(8, 128)):
    return lax.broadcasted_iota(jnp.int32, shape, 1)


def spread_lane(tile, lane):
    return jnp.broadcast_to(tile[:, lane : lane + 1], tile.shape)


def inv_stretch_at(index, total_depth):
    return 1.0 / jnp.exp(stretch_rate * ((index + 0.5) / total_depth - 1.0))


def even(axis):
    return lax.rem(lax.axis_index(axis), 2) == 0


def flux_of(rho, u1, u2, u3, p, enthalpy):
    mass = rho * u3
    return (mass, mass * u1, mass * u2, mass * u3 + p, mass * enthalpy)


def thermo(rho, u1, u2, u3, p):
    half = 0.5 * (u1 * u1 + u2 * u2 + u3 * u3)
    return gm * half, (gamma_ratio / gm) * (p / rho) + half


def part(array, q, rows):
    return pltpu.roll(array, 128 - rows * q, 1) if q else array


def prepare_kernel(
    rows, tiles, depth, total_depth, step_rows,
    prim_far, psi_far, height_far, shock_far, by_height_far, by_slope_far, flags_far,
    packet, su_a, su_b, sv_a, sv_b, normal, flux, enth, tone, inverse, prim, psi,
    turn, facts, tops, feet, spread, work, height, shock, by_height, by_slope, flags, small, large,
):
    surfaces = [
        pltpu.make_async_copy(far, near, small.at[n])
        for n, (far, near) in enumerate(
            (
                (height_far, height),
                (shock_far, shock),
                (by_height_far, by_height),
                (by_slope_far, by_slope),
                (flags_far, flags),
            )
        )
    ]
    chunks = rows // step_rows
    loads = []
    for c in range(chunks):
        part_rows = pl.ds(c * step_rows, step_rows)
        loads.append(
            [
                pltpu.make_async_copy(far.at[:, part_rows], near.at[:, part_rows], large.at[n, c])
                for n, (far, near) in enumerate(((prim_far, prim), (psi_far, psi)))
            ]
        )
    for copy in surfaces:
        copy.start()
    for pair in loads:
        for copy in pair:
            copy.start()

    nrm = lax.axis_index("nrm")
    first = nrm == 0
    lane = lanes()
    lane_row = lanes((1, 128))
    columns = 8 * tiles
    spans = [slice(8 * t, 8 * t + 8) for t in range(tiles)]
    depth_index = (lane_row + nrm * depth).astype(f32)
    weight = 0.5 * inv_stretch_at(depth_index, total_depth)
    lower = jnp.broadcast_to(jnp.where(lane_row == depth - 1, 0.0, weight), (8, 128))
    upper = jnp.broadcast_to(jnp.where(lane_row == 0, 0.0, weight), (8, 128))
    top_scale = 0.5 * inv_stretch_at(
        jnp.full((1, 128), total_depth - 1, f32), total_depth
    )
    front = jnp.where(first, 0.0, 1.0)
    extra = jnp.where(first, 1, 0)

    turn[...] = jnp.zeros_like(turn)
    tops[...] = jnp.zeros_like(tops)
    feet[...] = jnp.zeros_like(feet)
    packet[...] = jnp.zeros_like(packet)
    for c in range(chunks):
        for copy in loads[c]:
            copy.wait()
        mine = range(c * step_rows, (c + 1) * step_rows)
        for i in mine:
            for span in spans:
                rho, u1, u2, u3, p = (prim[q, i, span, :] for q in range(5))
                ratio = p / rho
                enthalpy = (gamma_ratio / gm) * ratio + 0.5 * (u1 * u1 + u2 * u2 + u3 * u3)
                for q, value in enumerate(flux_of(rho, u1, u2, u3, p, enthalpy)):
                    flux[q, i, span, :] = value
                enth[i, span, :] = enthalpy
                tone[i, span, :] = jnp.sqrt(gamma_ratio * ratio)
        if c == 0:
            for copy in surfaces:
                copy.wait()
            for place, array in enumerate(
                [height[...]]
                + [shock[q] for q in range(5)]
                + [flags[...].astype(f32)]
            ):
                turn[0, rows * place : rows * place + rows, 0:columns] = array
            for q in range(5):
                turn[1, rows * q : rows * q + rows, 0:columns] = by_height[q]
                turn[2, rows * q : rows * q + rows, 0:columns] = by_slope[q]
            for n in range(3):
                facts[n] = turn[n].T
            for span in spans:
                inverse[span, :] = jnp.where(
                    lane < rows, 1.0 / jnp.where(lane < rows, facts[0, span, :], 1.0), 0.0
                )
            for span in spans:
                inv_height = inverse[span, :]
                for i in range(rows):
                    spread[i, span, :] = spread_lane(inv_height, i)
        for i in mine:
            for span in spans:
                inv = spread[i, span, :]
                low, high = lower * inv, upper * inv
                total = None
                for q in range(5):
                    value = psi[q, i, span, :]
                    step = pltpu.roll(value * low, 1, 1) - pltpu.roll(value * high, 127, 1)
                    normal[q, i, span, :] = step
                    term = flux[q, i, span, :] * step
                    total = term if total is None else total + term
                work[i, span, :] = total
        for span in spans:
            high, low = tops[span, :], feet[span, :]
            packed = packet[span, 128:256]
            for q in range(5):
                for i in mine:
                    spot = rows * q + i
                    moved = pltpu.roll(psi[q, i, span, :], spot + 1, 1)
                    high = jnp.where(lane == spot, moved, high)
                    low = jnp.where(lane == spot + 1, moved, low)
                    moved = pltpu.roll(flux[q, i, span, :], spot + extra, 1)
                    packed = jnp.where(lane == spot, moved, packed)
            tops[span, :] = high
            feet[span, :] = low
            packet[span, 128:256] = packed

    for span in spans:
        packet[span, 0:128] = jnp.where(
            first, tops[span, :], pltpu.roll(feet[span, :], 127, 1)
        )

    for span in spans:
        gathered = jnp.zeros((8, 128), f32)
        for i in range(rows):
            total = jnp.sum(work[i, span, :], axis=1, keepdims=True)
            gathered = jnp.where(lane == i, jnp.broadcast_to(total, (8, 128)), gathered)
        turn[0, span, :] = gathered

    for span in spans:
        inv_height = inverse[span, :]
        gathered = turn[0, span, :]
        inside = lane < rows
        surf = facts[0, span, :]
        rho, u1, u2, u3, p = (
            jnp.where(inside, part(surf, q + 1, rows), 1.0) for q in range(5)
        )
        fitted = jnp.where(inside, part(surf, 6, rows), 0.0)
        scale = top_scale * inv_height
        last = tops[span, :]
        s0, s1, s2, s3, s4 = (part(last, q, rows) * scale for q in range(5))
        kinetic, enthalpy = thermo(rho, u1, u2, u3, p)
        fluxes = flux_of(rho, u1, u2, u3, p, enthalpy)
        top_work = (
            fluxes[0] * s0 + fluxes[1] * s1 + fluxes[2] * s2 + fluxes[3] * s3 + fluxes[4] * s4
        )
        dotted = u1 * s1 + u2 * s2 + u3 * s3
        shared = gm * (s3 + u3 * s4)
        common = s0 + dotted + enthalpy * s4
        adjoint = (
            kinetic * s3 - u3 * dotted + u3 * (kinetic - enthalpy) * s4,
            u3 * s1 - u1 * shared,
            u3 * s2 - u2 * shared,
            u3 * s3 - u3 * shared + common,
            gm * s3 + gamma_ratio * u3 * s4,
        )
        heights = facts[1, span, :]
        slopes = facts[2, span, :]
        by_h = sum(adjoint[q] * part(heights, q, rows) for q in range(5))
        by_s = sum(adjoint[q] * part(slopes, q, rows) for q in range(5))
        metric = -inv_height * (gathered + front * top_work)
        term = jnp.where(inside, metric + front * fitted * by_h, 0.0)
        tilt = jnp.where(inside, front * fitted * by_s, 0.0)
        packet[span, 0:128] = (
            packet[span, 0:128] + pltpu.roll(term, 5 * rows, 1) + pltpu.roll(tilt, 6 * rows, 1)
        )

    su_even, sv_even = even("su"), even("sv")
    high_row = rows - 2
    row_a = jnp.where(su_even, high_row, 0)
    row_b = high_row - row_a
    for r in range(2):
        for ref, row in ((su_a, row_a + r), (su_b, row_b + r)):
            for q in range(5):
                ref[q, r] = psi[q, row]
            ref[5, r] = jnp.abs(prim[1, row]) + tone[row]
    for i in range(rows):
        pair = slice(2 * i, 2 * i + 2)
        for q in range(6):
            if q < 5:
                low, high = psi[q, i, 0:2, :], psi[q, i, columns - 2 : columns, :]
            else:
                low = jnp.abs(prim[2, i, 0:2, :]) + tone[i, 0:2, :]
                high = (
                    jnp.abs(prim[2, i, columns - 2 : columns, :])
                    + tone[i, columns - 2 : columns, :]
                )
            sv_a[q, pair, :] = jnp.where(sv_even, high, low)
            sv_b[q, pair, :] = jnp.where(sv_even, low, high)


def join_kernel(
    rows, tiles, depth, total_depth, surface, fan, own, arrived, inverse, chunk, mine
):
    first = lax.axis_index("nrm") == 0
    lane = lanes()
    one = jnp.zeros((1, 128), f32)
    before = 0.5 * inv_stretch_at(one + (depth - 1), total_depth)
    after = 0.5 * inv_stretch_at(one + depth, total_depth)
    own_scale = jnp.where(first, before, after)
    far_scale = jnp.where(first, after, before)
    sign = jnp.where(first, 1.0, -1.0)
    sums = jnp.zeros((8, 128), f32)
    kept = jnp.zeros((8, 128), f32)
    for t in range(tiles):
        span = slice(8 * t, 8 * t + 8)
        near, near_flux = own[span, 0:128], own[span, 128:256]
        far, far_flux = arrived[span, 0:128], arrived[span, 128:256]
        cross = near_flux * (far * far_scale) - far_flux * (near * own_scale)
        cross = jnp.where(lane < 5 * rows, cross, 0.0)
        for d in (1, 2, 4):
            cross = cross + pltpu.roll(cross, rows * d, 1)
        inv_height = inverse[span, :]
        total = near + far
        inside = lane < rows
        term = jnp.where(
            inside, part(total, 5, rows) + sign * inv_height * inv_height * cross, 0.0
        )
        for d in (1, 2, 4, 8):
            term = term + pltpu.roll(term, 128 - d, 1)
        share = term * (1.0 / surface)
        slope = jnp.where(inside, share + part(total, 6, rows), 0.0)
        kept = kept + (pltpu.roll(slope, rows * t, 1) if t else slope)
        sums = jnp.where(lane == t, pltpu.roll(share, t, 1) if t else share, sums)
    mine[...] = kept
    for n in range(fan):
        chunk[n] = sums


def transposed(speeds, kinetic, enthalpy, first, second, third):
    given = [(d, g) for d, g in ((0, first), (1, second), (2, third)) if g is not None]
    add = lambda parts: functools.reduce(lambda x, y: x + y, parts)
    projected = add([g[d + 1] for d, g in given])
    energy = add([speeds[d] * g[4] for d, g in given])
    dots = {
        d: speeds[0] * g[1] + speeds[1] * g[2] + speeds[2] * g[3] for d, g in given
    }
    shared = gm * (projected + energy)
    out = [
        kinetic * projected
        - add([speeds[d] * dots[d] for d, _ in given])
        + (kinetic - enthalpy) * energy
    ]
    for c in range(3):
        value = add([speeds[d] * g[c + 1] for d, g in given]) - speeds[c] * shared
        for d, g in given:
            if d == c:
                value = value + (g[0] + dots[d] + enthalpy * g[4])
        out.append(value)
    out.append(gm * projected + gamma_ratio * energy)
    return out


near_weight, far_weight = 8.0 / 12.0, 1.0 / 12.0


def interior_kernel(
    rows, tiles, prim, psi, target_far, normal, enth, tone,
    base,
    wide, along, across, target, large,
):
    step_rows = 4
    columns = 8 * tiles
    loads = [
        pltpu.make_async_copy(
            target_far.at[:, pl.ds(r, step_rows)], target.at[:, pl.ds(r, step_rows)],
            large.at[r // step_rows],
        )
        for r in range(0, rows, step_rows)
    ]
    for copy in loads:
        copy.start()
    for q in range(5):
        for i in range(rows):
            for low in (0, 8 + columns):
                wide[q, i + 2, low : low + 8, :] = jnp.zeros((8, 128), f32)
                across[q, i, low : low + 8, :] = jnp.zeros((8, 128), f32)

    @pl.loop(0, rows, unroll=4)
    def _(i):
        for t in range(tiles):
            span = slice(8 * t, 8 * t + 8)
            inner = slice(8 * t + 8, 8 * t + 16)
            sound = tone[i, span, :]
            radius_u = jnp.abs(prim[1, i, span, :]) + sound
            radius_v = jnp.abs(prim[2, i, span, :]) + sound
            for q in range(5):
                value = psi[q, i, span, :]
                wide[q, i + 2, inner, :] = value
                along[q, i, span, :] = radius_u * value
                across[q, i, inner, :] = radius_v * value

    def pair(i, tap, k, sign):
        if i < k:
            return sign * tap(k)
        if i + k >= rows:
            return tap(-k)
        return tap(-k) + tap(k) if sign > 0 else tap(-k) - tap(k)

    def fill(i):
        for t in range(tiles):
            span = slice(8 * t, 8 * t + 8)
            at = lambda k: slice(8 * t + 8 + k, 8 * t + 16 + k)
            first, second, third, damp = [], [], [], []
            for q in range(5):
                tap = lambda k: wide[q, i + 2 + k, at(0), :]
                first.append(
                    near_weight * pair(i, tap, 1, -1.0) - far_weight * pair(i, tap, 2, -1.0)
                )
                second.append(
                    near_weight * (wide[q, i + 2, at(-1), :] - wide[q, i + 2, at(1), :])
                    - far_weight * (wide[q, i + 2, at(-2), :] - wide[q, i + 2, at(2), :])
                )
                tap = lambda k: along[q, i + k, span, :]
                far = pair(i, tap, 2, 1.0) + (across[q, i, at(-2), :] + across[q, i, at(2), :])
                near = pair(i, tap, 1, 1.0) + (across[q, i, at(-1), :] + across[q, i, at(1), :])
                here = along[q, i, span, :] + across[q, i, at(0), :]
                damp.append(
                    damping_coef * far - (4.0 * damping_coef) * near + (6.0 * damping_coef) * here
                )
                third.append(normal[q, i, span, :])
            speeds = tuple(prim[q, i, span, :] for q in (1, 2, 3))
            u1, u2, u3 = speeds
            kinetic = (0.5 * gm) * (u1 * u1 + u2 * u2 + u3 * u3)
            terms = transposed(speeds, kinetic, enth[i, span, :], first, second, third)
            for q in range(5):
                base[q, i, span, :] = target[q, i, span, :] + terms[q] + damp[q]

    for c, copy in enumerate(loads):
        copy.wait()
        for i in range(c * step_rows, (c + 1) * step_rows):
            fill(i)


def final_kernel(
    rows, tiles, depth, total_depth, su_count, sv_count,
    prim, base, flux, enth, inverse, arrived, mine,
    su_a, su_b, sv_a, sv_b, chunks,
    result, slope,
    left, right, turn, done, sems,
):
    su, sv, nrm = lax.axis_index("su"), lax.axis_index("sv"), lax.axis_index("nrm")
    before = nrm == 0
    lane = lanes()
    line = lax.broadcasted_iota(jnp.int32, (8, 128), 0)
    columns = 8 * tiles
    ahead = jnp.zeros((8, 128), f32)
    for n in range(su_count):
        ahead = ahead + jnp.where(n > su, chunks[n], 0.0)
    upstream = jnp.zeros((8, 128), f32)
    for t in range(tiles):
        upstream = jnp.where(
            (lane >= rows * t) & (lane < rows * t + rows), spread_lane(ahead, t), upstream
        )
    packed = mine[...] + upstream
    turn[...] = jnp.zeros_like(turn)
    for t in range(tiles):
        turn[8 * t : 8 * t + 8, :] = pltpu.roll(packed, 128 - rows * t, 1) if t else packed
    slope[...] = turn[...].T[0:rows, 0:columns]

    one = jnp.zeros((1, 128), f32)
    edge_scale = jnp.where(
        before,
        -0.5 * inv_stretch_at(one + depth, total_depth),
        0.5 * inv_stretch_at(one + (depth - 1), total_depth),
    )
    entry = jnp.where(before, depth - 1, 0)
    at_entry = lane == entry
    for t in range(tiles):
        span = slice(8 * t, 8 * t + 8)
        repeated = inverse[span, :]
        for d in (1, 2, 4):
            repeated = repeated + pltpu.roll(repeated, rows * d, 1)
        turn[span, :] = arrived[span, 0:128] * edge_scale * repeated

    su_even, sv_even = even("su"), even("sv")
    for piece in range(2 * rows // 8):
        at = slice(8 * piece, 8 * piece + 8)
        outer = lax.rem(line, 2) == 0
        for swap, on, ref, offset, sign in (
            (sv_even, sv > 0, left, 0, 1.0),
            (~sv_even, sv < sv_count - 1, right, 8, -1.0),
        ):
            into = slice(8 * piece + offset, 8 * piece + offset + 8)
            pick = lambda q: jnp.where(swap, sv_b[q, at, :], sv_a[q, at, :])
            radius = pick(5)
            for q in range(5):
                value = jnp.where(on, pick(q), 0.0)
                weighted = value * radius
                grads, damps = [], []
                for array, close, away, kept in (
                    (value, sign * near_weight, -sign * far_weight, grads),
                    (weighted, -4.0 * damping_coef, damping_coef, damps),
                ):
                    if offset == 0:
                        even_part = close * pltpu.roll(array, 7, 0) + away * array
                        odd_part = away * array
                    else:
                        even_part = away * array
                        odd_part = close * pltpu.roll(array, 1, 0) + away * array
                    kept.append(jnp.where(outer, even_part, odd_part))
                ref[q, into, :] = grads[0]
                ref[5 + q, into, :] = damps[0]

    def out_copy(i):
        return pltpu.make_async_copy(done.at[:, i], result.at[:, i], sems.at[i])

    fraction = jnp.broadcast_to(
        ((lanes((1, 128)) + nrm * depth).astype(f32) + 0.5) / total_depth, (8, 128)
    )

    def finish(i, beside):
        turned = pltpu.roll(packed, 128 - i, 1)
        for t in range(tiles):
            span = slice(8 * t, 8 * t + 8)
            ends = turn[span, :]
            third = [
                jnp.where(at_entry, pltpu.roll(ends, entry + (128 - rows * q) - i, 1), 0.0)
                for q in range(5)
            ]
            first = second = None
            damp = [None] * 5
            if beside is not None:
                first, damp = beside(span)
            if t in (0, tiles - 1):
                ref, start = (left, 2 * i) if t == 0 else (right, 2 * i + 2)
                here = line < 2 if t == 0 else line >= 6
                load = lambda q: jnp.where(here, ref[q, pl.ds(start, 8), :], 0.0)
                second = [load(q) for q in range(5)]
                damp = [
                    load(5 + q) if damp[q] is None else damp[q] + load(5 + q) for q in range(5)
                ]
            speeds = tuple(prim[q, i, span, :] for q in (1, 2, 3))
            u1, u2, u3 = speeds
            kinetic = (0.5 * gm) * (u1 * u1 + u2 * u2 + u3 * u3)
            terms = transposed(speeds, kinetic, enth[i, span, :], first, second, third)
            ramp = fraction * spread_lane(turned, rows * t)
            for q in range(5):
                value = base[q, i, span, :] + terms[q] + ramp * flux[q, i, span, :]
                done[q, i, span, :] = value if damp[q] is None else value + damp[q]
        out_copy(i).start()

    def edge_row(low, inner):
        swap, on, sign = (
            (su_even, su > 0, 1.0) if low else (~su_even, su < su_count - 1, -1.0)
        )

        def beside(span):
            pick = lambda q, r: jnp.where(swap, su_b[q, r, span, :], su_a[q, r, span, :])
            close, away = (1, 0) if low else (0, 1)
            grads, damps = [], []
            for q in range(5):
                value = jnp.where(on, pick(q, close), 0.0)
                weighted = value * pick(5, close)
                if inner:
                    grads.append((-sign * far_weight) * value)
                    damps.append(damping_coef * weighted)
                else:
                    other = jnp.where(on, pick(q, away), 0.0)
                    grads.append((sign * near_weight) * value - (sign * far_weight) * other)
                    damps.append(
                        damping_coef * (other * pick(5, away)) - (4.0 * damping_coef) * weighted
                    )
            return grads, damps

        return beside

    finish(0, edge_row(True, False))
    finish(1, edge_row(True, True))
    pl.loop(2, rows - 2, unroll=4)(lambda i: finish(i, None))
    finish(rows - 2, edge_row(False, True))
    finish(rows - 1, edge_row(False, False))

    @pl.loop(0, rows)
    def _(i):
        out_copy(i).wait()


def call(kernel, outs, operands, scratch, flops, name, spaces=None, far=()):
    spec = lambda n: pl.BlockSpec(memory_space=pltpu.HBM if n in far else VMEM)
    size = sum(4 * a.size for a in operands) + sum(4 * o.size for o in outs)
    operands = [
        pltpu.with_memory_space_constraint(a, pltpu.HBM) if n in far else a
        for n, a in enumerate(operands)
    ]
    return pl.pallas_call(
        kernel,
        out_shape=outs,
        in_specs=[spec(n) for n in range(len(operands))],
        out_specs=[pl.BlockSpec(memory_space=s) for s in (spaces or [VMEM] * len(outs))],
        scratch_shapes=scratch,
        cost_estimate=pl.CostEstimate(flops=flops, transcendentals=0, bytes_accessed=size),
        compiler_params=pltpu.CompilerParams(vmem_limit_bytes=16 << 20),
        name=name,
    )(*operands)


def local(
    primitive, adjoint_state, objective_grad, front_height,
    shock_state, state_by_height, state_by_slope, fitted_flags,
):
    _, rows, columns, depth = adjoint_state.shape
    tiles = columns // 8
    su_count, sv_count, lines = (lax.axis_size(a) for a in ("su", "sv", "nrm"))
    total_depth = depth * lines
    shape = lambda *s: jax.ShapeDtypeStruct(s, f32)
    field = shape(5, rows, columns, depth)
    plane = shape(rows, columns, depth)
    points = 5 * rows * columns * depth

    packet, su_a, su_b, sv_a, sv_b, normal, flux, enth, tone, inverse, prim, psi = call(
        functools.partial(prepare_kernel, rows, tiles, depth, total_depth, rows // 8),
        [
            shape(columns, 256),
            shape(6, 2, columns, depth),
            shape(6, 2, columns, depth),
            shape(6, 2 * rows, depth),
            shape(6, 2 * rows, depth),
            field, field, plane, plane,
            shape(columns, 128),
            field, field,
        ],
        (
            primitive, adjoint_state, front_height,
            shock_state, state_by_height, state_by_slope, fitted_flags,
        ),
        [
            VMEM((3, 128, 128), f32),
            VMEM((3, 128, 128), f32),
            VMEM((columns, 128), f32),
            VMEM((columns, 128), f32),
            VMEM((rows, columns, depth), f32),
            VMEM((rows, columns, depth), f32),
            VMEM((rows, columns), f32),
            VMEM((5, rows, columns), f32),
            VMEM((5, rows, columns), f32),
            VMEM((5, rows, columns), f32),
            VMEM((rows, columns), jnp.int32),
            pltpu.SemaphoreType.DMA((5,)),
            pltpu.SemaphoreType.DMA((2, 8)),
        ],
        12 * points,
        "prepare",
        far=range(7),
    )

    def pairs(count, shift):
        out = []
        for i in range(0, count, 2):
            a, b = (i + shift) % count, (i + shift + 1) % count
            out += [(a, b), (b, a)]
        return out

    arrived = lax.ppermute(packet, "nrm", [(0, 1), (1, 0)])
    su_a = lax.ppermute(su_a, "su", pairs(su_count, 0))
    su_b = lax.ppermute(su_b, "su", pairs(su_count, 1))
    sv_a = lax.ppermute(sv_a, "sv", pairs(sv_count, 0))
    sv_b = lax.ppermute(sv_b, "sv", pairs(sv_count, 1))

    chunk, mine = call(
        functools.partial(
            join_kernel, rows, tiles, depth, total_depth, rows * su_count, su_count
        ),
        [shape(su_count, 8, 128), shape(8, 128)],
        (packet, arrived, inverse),
        [],
        JOIN_COST * points,
        "join",
    )
    (base,) = call(
        functools.partial(interior_kernel, rows, tiles),
        [field],
        (prim, psi, objective_grad, normal, enth, tone),
        [
            VMEM((5, rows + 4, columns + 16, depth), f32),
            VMEM((5, rows, columns, depth), f32),
            VMEM((5, rows, columns + 16, depth), f32),
            VMEM((5, rows, columns, depth), f32),
            pltpu.SemaphoreType.DMA((4,)),
        ],
        INTERIOR_COST * points,
        "interior",
        far=(2,),
    )
    chunk, su_a, su_b, sv_a, sv_b, base = lax.optimization_barrier(
        (chunk, su_a, su_b, sv_a, sv_b, base)
    )
    chunks = lax.all_to_all(chunk, "su", 0, 0)
    result, slope = call(
        functools.partial(
            final_kernel, rows, tiles, depth, total_depth, su_count, sv_count
        ),
        [field, shape(rows, columns)],
        (
            prim, base, flux, enth, inverse,
            arrived, mine, su_a, su_b, sv_a, sv_b, chunks,
        ),
        [
            VMEM((10, 2 * rows + 8, depth), f32),
            VMEM((10, 2 * rows + 16, depth), f32),
            VMEM((128, 128), f32),
            VMEM((5, rows, columns, depth), f32),
            pltpu.SemaphoreType.DMA((rows,)),
        ],
        20 * points,
        "final",
        [pltpu.HBM, VMEM],
    )
    return result, slope


def solution(mesh):
    wide = P(None, "su", "sv", "nrm")
    flat = P("su", "sv")
    front = P(None, "su", "sv")
    return jax.shard_map(
        local,
        mesh=mesh,
        in_specs=(wide, wide, wide, flat, front, front, front, flat),
        out_specs=(wide, flat),
        check_vma=False,
    )
```
